32 devices in a mesh: seq: 8 (over z, y), pass: 4 (over x, core).
Axes of the slice: x: 2, y: 2, z: 4, core: 2. Of those that a mesh axis runs over, the one named last changes fastest.
Arguments:
- x_rows: bfloat16 [4, 8192, 768], P('pass', 'seq'), may hold values from -6 to 6
- pass_depth: int32 [8, 1024], P('seq'), may hold values from 1 to 4
- cotangent: bfloat16 [4, 8192, 768], P('pass', 'seq'), may hold values from -6 to 6
- pass_emb: float32 [4, 768], replicated, may hold values from -3 to 3
- ln1_gain: float32 [768], replicated, may hold values from 0.1 to 1.9
- ln1_bias: float32 [768], replicated, may hold values from -2 to 2
- w_qkv: bfloat16 [768, 2304], P(('seq', 'pass')), may hold values from -0.21875 to 0.21875
- q_bias: float32 [768], replicated, may hold values from -2 to 2
- v_bias: float32 [768], replicated, may hold values from -0.6 to 0.6
- w_out: bfloat16 [768, 768], P(('seq', 'pass')), may hold values from -0.875 to 0.875
- out_bias: float32 [768], replicated, may hold values from -2 to 2
- ln2_gain: float32 [768], replicated, may hold values from 0.1 to 1.9
- ln2_bias: float32 [768], replicated, may hold values from -2 to 2
- w_up: bfloat16 [768, 3072], P(('seq', 'pass')), may hold values from -0.21875 to 0.21875
- up_bias: float32 [3072], replicated, may hold values from -3 to 3
- w_down: bfloat16 [3072, 768], P(('seq', 'pass')), may hold values from -0.109375 to 0.109375
- down_bias: float32 [768], replicated, may hold values from -2 to 2
Outputs:
- out_rows: bfloat16 [4, 8192, 768], P('pass', 'seq')
- x_grad: float32 [4, 8192, 768], P('pass', 'seq')
- w_qkv_grad: float32 [768, 2304], P(('seq', 'pass'))
- q_bias_grad: float32 [768], replicated
- v_bias_grad: float32 [768], replicated
- w_out_grad: float32 [768, 768], P(('seq', 'pass'))
- out_bias_grad: float32 [768], replicated
- ln1_gain_grad: float32 [768], replicated
- ln1_bias_grad: float32 [768], replicated
- ln2_gain_grad: float32 [768], replicated
- ln2_bias_grad: float32 [768], replicated
- w_up_grad: float32 [768, 3072], P(('seq', 'pass'))
- up_bias_grad: float32 [3072], replicated
- w_down_grad: float32 [3072, 768], P(('seq', 'pass'))
- down_bias_grad: float32 [768], replicated
- pass_emb_grad: float32 [4, 768], P('pass')
The draws below stay inside these ranges and needn't reach their ends.
Inputs may be any that keep to these rules, and one draw needn't show every extreme that they name: A token serves as a key in its first pass_depth passes only; every token counts as a key in pass 0.
All inputs are finite; a program needn't handle non-finite values.
Results may differ from the reference program's by a relative error of at most 0.012.
Values may be sent and summed in bfloat16 or wider, within the bound.
No kernel may reach another device: no remote copies, remote signals or barrier semaphores. Data moves between devices by JAX's collectives and lax.ppermute only.
A program may use at most 256 MiB of HBM per device.

```python
import math
import jax
import jax.numpy as jnp
from jax import lax

D = 768
HEADS = 12
HEAD_DIM = 64
FF = 3072
LEN = 1024
PASSES = 4
SEQS = 8


def with_ends(values, stream_key, smallest, largest):
    index_at = [jax.random.randint(jax.random.fold_in(stream_key, axis), (), 0, length) for axis, length in enumerate(values.shape)]
    longest = values.shape.index(max(values.shape))
    next_to = index_at[:longest] + [(index_at[longest] + 1) % values.shape[longest]] + index_at[longest + 1:]
    return values.at[tuple(index_at)].set(smallest).at[tuple(next_to)].set(largest)


def level_of(own_key, dims, split, smallest, largest):
    level = 1.0
    for dim, shards_of in split:
        draws = jax.random.uniform(jax.random.fold_in(jax.random.fold_in(own_key, 6), dim), (shards_of,), jnp.float32, smallest / len(split), largest / len(split))
        level = level * jnp.repeat(jnp.exp(draws), dims[dim] // shards_of).reshape((-1,) + (1,) * (len(dims) - 1 - dim))
    return level


def scatter_about(key, dims, width, most, pieces=(), held_as=jnp.bfloat16):
    loudness = level_of(key, dims, pieces, -0.22, 0.18) if pieces else 1.0
    values = jax.random.normal(key, dims, jnp.float32) * width * loudness
    return jnp.minimum(jnp.maximum(values, -most), most).astype(held_as)


def setup_inputs(seed: int = 0) -> dict:
    key_of = jax.random.split(jax.random.key(seed), 18)
    x_rows = scatter_about(key_of[0], (PASSES, SEQS * LEN, D), 1.0, 6.0, ((0, 4), (1, 8)))
    pass_depth = with_ends(jax.random.randint(key_of[1], (SEQS, LEN), 1, PASSES + 1), jax.random.fold_in(key_of[1], 1), 1, PASSES).astype(jnp.int32)
    cotangent = scatter_about(key_of[2], (PASSES, SEQS * LEN, D), 1.0, 6.0, ((0, 4), (1, 8)))
    pass_emb = scatter_about(key_of[3], (PASSES, D), 0.5, 3.0, (), jnp.float32)
    ln1_gain = jnp.clip(1.0 + 0.18 * jax.random.normal(key_of[4], (D,), jnp.float32), 0.1, 1.9)
    ln1_bias = scatter_about(key_of[5], (D,), 0.3, 2.0, (), jnp.float32)
    w_qkv = scatter_about(key_of[6], (D, 3 * D), D ** -0.5, 0.21875, ((0, 32),))
    q_bias = scatter_about(key_of[7], (D,), 0.3, 2.0, (), jnp.float32)
    v_bias = scatter_about(key_of[8], (D,), 0.1, 0.6, (), jnp.float32)
    w_out = scatter_about(key_of[9], (D, D), (D // 16) ** -0.5, 0.875, ((0, 32),))
    out_bias = scatter_about(key_of[10], (D,), 0.3, 2.0, (), jnp.float32)
    ln2_gain = jnp.clip(1.0 + 0.18 * jax.random.normal(key_of[11], (D,), jnp.float32), 0.1, 1.9)
    ln2_bias = scatter_about(key_of[12], (D,), 0.3, 2.0, (), jnp.float32)
    w_up = scatter_about(key_of[13], (D, FF), D ** -0.5, 0.21875, ((0, 32),))
    up_bias = scatter_about(key_of[14], (FF,), 0.5, 3.0, (), jnp.float32)
    w_down = scatter_about(key_of[15], (FF, D), FF ** -0.5, 0.109375, ((0, 32),))
    down_bias = scatter_about(key_of[16], (D,), 0.3, 2.0, (), jnp.float32)
    return {"x_rows": x_rows, "pass_depth": pass_depth, "cotangent": cotangent, "pass_emb": pass_emb, "ln1_gain": ln1_gain, "ln1_bias": ln1_bias, "w_qkv": w_qkv, "q_bias": q_bias, "v_bias": v_bias, "w_out": w_out, "out_bias": out_bias, "ln2_gain": ln2_gain, "ln2_bias": ln2_bias, "w_up": w_up, "up_bias": up_bias, "w_down": w_down, "down_bias": down_bias}


@jax.custom_vjp
def low(v):
    return lax.optimization_barrier(v.astype(jnp.bfloat16)).astype(jnp.float32)

@jax.custom_vjp
def low_back(v):
    return v

def low_keep(v):
    return (low(v), None)

def low_pass(kept, grad):
    return (grad,)

def back_keep(v):
    return (v, None)

def back_low(kept, grad):
    return (low(grad),)
low.defvjp(low_keep, low_pass)
low_back.defvjp(back_keep, back_low)
norm_eps = 1e-05

def layer_norm(values, gain_row, shift_row):
    center = values - lax.optimization_barrier(jnp.mean(values, axis=-1, keepdims=True))
    inverse = lax.rsqrt(lax.optimization_barrier(jnp.mean(center * center, axis=-1, keepdims=True)) + norm_eps)
    return center * inverse * gain_row + shift_row

def both_round(values):
    return low_back(low(values))

def high_dot(first_op, second_op):
    return jnp.dot(first_op, second_op, precision=lax.Precision.HIGHEST, preferred_element_type=jnp.float32)

def sequence_forward(params, seq_rows, seq_depth):
    pass_emb, ln1_gain, ln1_bias, w_qkv, q_bias, v_bias, w_out, out_bias, ln2_gain, ln2_bias, w_up, up_bias, w_down, down_bias = params
    passes, seq_len, model_width = seq_rows.shape
    total_rows = passes * seq_len
    stream_in = (seq_rows + pass_emb[:, None, :]).reshape(total_rows, model_width)
    normed_one = low(layer_norm(stream_in, ln1_gain, ln1_bias))
    projected = high_dot(normed_one, w_qkv)
    queries = both_round(projected[:, :model_width] + q_bias)
    key_rows = both_round(projected[:, model_width:2 * model_width])
    value_rows = both_round(projected[:, 2 * model_width:] + v_bias)
    row_index = jnp.arange(total_rows, dtype=jnp.int32)
    row_pass = row_index // seq_len
    row_pos = row_index % seq_len
    key_ok = row_pass < jnp.tile(seq_depth, passes)
    query_heads = queries.reshape(total_rows, HEADS, HEAD_DIM)
    key_heads = key_rows.reshape(total_rows, HEADS, HEAD_DIM)
    value_heads = value_rows.reshape(total_rows, HEADS, HEAD_DIM)
    block_rows = math.gcd(total_rows, 512)
    score_scale = HEAD_DIM ** (-0.5)

    def attend(block_index):
        start = (block_index * block_rows).astype(jnp.int32)
        query_part = lax.dynamic_slice_in_dim(query_heads, start, block_rows, 0)
        query_pass = lax.dynamic_slice_in_dim(row_pass, start, block_rows, 0)
        query_pos = lax.dynamic_slice_in_dim(row_pos, start, block_rows, 0)
        allowed = key_ok[None, :] & (row_pass[None, :] <= query_pass[:, None]) & (row_pos[None, :] <= query_pos[:, None])
        raw_scores = low_back(jnp.einsum('qhd,khd->hqk', query_part, key_heads, precision=lax.Precision.HIGHEST) * score_scale)
        scores = jnp.where(allowed[None], raw_scores, -1e+30)
        attn_prob = low(jax.nn.softmax(scores, axis=-1))
        return jnp.einsum('hqk,khd->qhd', attn_prob, value_heads, precision=lax.Precision.HIGHEST)
    head_out = lax.map(jax.checkpoint(attend), jnp.arange(total_rows // block_rows, dtype=jnp.int32))
    attn_rows = both_round(head_out.reshape(total_rows, model_width))
    mixed = stream_in + low_back(high_dot(attn_rows, w_out)) + out_bias
    normed_two = low(layer_norm(mixed, ln2_gain, ln2_bias))
    upper = low_back(high_dot(normed_two, w_up) + up_bias)
    activated = low(jax.nn.gelu(upper, approximate=False))
    result = mixed + low_back(high_dot(activated, w_down)) + down_bias
    return result.reshape(passes, seq_len, model_width)

def reference(x_rows, pass_depth, cotangent, pass_emb, ln1_gain, ln1_bias, w_qkv, q_bias, v_bias, w_out, out_bias, ln2_gain, ln2_bias, w_up, up_bias, w_down, down_bias):
    passes = x_rows.shape[0]
    model_width = x_rows.shape[2]
    seq_total, seq_len = pass_depth.shape
    inputs = x_rows.astype(jnp.float32).reshape(passes, seq_total, seq_len, model_width).transpose(1, 0, 2, 3)
    cot_rows = cotangent.astype(jnp.float32).reshape(passes, seq_total, seq_len, model_width).transpose(1, 0, 2, 3)
    params = tuple((arr.astype(jnp.float32) for arr in (pass_emb, ln1_gain, ln1_bias, w_qkv, q_bias, v_bias, w_out, out_bias, ln2_gain, ln2_bias, w_up, up_bias, w_down, down_bias)))
    zero_grads = tuple((jnp.zeros_like(arr) for arr in params))

    def one_sequence(carry, scanned):
        seq_rows, seq_cot, seq_depth = scanned

        def forward_of(param_set, row_set):
            return sequence_forward(param_set, row_set, seq_depth)
        result, backward = jax.vjp(forward_of, params, seq_rows)
        param_grads, row_grads = backward(seq_cot)
        carry = jax.tree.map(jnp.add, carry, param_grads)
        return (carry, (result, row_grads))
    grads, (results, row_grads) = lax.scan(one_sequence, zero_grads, (inputs, cot_rows, pass_depth))
    out_rows = results.transpose(1, 0, 2, 3).reshape(passes, seq_total * seq_len, model_width).astype(jnp.bfloat16)
    x_grad = row_grads.transpose(1, 0, 2, 3).reshape(passes, seq_total * seq_len, model_width)
    pass_emb_grad, ln1_gain_grad, ln1_bias_grad, w_qkv_grad, q_bias_grad, v_bias_grad, w_out_grad, out_bias_grad, ln2_gain_grad, ln2_bias_grad, w_up_grad, up_bias_grad, w_down_grad, down_bias_grad = grads
    return (out_rows, x_grad, w_qkv_grad, q_bias_grad, v_bias_grad, w_out_grad, out_bias_grad, ln1_gain_grad, ln1_bias_grad, ln2_gain_grad, ln2_bias_grad, w_up_grad, up_bias_grad, w_down_grad, down_bias_grad, pass_emb_grad)
```

```python
import functools

import jax
import jax.numpy as jnp
from jax import lax
from jax.experimental import pallas as pl
from jax.experimental.pallas import tpu as pltpu
from jax.sharding import PartitionSpec as P

HEADS = 12
HEAD_DIM = 64
LANES = 128
NORM_EPS = 1e-05
MASKED = -1e30
BIAS_COL = 64
STAT_COL = 65
DELTA_COL = 64

bfloat = jnp.bfloat16
single = jnp.float32


def dot_nn(a, b):
    return jnp.dot(a, b, preferred_element_type=single)


def dot_nt(a, b):
    return lax.dot_general(a, b, (((1,), (1,)), ((), ())), preferred_element_type=single)


def dot_tn(a, b):
    return lax.dot_general(a, b, (((0,), (0,)), ((), ())), preferred_element_type=single)


def three_parts(value):
    first = value.astype(bfloat).astype(single)
    rest = value - first
    second = rest.astype(bfloat).astype(single)
    return first, second, rest - second


def with_columns(base, start, columns):
    lane = lax.broadcasted_iota(jnp.int32, base.shape, 1)
    for offset, column in enumerate(columns):
        base = jnp.where(lane == start + offset, column, base)
    return base


def norm_parts(values):
    center = values - jnp.mean(values, axis=-1, keepdims=True)
    inverse = lax.rsqrt(jnp.mean(center * center, axis=-1, keepdims=True) + NORM_EPS)
    return center * inverse, inverse


def norm_back(grad, gain, normed, inverse):
    scaled = grad * gain
    mean_one = jnp.mean(scaled, axis=-1, keepdims=True)
    mean_two = jnp.mean(scaled * normed, axis=-1, keepdims=True)
    return inverse * (scaled - mean_one - normed * mean_two)


def head_slab(packed, index):
    low = (index // 2) * LANES
    slab = packed[:, low : low + LANES]
    if index % 2:
        slab = pltpu.roll(slab, HEAD_DIM, axis=1)
    return slab


def pack_heads(slabs):
    packed = []
    lane = lax.broadcasted_iota(jnp.int32, slabs[0].shape, 1)
    for index in range(0, len(slabs), 2):
        if index + 1 < len(slabs):
            other = pltpu.roll(slabs[index + 1], HEAD_DIM, axis=1)
            packed.append(jnp.where(lane < HEAD_DIM, slabs[index], other))
        else:
            packed.append(slabs[index])
    width = len(slabs) * HEAD_DIM
    return jnp.concatenate(packed, axis=1)[:, :width]


def project_kernel(heads, count, me_ref, *refs):
    pieces = refs[:count]
    pass_ref, gain_ref, shift_ref, weight_ref, bias_ref, depth_ref = refs[count : count + 6]
    q_ref, k_ref, v_ref = refs[-3:]
    slot = pl.program_id(0)
    pass_index = me_ref[1 + slot]
    pass_row = pass_ref[pl.ds(pass_index, 1), :]
    rows = pieces[0][...]
    for index in range(1, count):
        rows = jnp.where(slot == index, pieces[index][...], rows)
    normed, _ = norm_parts(rows.astype(single) + pass_row)
    low = (normed * gain_ref[...] + shift_ref[...]).astype(bfloat)
    projected = dot_nn(low, weight_ref[...]) + bias_ref[...]
    lane = lax.broadcasted_iota(jnp.int32, (low.shape[0], LANES), 1)
    inside = lane < HEAD_DIM
    depth_bias = jnp.where(pass_index < depth_ref[...], 0.0, MASKED)
    q_rest = jnp.where(lane == BIAS_COL, 1.0, 0.0)
    k_rest = jnp.where(
        lane == BIAS_COL, depth_bias, jnp.where((lane >= STAT_COL) & (lane < STAT_COL + 3), 1.0, 0.0)
    )
    v_rest = jnp.where((lane >= DELTA_COL) & (lane < DELTA_COL + 3), 1.0, 0.0)
    for head in range(heads):
        q_part = head_slab(projected, head).astype(bfloat).astype(single) * (HEAD_DIM**-0.5)
        q_ref[head] = jnp.where(inside, q_part, q_rest).astype(bfloat)
        k_ref[head] = jnp.where(inside, head_slab(projected, heads + head), k_rest).astype(bfloat)
        v_ref[head] = jnp.where(inside, head_slab(projected, 2 * heads + head), v_rest).astype(bfloat)


def project(order, pieces, passes, pass_emb, gain, shift, weight, bias, depth, previous):
    count = len(pieces)
    length, width = pieces[0].shape
    heads = weight.shape[1] // (3 * HEAD_DIM)
    block = min(512, length)
    steps = length // block

    def piece_spec(index):
        def where(slot, step, order_ref):
            return (jnp.where(slot == index, step, jnp.where(slot < index, 0, steps - 1)), 0)

        return pl.BlockSpec((block, width), where)

    def whole(shape):
        return pl.BlockSpec(shape, lambda slot, step, order_ref: (0,) * len(shape))

    out_spec = pl.BlockSpec(
        (heads, pl.Squeezed(), block, LANES),
        lambda slot, step, order_ref: (0, order_ref[1 + slot], step, 0),
    )
    shape = jax.ShapeDtypeStruct((heads, passes, length, LANES), bfloat)
    in_specs = [piece_spec(index) for index in range(count)] + [
        whole(pass_emb.shape),
        whole(gain.shape),
        whole(shift.shape),
        whole(weight.shape),
        whole(bias.shape),
        pl.BlockSpec((block, 1), lambda slot, step, order_ref: (step, 0)),
    ]
    operands = [*pieces, pass_emb, gain, shift, weight, bias, depth]
    aliases = {}
    if previous is not None:
        aliases = {1 + len(operands) + index: index for index in range(3)}
        in_specs += [pl.BlockSpec(memory_space=pl.ANY)] * 3
        operands += list(previous)
    return pl.pallas_call(
        functools.partial(project_kernel, heads, count),
        grid_spec=pltpu.PrefetchScalarGridSpec(
            num_scalar_prefetch=1,
            grid=(count, steps),
            in_specs=in_specs,
            out_specs=[out_spec] * 3,
        ),
        out_shape=[shape] * 3,
        input_output_aliases=aliases,
        compiler_params=pltpu.CompilerParams(vmem_limit_bytes=40 << 20),
        name="project",
    )(order, *operands)


def attend_kernel(passes, block, q_ref, k_ref, v_ref, out_ref, q_next_ref, held):
    heads = q_ref.shape[0]
    blocks = k_ref.shape[2] // block
    step = pl.program_id(0)
    row = lax.broadcasted_iota(jnp.int32, (block, block), 0)
    col = lax.broadcasted_iota(jnp.int32, (block, block), 1)
    causal = col <= row

    def one_head(head, count):
        for query_pass in range(passes):
            query = q_ref[head, query_pass]
            highest = None
            kept = []
            for key_pass in range(query_pass + 1):
                for tile in range(count):
                    scores = dot_nt(query, k_ref[head, key_pass, tile * block : (tile + 1) * block, :])
                    if tile == count - 1:
                        scores = jnp.where(causal, scores, MASKED)
                    kept.append(scores)
                    for lane in range(0, block, LANES):
                        part = scores[:, lane : lane + LANES]
                        highest = part if highest is None else jnp.maximum(highest, part)
            highest = jnp.max(highest, axis=-1, keepdims=True)
            total = None
            for index, scores in enumerate(kept):
                key_pass, tile = divmod(index, count)
                weights = jnp.exp(scores - highest).astype(bfloat)
                term = dot_nn(weights, v_ref[head, key_pass, tile * block : (tile + 1) * block, :])
                total = term if total is None else total + term
            row_sum = total[:, DELTA_COL : DELTA_COL + 1]
            log_sum = highest + jnp.log(row_sum)
            q_next_ref[head, query_pass] = with_columns(
                query.astype(single), STAT_COL, three_parts(-log_sum)
            ).astype(bfloat)
            held[head, query_pass] = total * (1.0 / row_sum)

    for index in range(blocks):

        @pl.when(step == index)
        def _():
            lax.fori_loop(0, heads, lambda head, _: (one_head(head, index + 1), 0)[1], 0)

    for query_pass in range(passes):
        out_ref[query_pass] = pack_heads([held[head, query_pass] for head in range(heads)]).astype(bfloat)


def attend(queries, keys, values):
    heads, passes, length, _ = queries.shape
    block = min(256, length)
    whole = pl.BlockSpec(keys.shape, lambda step: (0, 0, 0, 0), pipeline_mode=pl.Buffered(1))
    part = pl.BlockSpec((heads, passes, block, LANES), lambda step: (0, 0, step, 0))
    packed = heads * HEAD_DIM
    return pl.pallas_call(
        functools.partial(attend_kernel, passes, block),
        grid=(length // block,),
        in_specs=[part, whole, whole],
        out_specs=[pl.BlockSpec((passes, block, packed), lambda step: (0, step, 0)), part],
        out_shape=[
            jax.ShapeDtypeStruct((passes, length, packed), bfloat),
            jax.ShapeDtypeStruct(queries.shape, bfloat),
        ],
        scratch_shapes=[pltpu.VMEM((heads, passes, block, LANES), single)],
        compiler_params=pltpu.CompilerParams(vmem_limit_bytes=56 << 20),
        name="attend",
    )(queries, keys, values)


def attend_back_kernel(
    passes, block, me_ref, q_ref, out_ref, k_ref, v_ref, grad_a, grad_b, grad_c, grad_d, all_ref, *scratch
):
    grad_refs = (grad_a, grad_b, grad_c, grad_d)
    key_acc, value_acc, grad_held, query_held = scratch
    heads = q_ref.shape[0]
    blocks = k_ref.shape[2] // block
    step = pl.program_id(0)
    me = me_ref[0]
    row = lax.broadcasted_iota(jnp.int32, (block, block), 0)
    col = lax.broadcasted_iota(jnp.int32, (block, block), 1)
    causal = row <= col
    inside = lax.broadcasted_iota(jnp.int32, (block, LANES), 1) < HEAD_DIM

    @pl.when(step == 0)
    def _():
        key_acc[...] = jnp.zeros(key_acc.shape, single)
        value_acc[...] = jnp.zeros(value_acc.shape, single)

    padded = ((heads * HEAD_DIM + LANES - 1) // LANES) * LANES
    for slot in range(passes):
        query_pass = jnp.bitwise_xor(me, slot)
        grad = grad_refs[slot][...].astype(single)
        out = out_ref[query_pass].astype(single)
        tail = jnp.zeros((block, padded - heads * HEAD_DIM), single)
        if padded > heads * HEAD_DIM:
            grad = jnp.concatenate([grad, tail], axis=1)
            out = jnp.concatenate([out, tail], axis=1)
        product = grad * out
        for head in range(heads):
            delta = jnp.sum(
                jnp.where(inside, head_slab(product, head), 0.0), axis=-1, keepdims=True
            )
            base = jnp.where(inside, head_slab(grad, head), 0.0)
            grad_held[head, query_pass] = with_columns(base, DELTA_COL, three_parts(-delta)).astype(bfloat)

    def one_head(head, count):
        query_sums = [None] * passes
        for key_pass in range(passes):
            span = passes - key_pass
            query = q_ref[head, key_pass:passes].reshape(span * block, LANES)
            grad = grad_held[head, key_pass:passes].reshape(span * block, LANES)
            for tile in range(count):
                window = slice(tile * block, (tile + 1) * block)
                key = k_ref[head, key_pass, window, :]
                value = v_ref[head, key_pass, window, :]
                prob = jnp.exp(dot_nt(key, query))
                if tile == count - 1:
                    prob = jnp.where(jnp.concatenate([causal] * span, axis=1), prob, 0.0)
                value_acc[head, key_pass, window, :] += dot_nn(prob.astype(bfloat), grad)
                score_grad = (prob * dot_nt(value, grad)).astype(bfloat)
                key_acc[head, key_pass, window, :] += dot_nn(score_grad, query)
                term = dot_tn(key, score_grad)
                for query_pass in range(key_pass, passes):
                    first = (query_pass - key_pass) * block
                    part = term[:, first : first + block]
                    old = query_sums[query_pass]
                    query_sums[query_pass] = part if old is None else old + part
        for query_pass in range(passes):
            query_held[head, query_pass] = query_sums[query_pass].T * (HEAD_DIM**-0.5)

    for index in range(blocks):

        @pl.when(step == blocks - 1 - index)
        def _():
            lax.fori_loop(0, heads, lambda head, _: (one_head(head, index + 1), 0)[1], 0)
            window = slice(index * block, (index + 1) * block)
            for query_pass in range(passes):
                slabs = [query_held[head, query_pass] for head in range(heads)]
                slabs += [key_acc[head, query_pass, window, :] for head in range(heads)]
                slabs += [value_acc[head, query_pass, window, :] for head in range(heads)]
                all_ref[query_pass] = pack_heads(slabs).astype(bfloat)


def attend_back(me, queries, outs, keys, values, grads):
    heads, passes, length, _ = queries.shape
    block = min(256, length)
    steps = length // block
    packed = heads * HEAD_DIM
    whole = pl.BlockSpec(keys.shape, lambda step, me_ref: (0, 0, 0, 0), pipeline_mode=pl.Buffered(1))
    part = pl.BlockSpec((heads, passes, block, LANES), lambda step, me_ref: (0, 0, steps - 1 - step, 0))
    return pl.pallas_call(
        functools.partial(attend_back_kernel, passes, block),
        grid_spec=pltpu.PrefetchScalarGridSpec(
            num_scalar_prefetch=1,
            grid=(steps,),
            in_specs=[
                part,
                pl.BlockSpec((passes, block, packed), lambda step, me_ref: (0, steps - 1 - step, 0)),
                whole,
                whole,
            ]
            + [pl.BlockSpec((block, packed), lambda step, me_ref: (steps - 1 - step, 0))] * passes,
            out_specs=pl.BlockSpec(
                (passes, block, 3 * packed), lambda step, me_ref: (0, steps - 1 - step, 0)
            ),
            scratch_shapes=[
                pltpu.VMEM(keys.shape, single),
                pltpu.VMEM(keys.shape, single),
                pltpu.VMEM((heads, passes, block, LANES), bfloat),
                pltpu.VMEM((heads, passes, block, LANES), single),
            ],
        ),
        out_shape=jax.ShapeDtypeStruct((passes, length, 3 * packed), bfloat),
        compiler_params=pltpu.CompilerParams(vmem_limit_bytes=60 << 20),
        name="attend_back",
    )(me, queries, outs, keys, values, *grads)


def middle_kernel(groups, chunks, me_ref, *refs):
    parts = refs[:groups]
    (
        x_ref,
        cot_ref,
        pass_ref,
        w_out_ref,
        w_up_ref,
        w_down_ref,
        out_bias_ref,
        gain_ref,
        shift_ref,
        up_bias_ref,
        down_bias_ref,
    ) = refs[groups : groups + 11]
    outs = refs[groups + 11 :]
    rows_ref, mixed_grad_ref, normed_ref, active_ref, upper_ref, proj_ref, sums_ref, up_sum_ref = outs[:8]
    grads = outs[8:]
    me = me_ref[0]
    width = x_ref.shape[1]
    packed = width // groups
    step = pl.program_id(0)

    def group_window(slot):
        start = pl.multiple_of(jnp.bitwise_xor(me, slot) * packed, packed)
        return pl.ds(start, packed)

    mixed = x_ref[...].astype(single) + pass_ref[...] + out_bias_ref[...]
    for slot in range(groups):
        mixed += dot_nn(parts[slot][...], w_out_ref[group_window(slot), :])
    normed, inverse = norm_parts(mixed)
    low = (normed * gain_ref[...] + shift_ref[...]).astype(bfloat)
    normed_ref[...] = low
    down_low = cot_ref[...]
    out_grad = down_low.astype(single)
    total = mixed + down_bias_ref[...]
    back = jnp.zeros_like(mixed)
    hidden = w_up_ref.shape[1]
    size = hidden // chunks
    up_sums = []
    for chunk in range(chunks):
        window = slice(chunk * size, (chunk + 1) * size)
        upper = dot_nn(low, w_up_ref[:, window]) + up_bias_ref[:, window]
        below = 0.5 + 0.5 * lax.erf(upper * (0.5**0.5))
        density = jnp.exp(-0.5 * upper * upper) * 0.3989422804014327
        active = (upper * below).astype(bfloat)
        active_ref[:, window] = active
        total += dot_nn(active, w_down_ref[window, :])
        grad = dot_nt(down_low, w_down_ref[window, :]) * (below + upper * density)
        upper_low = grad.astype(bfloat)
        upper_ref[:, window] = upper_low
        up_sums.append(jnp.sum(upper_low.astype(single), axis=0, keepdims=True))
        back += dot_nt(upper_low, w_up_ref[:, window])
    rows_ref[...] = total.astype(bfloat)
    mixed_grad = out_grad + norm_back(back, gain_ref[...], normed, inverse)
    mixed_grad_ref[...] = mixed_grad
    proj_low = mixed_grad.astype(bfloat)
    proj_ref[...] = proj_low
    for slot in range(groups):
        grads[slot][...] = dot_nt(proj_low, w_out_ref[group_window(slot), :]).astype(bfloat)

    @pl.when(step == 0)
    def _():
        sums_ref[...] = jnp.zeros(sums_ref.shape, single)
        up_sum_ref[...] = jnp.zeros(up_sum_ref.shape, single)

    def column_sum(values):
        return jnp.sum(values, axis=0, keepdims=True)

    sums_ref[0:1, :] += column_sum(mixed_grad)
    sums_ref[1:2, :] += column_sum(back * normed)
    sums_ref[2:3, :] += column_sum(back)
    sums_ref[3:4, :] += column_sum(out_grad)
    up_sum_ref[...] += jnp.concatenate(up_sums, axis=1)


def middle(me, parts, x_own, cot, pass_row, w_out, w_up, w_down, out_bias, gain, shift, up_bias, down_bias):
    length, width = x_own.shape
    hidden = w_up.shape[1]
    groups = len(parts)
    packed = width // groups
    block = min(256, length)

    def rows(size):
        return pl.BlockSpec((block, size), lambda step, me_ref: (step, 0))

    def whole(shape):
        return pl.BlockSpec(shape, lambda step, me_ref: (0, 0), pipeline_mode=pl.Buffered(1))

    def fixed(shape):
        return pl.BlockSpec(shape, lambda step, me_ref: (0, 0))

    struct = jax.ShapeDtypeStruct
    operands = (x_own, cot, pass_row, w_out, w_up, w_down, out_bias, gain, shift, up_bias, down_bias)
    return pl.pallas_call(
        functools.partial(middle_kernel, groups, 4),
        grid_spec=pltpu.PrefetchScalarGridSpec(
            num_scalar_prefetch=1,
            grid=(length // block,),
            in_specs=[rows(packed)] * groups
            + [rows(width), rows(width)]
            + [whole(operand.shape) for operand in operands[2:]],
            out_specs=[
                rows(width),
                rows(width),
                rows(width),
                rows(hidden),
                rows(hidden),
                rows(width),
                fixed((8, width)),
                fixed((1, hidden)),
            ]
            + [rows(packed)] * groups,
        ),
        out_shape=[
            struct((length, width), bfloat),
            struct((length, width), single),
            struct((length, width), bfloat),
            struct((length, hidden), bfloat),
            struct((length, hidden), bfloat),
            struct((length, width), bfloat),
            struct((8, width), single),
            struct((1, hidden), single),
        ]
        + [struct((length, packed), bfloat)] * groups,
        compiler_params=pltpu.CompilerParams(vmem_limit_bytes=60 << 20),
        name="middle",
    )(me, *parts, *operands)


def project_back_kernel(count, me_ref, *refs):
    pieces = refs[:count]
    pass_ref, gain_ref, shift_ref, weight_ref, grad_ref = refs[count : count + 5]
    rows_ref, weight_grad_ref, sums_ref, bias_ref, pass_sum_ref = refs[count + 5 :]
    slot = pl.program_id(0)
    step = pl.program_id(1)
    pass_index = me_ref[1 + slot]
    rows = pieces[0][...]
    for index in range(1, count):
        rows = jnp.where(slot == index, pieces[index][...], rows)
    normed, inverse = norm_parts(rows.astype(single) + pass_ref[pl.ds(pass_index, 1), :])
    low = (normed * gain_ref[...] + shift_ref[...]).astype(bfloat)
    grad = grad_ref[...]
    back = dot_nt(grad, weight_ref[...])
    part = norm_back(back, gain_ref[...], normed, inverse)
    rows_ref[...] = part.astype(bfloat)

    def column_sum(values):
        return jnp.sum(values, axis=0, keepdims=True)

    @pl.when((slot == 0) & (step == 0))
    def _():
        weight_grad_ref[...] = jnp.zeros(weight_grad_ref.shape, single)
        sums_ref[...] = jnp.zeros(sums_ref.shape, single)
        bias_ref[...] = jnp.zeros(bias_ref.shape, single)
        pass_sum_ref[...] = jnp.zeros(pass_sum_ref.shape, single)

    weight_grad_ref[...] += dot_tn(low, grad)
    sums_ref[0:1, :] += column_sum(back * normed)
    sums_ref[1:2, :] += column_sum(back)
    bias_ref[...] += column_sum(grad.astype(single))
    pass_sum_ref[pl.ds(pass_index, 1), :] += column_sum(part)


def project_back(order, pieces, pass_emb, gain, shift, weight, grads):
    count = len(pieces)
    length, width = pieces[0].shape
    passes, _, packed = grads.shape
    block = min(512, length)
    steps = length // block

    def piece_spec(index):
        def where(slot, step, order_ref):
            return (jnp.where(slot == index, step, jnp.where(slot < index, 0, steps - 1)), 0)

        return pl.BlockSpec((block, width), where)

    def whole(shape):
        return pl.BlockSpec(shape, lambda slot, step, order_ref: (0,) * len(shape))

    struct = jax.ShapeDtypeStruct
    return pl.pallas_call(
        functools.partial(project_back_kernel, count),
        grid_spec=pltpu.PrefetchScalarGridSpec(
            num_scalar_prefetch=1,
            grid=(count, steps),
            in_specs=[piece_spec(index) for index in range(count)]
            + [
                whole(pass_emb.shape),
                whole(gain.shape),
                whole(shift.shape),
                whole(weight.shape),
                pl.BlockSpec(
                    (pl.Squeezed(), block, packed),
                    lambda slot, step, order_ref: (order_ref[1 + slot], step, 0),
                ),
            ],
            out_specs=[
                pl.BlockSpec((pl.Squeezed(), block, width), lambda slot, step, order_ref: (slot, step, 0)),
                whole((width, packed)),
                whole((8, width)),
                whole((1, packed)),
                whole((passes, width)),
            ],
        ),
        out_shape=[
            struct((passes, length, width), bfloat),
            struct((width, packed), single),
            struct((8, width), single),
            struct((1, packed), single),
            struct((passes, width), single),
        ],
        compiler_params=pltpu.CompilerParams(vmem_limit_bytes=48 << 20),
        name="project_back",
    )(order, *pieces, pass_emb, gain, shift, weight, grads)


def per_device(
    x_rows,
    pass_depth,
    cotangent,
    pass_emb,
    ln1_gain,
    ln1_bias,
    w_qkv,
    q_bias,
    v_bias,
    w_out,
    out_bias,
    ln2_gain,
    ln2_bias,
    w_up,
    up_bias,
    w_down,
    down_bias,
):
    everyone = ("seq", "pass")
    _, length, width = x_rows.shape
    hidden = w_up.shape[1]
    passes = lax.axis_size("pass")
    devices = passes * lax.axis_size("seq")
    shard = w_qkv.shape[0]
    group = width // passes
    group_heads = group // HEAD_DIM
    me = lax.axis_index("pass")
    order = jnp.concatenate([me[None], jnp.bitwise_xor(me, jnp.arange(passes))]).astype(jnp.int32)

    def swap(value, distance):
        return lax.ppermute(value, "pass", [(k, k ^ distance) for k in range(passes)])

    x_own = x_rows[0]
    x_one = swap(x_own, 1)
    x_two = swap(x_own, 2)
    x_three = swap(x_two, 1)

    by_group = w_qkv.reshape(shard, 3, passes, group).transpose(2, 0, 1, 3).reshape(passes, shard, 3 * group)
    by_rows = lax.all_to_all(by_group, "pass", 0, 0, tiled=True).reshape(passes * shard, 3 * group)
    w_heads = lax.all_gather(by_rows, "seq", axis=0, tiled=True)

    down_cols = w_down.reshape(passes, shard, width).transpose(1, 0, 2).reshape(shard, hidden)
    gathered = lax.all_gather(
        jnp.concatenate([w_out, w_up, down_cols], axis=1), everyone, axis=0, tiled=True
    )
    full_out = gathered[:, :width]
    full_up = gathered[:, width : width + hidden]
    full_down = (
        gathered[:, width + hidden :]
        .reshape(devices, shard, hidden // width, width)
        .transpose(0, 2, 1, 3)
        .reshape(hidden, width)
    )

    gain_one, shift_one = ln1_gain[None], ln1_bias[None]
    own_q_bias = lax.dynamic_slice_in_dim(q_bias, me * group, group)
    own_v_bias = lax.dynamic_slice_in_dim(v_bias, me * group, group)
    bias_row = jnp.concatenate([own_q_bias, jnp.zeros((group,), single), own_v_bias])[None]
    pad = (-3 * group) % LANES
    w_wide = jnp.pad(w_heads, ((0, 0), (0, pad)))
    bias_wide = jnp.pad(bias_row, ((0, 0), (0, pad)))
    depth = pass_depth.reshape(length, 1)
    near = project(
        order[:3], (x_own, x_one), passes, pass_emb, gain_one, shift_one, w_wide, bias_wide, depth, None
    )
    far_order = jnp.concatenate([order[:1], order[3:]])
    queries, keys, values = project(
        far_order, (x_two, x_three), passes, pass_emb, gain_one, shift_one, w_wide, bias_wide, depth, near
    )

    outs, queries = attend(queries, keys, values)

    def slot_of(value, slot):
        return lax.dynamic_index_in_dim(value, order[1 + slot], 0, keepdims=False)

    parts = [slot_of(outs, 0)] + [swap(slot_of(outs, slot), slot) for slot in range(1, passes)]
    pass_row = lax.dynamic_index_in_dim(pass_emb, me, 0, keepdims=True)
    (
        out_rows,
        mixed_grad,
        normed_two,
        activated,
        upper_low,
        proj_low,
        sums,
        up_sum,
        *head_grads,
    ) = middle(
        order[:1],
        parts,
        x_own,
        cotangent[0],
        pass_row,
        full_out,
        full_up,
        full_down,
        out_bias[None],
        ln2_gain[None],
        ln2_bias[None],
        up_bias[None],
        down_bias[None],
    )
    head_grads = [head_grads[0]] + [swap(head_grads[slot], slot) for slot in range(1, passes)]

    by_slot = jnp.stack([dot_tn(part, proj_low) for part in parts]).astype(bfloat)
    out_weight = jnp.concatenate([slot_of(by_slot, slot) for slot in range(passes)], axis=0)
    up_weight = dot_tn(normed_two, upper_low).astype(bfloat)
    down_weight = dot_tn(activated, cotangent[0]).astype(bfloat)
    down_weight = (
        down_weight.reshape(devices, hidden // width, shard, width)
        .transpose(0, 2, 1, 3)
        .reshape(width, hidden)
    )
    reduced = lax.psum_scatter(
        jnp.concatenate([out_weight, up_weight, down_weight], axis=1),
        everyone,
        scatter_dimension=0,
        tiled=True,
    ).astype(single)
    shard_out = reduced[:, :width]
    shard_up = reduced[:, width : width + hidden]
    shard_down = (
        reduced[:, width + hidden :]
        .reshape(shard, hidden // width, width)
        .transpose(1, 0, 2)
        .reshape(w_down.shape)
    )

    qkv_low = attend_back(order[:1], queries, outs, keys, values, head_grads)
    row_parts, head_weight, sums_one, head_bias, pass_sums = project_back(
        order, (x_own, x_one, x_two, x_three), pass_emb, gain_one, shift_one, w_heads, qkv_low
    )

    near_part = swap(row_parts[1], 1)
    far_part = swap(row_parts[3], 1)
    far_sum = (row_parts[2].astype(single) + far_part.astype(single)).astype(bfloat)
    far_sum = swap(far_sum, 2)
    x_grad = (
        mixed_grad
        + row_parts[0].astype(single)
        + near_part.astype(single)
        + far_sum.astype(single)
    )

    scattered = lax.psum_scatter(head_weight, "seq", scatter_dimension=0, tiled=True)
    scattered = scattered.reshape(passes, shard, 3 * group)
    shard_qkv = lax.all_to_all(scattered, "pass", 0, 0, tiled=True)
    shard_qkv = shard_qkv.reshape(passes, shard, 3, group).transpose(1, 2, 0, 3).reshape(w_qkv.shape)

    own_pass = (jnp.arange(passes) == me).astype(single)[:, None]
    pass_part = pass_sums + own_pass * sums[0:1]

    def placed(row):
        return lax.dynamic_update_slice(jnp.zeros((width,), single), row, (me * group,))

    totals = lax.psum(
        jnp.concatenate(
            [
                placed(head_bias[0, :group]),
                placed(head_bias[0, 2 * group :]),
                sums[0],
                sums_one[0],
                sums_one[1],
                sums[1],
                sums[2],
                up_sum[0],
                sums[3],
                pass_part.reshape(-1),
            ]
        ).reshape(-1, width),
        everyone,
    )
    up_rows = hidden // width
    pass_grad = lax.dynamic_slice_in_dim(totals[8 + up_rows :], me, 1, 0)
    return (
        out_rows[None],
        x_grad[None],
        shard_qkv,
        totals[0],
        totals[1],
        shard_out,
        totals[2],
        totals[3],
        totals[4],
        totals[5],
        totals[6],
        shard_up,
        totals[7 : 7 + up_rows].reshape(-1),
        shard_down,
        totals[7 + up_rows],
        pass_grad,
    )


def solution(mesh):
    placed = (
        P("pass", "seq", None),
        P("seq", None),
        P("pass", "seq", None),
        P(),
        P(),
        P(),
        P(("seq", "pass"), None),
        P(),
        P(),
        P(("seq", "pass"), None),
        P(),
        P(),
        P(),
        P(("seq", "pass"), None),
        P(),
        P(("seq", "pass"), None),
        P(),
    )
    return jax.shard_map(
        per_device,
        mesh=mesh,
        in_specs=placed,
        out_specs=(
            P("pass", "seq", None),
            P("pass", "seq", None),
            P(("seq", "pass"), None),
            P(),
            P(),
            P(("seq", "pass"), None),
            P(),
            P(),
            P(),
            P(),
            P(),
            P(("seq", "pass"), None),
            P(),
            P(("seq", "pass"), None),
            P(),
            P("pass", None),
        ),
        check_vma=False,
    )
```

```python
import functools

import jax
import jax.numpy as jnp
from jax import lax
from jax.experimental import pallas as pl
from jax.experimental.pallas import tpu as pltpu
from jax.sharding import PartitionSpec as P

HEADS = 12
HEAD_DIM = 64
LANES = 128
NORM_EPS = 1e-05
MASKED = -1e30
BIAS_COL = 64
STAT_COL = 65
DELTA_COL = 64

bfloat = jnp.bfloat16
single = jnp.float32


def in_hbm(shape, dtype):
    return pltpu.HBM(shape, dtype)


def from_hbm(values):
    return [pltpu.with_memory_space_constraint(value, pltpu.HBM) for value in values]


def dot_nn(a, b):
    return jnp.dot(a, b, preferred_element_type=single)


def dot_nt(a, b):
    return lax.dot_general(a, b, (((1,), (1,)), ((), ())), preferred_element_type=single)


def dot_tn(a, b):
    return lax.dot_general(a, b, (((0,), (0,)), ((), ())), preferred_element_type=single)


def three_parts(value):
    first = value.astype(bfloat).astype(single)
    rest = value - first
    second = rest.astype(bfloat).astype(single)
    return first, second, rest - second


def with_columns(base, start, columns):
    lane = lax.broadcasted_iota(jnp.int32, base.shape, 1)
    for offset, column in enumerate(columns):
        base = jnp.where(lane == start + offset, column, base)
    return base


def norm_parts(values):
    center = values - jnp.mean(values, axis=-1, keepdims=True)
    inverse = lax.rsqrt(jnp.mean(center * center, axis=-1, keepdims=True) + NORM_EPS)
    return center * inverse, inverse


def norm_back(grad, gain, normed, inverse):
    scaled = grad * gain
    mean_one = jnp.mean(scaled, axis=-1, keepdims=True)
    mean_two = jnp.mean(scaled * normed, axis=-1, keepdims=True)
    return inverse * (scaled - mean_one - normed * mean_two)


def head_slab(packed, index):
    low = (index // 2) * LANES
    slab = packed[:, low : low + LANES]
    if index % 2:
        slab = pltpu.roll(slab, HEAD_DIM, axis=1)
    return slab


def pack_heads(slabs):
    packed = []
    lane = lax.broadcasted_iota(jnp.int32, slabs[0].shape, 1)
    for index in range(0, len(slabs), 2):
        if index + 1 < len(slabs):
            other = pltpu.roll(slabs[index + 1], HEAD_DIM, axis=1)
            packed.append(jnp.where(lane < HEAD_DIM, slabs[index], other))
        else:
            packed.append(slabs[index])
    width = len(slabs) * HEAD_DIM
    return jnp.concatenate(packed, axis=1)[:, :width]


def project_kernel(heads, count, me_ref, *refs):
    pieces = refs[:count]
    pass_ref, gain_ref, shift_ref, weight_ref, bias_ref, depth_ref = refs[count : count + 6]
    q_ref, k_ref, v_ref, stats_ref = refs[-4:]
    slot = pl.program_id(0)
    pass_index = me_ref[1 + slot]
    pass_row = pass_ref[pl.ds(pass_index, 1), :]
    rows = pieces[0][...]
    for index in range(1, count):
        rows = jnp.where(slot == index, pieces[index][...], rows)
    rows = rows.astype(single) + pass_row
    mean = jnp.mean(rows, axis=-1, keepdims=True)
    center = rows - mean
    inverse = lax.rsqrt(jnp.mean(center * center, axis=-1, keepdims=True) + NORM_EPS)
    lane = lax.broadcasted_iota(jnp.int32, stats_ref.shape, 1)
    stats_ref[...] = jnp.where(lane == 0, inverse, -mean * inverse)
    low = (center * inverse * gain_ref[...] + shift_ref[...]).astype(bfloat)
    projected = dot_nn(low, weight_ref[...]) + bias_ref[...]
    lane = lax.broadcasted_iota(jnp.int32, (low.shape[0], LANES), 1)
    inside = lane < HEAD_DIM
    depth_bias = jnp.where(pass_index < depth_ref[...], 0.0, MASKED)
    q_rest = jnp.where(lane == BIAS_COL, 1.0, 0.0)
    k_rest = jnp.where(
        lane == BIAS_COL, depth_bias, jnp.where((lane >= STAT_COL) & (lane < STAT_COL + 3), 1.0, 0.0)
    )
    v_rest = jnp.where((lane >= DELTA_COL) & (lane < DELTA_COL + 3), 1.0, 0.0)
    for head in range(heads):
        q_part = head_slab(projected, head).astype(bfloat).astype(single) * (HEAD_DIM**-0.5)
        q_ref[head] = jnp.where(inside, q_part, q_rest).astype(bfloat)
        k_ref[head] = jnp.where(inside, head_slab(projected, heads + head), k_rest).astype(bfloat)
        v_ref[head] = jnp.where(inside, head_slab(projected, 2 * heads + head), v_rest).astype(bfloat)


def project(order, pieces, passes, pass_emb, gain, shift, weight, bias, depth, previous):
    count = len(pieces)
    length, width = pieces[0].shape
    heads = weight.shape[1] // (3 * HEAD_DIM)
    block = min(512, length)
    steps = length // block

    def piece_spec(index):
        def where(slot, step, order_ref):
            return (jnp.where(slot == index, step, jnp.where(slot < index, 0, steps - 1)), 0)

        return pl.BlockSpec((block, width), where)

    def whole(shape):
        return pl.BlockSpec(shape, lambda slot, step, order_ref: (0,) * len(shape))

    out_spec = pl.BlockSpec(
        (heads, pl.Squeezed(), block, LANES),
        lambda slot, step, order_ref: (0, order_ref[1 + slot], step, 0),
    )
    shape = in_hbm((heads, passes, length, LANES), bfloat)
    stats_spec = pl.BlockSpec(
        (pl.Squeezed(), block, 2), lambda slot, step, order_ref: (order_ref[1 + slot], step, 0)
    )
    in_specs = [piece_spec(index) for index in range(count)] + [
        whole(pass_emb.shape),
        whole(gain.shape),
        whole(shift.shape),
        whole(weight.shape),
        whole(bias.shape),
        pl.BlockSpec((block, 1), lambda slot, step, order_ref: (step, 0)),
    ]
    operands = [*pieces, pass_emb, gain, shift, weight, bias, depth]
    aliases = {}
    if previous is not None:
        aliases = {1 + len(operands) + index: index for index in range(4)}
        in_specs += [pl.BlockSpec(memory_space=pl.ANY)] * 4
        operands += list(previous)
    return pl.pallas_call(
        functools.partial(project_kernel, heads, count),
        grid_spec=pltpu.PrefetchScalarGridSpec(
            num_scalar_prefetch=1,
            grid=(count, steps),
            in_specs=in_specs,
            out_specs=[out_spec] * 3 + [stats_spec],
        ),
        out_shape=[shape] * 3 + [in_hbm((passes, length, 2), single)],
        input_output_aliases=aliases,
        compiler_params=pltpu.CompilerParams(vmem_limit_bytes=40 << 20),
        cost_estimate=pl.CostEstimate(flops=8 << 30, transcendentals=0, bytes_accessed=12 << 20),
        name="project",
    )(order, *operands)


def attend_kernel(passes, block, first, last, me_ref, q_ref, k_ref, v_ref, *refs):
    out_refs, q_next_ref, held = refs[:passes], refs[passes], refs[passes + 1]
    heads = q_ref.shape[0]
    step = pl.program_id(0)
    row = lax.broadcasted_iota(jnp.int32, (block, block), 0)
    col = lax.broadcasted_iota(jnp.int32, (block, block), 1)
    causal = col <= row

    def one_head(head, count):
        for query_pass in range(passes):
            query = q_ref[head, query_pass]
            highest = None
            kept = []
            for key_pass in range(query_pass + 1):
                for tile in range(count):
                    scores = dot_nt(query, k_ref[head, key_pass, tile * block : (tile + 1) * block, :])
                    if tile == count - 1:
                        scores = jnp.where(causal, scores, MASKED)
                    kept.append(scores)
                    for lane in range(0, block, LANES):
                        part = scores[:, lane : lane + LANES]
                        highest = part if highest is None else jnp.maximum(highest, part)
            highest = jnp.max(highest, axis=-1, keepdims=True)
            total = None
            for index, scores in enumerate(kept):
                key_pass, tile = divmod(index, count)
                weights = jnp.exp(scores - highest).astype(bfloat)
                term = dot_nn(weights, v_ref[head, key_pass, tile * block : (tile + 1) * block, :])
                total = term if total is None else total + term
            row_sum = total[:, DELTA_COL : DELTA_COL + 1]
            log_sum = highest + jnp.log(row_sum)
            q_next_ref[head, query_pass] = with_columns(
                query.astype(single), STAT_COL, three_parts(-log_sum)
            ).astype(bfloat)
            held[head, query_pass] = total * (1.0 / row_sum)

    for index in range(first, last):

        @pl.when(step == index - first)
        def _():
            lax.fori_loop(0, heads, lambda head, _: (one_head(head, index + 1), 0)[1], 0)

    for slot in range(passes):
        query_pass = jnp.bitwise_xor(me_ref[0], slot)
        out_refs[slot][...] = pack_heads([held[head, query_pass] for head in range(heads)]).astype(bfloat)


def attend(me, queries, keys, values, half):
    heads, passes, length, _ = queries.shape
    block = min(256, length // 2)
    count = length // 2 // block
    first, last = half * count, (half + 1) * count
    seen = pl.BlockSpec(
        (heads, passes, last * block, LANES),
        lambda step, me_ref: (0, 0, 0, 0),
        pipeline_mode=pl.Buffered(1),
    )
    part = pl.BlockSpec((heads, passes, block, LANES), lambda step, me_ref: (0, 0, first + step, 0))
    part_out = pl.BlockSpec((heads, passes, block, LANES), lambda step, me_ref: (0, 0, step, 0))
    packed = heads * HEAD_DIM
    *outs, queries = pl.pallas_call(
        functools.partial(attend_kernel, passes, block, first, last),
        grid_spec=pltpu.PrefetchScalarGridSpec(
            num_scalar_prefetch=1,
            grid=(count,),
            in_specs=[part, seen, seen],
            out_specs=[pl.BlockSpec((block, packed), lambda step, me_ref: (step, 0))] * passes + [part_out],
            scratch_shapes=[pltpu.VMEM((heads, passes, block, LANES), single)],
        ),
        out_shape=[in_hbm((length // 2, packed), bfloat)] * passes
        + [in_hbm((heads, passes, length // 2, LANES), bfloat)],
        compiler_params=pltpu.CompilerParams(vmem_limit_bytes=48 << 20),
        cost_estimate=pl.CostEstimate(
            flops=(10 + 20 * half) << 30,
            transcendentals=heads * (1 + 2 * half) * length * length,
            bytes_accessed=12 << 20,
        ),
        name="attend",
    )(me, *from_hbm((queries, keys, values)))
    return outs, queries


def attend_back_kernel(passes, block, me_ref, *refs):
    q_refs, (k_ref, v_ref), refs = refs[:2], refs[2:4], refs[4:]
    out_refs = refs[:passes], refs[passes : 2 * passes]
    grad_refs = refs[2 * passes : 3 * passes], refs[3 * passes : 4 * passes]
    all_ref, key_acc, value_acc, grad_held, query_held = refs[4 * passes :]
    heads = k_ref.shape[0]
    blocks = k_ref.shape[2] // block
    step = pl.program_id(0)
    me = me_ref[0]
    row = lax.broadcasted_iota(jnp.int32, (block, block), 0)
    col = lax.broadcasted_iota(jnp.int32, (block, block), 1)
    causal = row <= col
    inside = lax.broadcasted_iota(jnp.int32, (block, LANES), 1) < HEAD_DIM
    padded = ((heads * HEAD_DIM + LANES - 1) // LANES) * LANES

    @pl.when(step == 0)
    def _():
        key_acc[...] = jnp.zeros(key_acc.shape, single)
        value_acc[...] = jnp.zeros(value_acc.shape, single)

    def prepare(half):
        for slot in range(passes):
            query_pass = jnp.bitwise_xor(me, slot)
            grad = grad_refs[half][slot][...].astype(single)
            out = out_refs[half][slot][...].astype(single)
            if padded > heads * HEAD_DIM:
                tail = jnp.zeros((block, padded - heads * HEAD_DIM), single)
                grad = jnp.concatenate([grad, tail], axis=1)
                out = jnp.concatenate([out, tail], axis=1)
            product = grad * out
            for head in range(heads):
                delta = jnp.sum(
                    jnp.where(inside, head_slab(product, head), 0.0), axis=-1, keepdims=True
                )
                base = jnp.where(inside, head_slab(grad, head), 0.0)
                grad_held[head, query_pass] = with_columns(base, DELTA_COL, three_parts(-delta)).astype(bfloat)

    def one_head(head, count, q_ref):
        query_sums = [None] * passes
        for key_pass in range(passes):
            span = passes - key_pass
            query = q_ref[head, key_pass:passes].reshape(span * block, LANES)
            grad = grad_held[head, key_pass:passes].reshape(span * block, LANES)
            for tile in range(count):
                window = slice(tile * block, (tile + 1) * block)
                key = k_ref[head, key_pass, window, :]
                value = v_ref[head, key_pass, window, :]
                prob = jnp.exp(dot_nt(key, query))
                if tile == count - 1:
                    prob = jnp.where(jnp.concatenate([causal] * span, axis=1), prob, 0.0)
                value_acc[head, key_pass, window, :] += dot_nn(prob.astype(bfloat), grad)
                score_grad = (prob * dot_nt(value, grad)).astype(bfloat)
                key_acc[head, key_pass, window, :] += dot_nn(score_grad, query)
                term = dot_tn(key, score_grad)
                for query_pass in range(key_pass, passes):
                    start = (query_pass - key_pass) * block
                    part = term[:, start : start + block]
                    old = query_sums[query_pass]
                    query_sums[query_pass] = part if old is None else old + part
        for query_pass in range(passes):
            query_held[head, query_pass] = query_sums[query_pass].T * (HEAD_DIM**-0.5)

    for index in range(blocks):

        @pl.when(step == blocks - 1 - index)
        def _():
            half = index // (blocks // 2)
            prepare(half)
            lax.fori_loop(0, heads, lambda head, _: (one_head(head, index + 1, q_refs[half]), 0)[1], 0)
            window = slice(index * block, (index + 1) * block)
            for query_pass in range(passes):
                slabs = [query_held[head, query_pass] for head in range(heads)]
                slabs += [key_acc[head, query_pass, window, :] for head in range(heads)]
                slabs += [value_acc[head, query_pass, window, :] for head in range(heads)]
                all_ref[query_pass] = pack_heads(slabs).astype(bfloat)


def attend_back(me, queries, keys, values, outs, grads):
    heads, passes, length, _ = keys.shape
    block = min(256, length // 2)
    count = length // 2 // block
    packed = heads * HEAD_DIM

    def spot(half):
        return lambda step: jnp.clip(2 * count - 1 - step - half * count, 0, count - 1)

    def query_spec(half):
        return pl.BlockSpec((heads, passes, block, LANES), lambda step, me_ref: (0, 0, spot(half)(step), 0))

    def rows_spec(half):
        return pl.BlockSpec((block, packed), lambda step, me_ref: (spot(half)(step), 0))

    whole = pl.BlockSpec(keys.shape, lambda step, me_ref: (0, 0, 0, 0), pipeline_mode=pl.Buffered(1))
    rows_specs = [rows_spec(half) for half in range(2) for _ in range(passes)]
    return pl.pallas_call(
        functools.partial(attend_back_kernel, passes, block),
        grid_spec=pltpu.PrefetchScalarGridSpec(
            num_scalar_prefetch=1,
            grid=(2 * count,),
            in_specs=[query_spec(0), query_spec(1), whole, whole] + rows_specs * 2,
            out_specs=pl.BlockSpec(
                (passes, block, 3 * packed), lambda step, me_ref: (0, 2 * count - 1 - step, 0)
            ),
            scratch_shapes=[
                pltpu.VMEM(keys.shape, single),
                pltpu.VMEM(keys.shape, single),
                pltpu.VMEM((heads, passes, block, LANES), bfloat),
                pltpu.VMEM((heads, passes, block, LANES), single),
            ],
        ),
        out_shape=in_hbm((passes, length, 3 * packed), bfloat),
        compiler_params=pltpu.CompilerParams(vmem_limit_bytes=58 << 20),
        cost_estimate=pl.CostEstimate(
            flops=300 << 30, transcendentals=heads * 6 * length * length, bytes_accessed=20 << 20
        ),
        name="attend_back",
    )(me, *from_hbm((*queries, keys, values, *outs[0], *outs[1], *grads[0], *grads[1])))


def middle_kernel(groups, chunks, shard, begins, me_ref, *refs):
    parts = refs[:groups]
    x_ref, cot_ref, pass_ref, out_bias_ref, gain_ref, shift_ref, up_bias_ref, down_bias_ref, w_out_ref = refs[
        groups : groups + 9
    ]
    refs = refs[groups + 9 :]
    w_up_refs, down_refs = refs[:chunks], refs[chunks : 2 * chunks]
    last_sums_ref = None if begins else refs[2 * chunks]
    outs = refs[-7 - groups :] if not shard else refs[-8 - groups : -1]
    rows_ref, mixed_grad_ref, normed_ref, active_ref, upper_ref, proj_ref, sums_ref = outs[:7]
    grads = outs[7:]
    w_down_ref = refs[-1] if shard else None
    me = me_ref[0]
    width = x_ref.shape[1]
    packed = width // groups
    step = pl.program_id(0)

    def group_window(slot):
        start = pl.multiple_of(jnp.bitwise_xor(me, slot) * packed, packed)
        return pl.ds(start, packed)

    @pl.when(step == 0)
    def _():
        sums_ref[...] = jnp.zeros(sums_ref.shape, single) if begins else last_sums_ref[...]
        if shard:
            def two_devices(index, _):
                start = pl.multiple_of(index * 2 * shard, 2 * shard)
                blocks = [ref[pl.ds(start, 2 * shard), :].astype(single) for ref in down_refs]
                pieces = [block[side * shard : (side + 1) * shard] for side in range(2) for block in blocks]
                start = pl.multiple_of(index * 2 * shard * chunks, 2 * shard * chunks)
                w_down_ref[pl.ds(start, 2 * shard * chunks), :] = jnp.concatenate(pieces, axis=0).astype(bfloat)
                return 0

            lax.fori_loop(0, width // (2 * shard), two_devices, 0)

    def w_down(chunk):
        return w_down_ref[chunk * width : (chunk + 1) * width, :] if shard else down_refs[chunk][...]

    mixed = x_ref[...].astype(single) + pass_ref[...] + out_bias_ref[...]
    for slot in range(groups):
        mixed += dot_nn(parts[slot][...], w_out_ref[group_window(slot), :])
    normed, inverse = norm_parts(mixed)
    low = (normed * gain_ref[...] + shift_ref[...]).astype(bfloat)
    normed_ref[...] = low
    down_low = cot_ref[...]
    out_grad = down_low.astype(single)
    total = mixed + down_bias_ref[...]
    back = jnp.zeros_like(mixed)
    up_sums = []
    for chunk in range(chunks):
        window = slice(chunk * width, (chunk + 1) * width)
        upper = dot_nn(low, w_up_refs[chunk][...]) + up_bias_ref[:, window]
        below = 0.5 + 0.5 * lax.erf(upper * (0.5**0.5))
        density = jnp.exp(-0.5 * upper * upper) * 0.3989422804014327
        active = (upper * below).astype(bfloat)
        active_ref[:, window] = active
        total += dot_nn(active, w_down(chunk))
        grad = dot_nt(down_low, w_down(chunk)) * (below + upper * density)
        upper_low = grad.astype(bfloat)
        upper_ref[:, window] = upper_low
        up_sums.append(jnp.sum(upper_low.astype(single), axis=0, keepdims=True))
        back += dot_nt(upper_low, w_up_refs[chunk][...])
    rows_ref[...] = total.astype(bfloat)
    mixed_grad = out_grad + norm_back(back, gain_ref[...], normed, inverse)
    mixed_grad_ref[...] = mixed_grad
    proj_low = mixed_grad.astype(bfloat)
    proj_ref[...] = proj_low
    for slot in range(groups):
        grads[slot][...] = dot_nt(proj_low, w_out_ref[group_window(slot), :]).astype(bfloat)

    def column_sum(values):
        return jnp.sum(values, axis=0, keepdims=True)

    sums_ref[0:1, :] += column_sum(mixed_grad)
    sums_ref[1:2, :] += column_sum(back * normed)
    sums_ref[2:3, :] += column_sum(back)
    sums_ref[3:4, :] += column_sum(out_grad)
    for chunk in range(chunks):
        sums_ref[4 + chunk : 5 + chunk, :] += up_sums[chunk]


def middle(
    me,
    parts,
    x_own,
    cot,
    pass_row,
    out_bias,
    gain,
    shift,
    up_bias,
    down_bias,
    gathered,
    w_down,
    shard,
    half,
    previous,
):
    length, width = x_own.shape
    hidden = up_bias.shape[1]
    chunks = hidden // width
    groups = len(parts)
    packed = width // groups
    block = min(256, length // 2)
    count = length // 2 // block

    def rows(size):
        return pl.BlockSpec((block, size), lambda step, me_ref: (half * count + step, 0))

    def half_rows(size):
        return pl.BlockSpec((block, size), lambda step, me_ref: (step, 0))

    def whole(shape, row=0, col=0):
        return pl.BlockSpec(shape, lambda step, me_ref: (row, col), pipeline_mode=pl.Buffered(1))

    def fixed(shape):
        return pl.BlockSpec(shape, lambda step, me_ref: (0, 0))

    sums_shape = ((4 + chunks + 7) // 8 * 8, width)
    square = (width, width)
    small = (pass_row, out_bias, gain, shift, up_bias, down_bias)
    if w_down is None:
        down_specs = [whole(square, 0, 1 + chunks + chunk) for chunk in range(chunks)]
        down = [gathered] * chunks
    else:
        down_specs = [whole(square, chunk, 0) for chunk in range(chunks)]
        down = [w_down] * chunks
        shard = None
    in_specs = (
        [half_rows(packed)] * groups
        + [rows(width), rows(width)]
        + [whole(operand.shape) for operand in small]
        + [whole(square, 0, col) for col in range(1 + chunks)]
        + down_specs
    )
    operands = [*from_hbm([*parts, x_own, cot]), *small, *from_hbm([gathered] * (1 + chunks) + down)]
    aliases = {}
    if previous is not None:
        in_specs += [fixed(sums_shape)] + [pl.BlockSpec(memory_space=pl.ANY)] * 6
        aliases = {2 + len(operands) + index: index for index in range(6)}
        operands += [previous[6], *previous[:6]]
    out_specs = [rows(width), rows(width), rows(width), rows(hidden), rows(hidden), rows(width), fixed(sums_shape)]
    out_shape = [
        in_hbm((length, width), bfloat),
        in_hbm((length, width), single),
        in_hbm((length, width), bfloat),
        in_hbm((length, hidden), bfloat),
        in_hbm((length, hidden), bfloat),
        in_hbm((length, width), bfloat),
        jax.ShapeDtypeStruct(sums_shape, single),
    ]
    out_specs += [half_rows(packed)] * groups
    out_shape += [in_hbm((length // 2, packed), bfloat)] * groups
    if shard:
        out_specs.append(fixed((hidden, width)))
        out_shape.append(in_hbm((hidden, width), bfloat))
    results = pl.pallas_call(
        functools.partial(middle_kernel, groups, chunks, shard, previous is None),
        grid_spec=pltpu.PrefetchScalarGridSpec(
            num_scalar_prefetch=1, grid=(count,), in_specs=in_specs, out_specs=out_specs
        ),
        out_shape=out_shape,
        input_output_aliases=aliases,
        compiler_params=pltpu.CompilerParams(vmem_limit_bytes=58 << 20),
        cost_estimate=pl.CostEstimate(
            flops=20 << 30, transcendentals=length * hidden, bytes_accessed=24 << 20
        ),
        name="middle",
    )(me, *operands)
    return results[:7], results[7 : 7 + groups], results[-1] if shard else w_down


def weight_grad_kernel(groups, chunks, shard, me_ref, *refs):
    early, late = refs[:groups], refs[groups : 2 * groups]
    proj_ref, normed_ref, cot_ref, upper_ref, active_ref, out_ref, held = refs[2 * groups :]
    middle_row = proj_ref.shape[0] // 2
    step = pl.program_id(0)
    width = proj_ref.shape[1]
    packed = width // groups

    @pl.when(step == 0)
    def _():
        for slot in range(groups):
            start = pl.multiple_of(jnp.bitwise_xor(me_ref[0], slot) * packed, packed)
            out_ref[pl.ds(start, packed), :] = (
                dot_tn(early[slot][...], proj_ref[:middle_row, :])
                + dot_tn(late[slot][...], proj_ref[middle_row:, :])
            ).astype(bfloat)

    @pl.when((step >= 1) & (step <= chunks))
    def _():
        out_ref[...] = dot_tn(normed_ref[...], upper_ref[...]).astype(bfloat)
        start = pl.multiple_of((step - 1) * width, width)
        held[pl.ds(start, width), :] = dot_tn(active_ref[...], cot_ref[...])

    @pl.when(step > chunks)
    def _():
        if shard:
            def two_devices(index, _):
                start = pl.multiple_of((index * 2 * chunks + step - 1 - chunks) * shard, 8)
                first = held[pl.ds(start, shard), :]
                second = held[pl.ds(pl.multiple_of(start + chunks * shard, 8), shard), :]
                start = pl.multiple_of(index * 2 * shard, 2 * shard)
                out_ref[pl.ds(start, 2 * shard), :] = jnp.concatenate([first, second], axis=0).astype(bfloat)
                return 0

            lax.fori_loop(0, width // (2 * shard), two_devices, 0)
        else:
            start = pl.multiple_of((step - 1 - chunks) * width, width)
            out_ref[...] = held[pl.ds(start, width), :].astype(bfloat)


def weight_grads(me, early, late, proj, normed, cot, upper, active, shard):
    length, width = proj.shape
    hidden = upper.shape[1]
    chunks = hidden // width
    groups = len(early)
    parts = [*early, *late]

    def whole(shape):
        return pl.BlockSpec(shape, lambda step, me_ref: (0, 0), pipeline_mode=pl.Buffered(1))

    by_chunk = pl.BlockSpec((length, width), lambda step, me_ref: (0, jnp.clip(step - 1, 0, chunks - 1)))
    return pl.pallas_call(
        functools.partial(weight_grad_kernel, groups, chunks, shard),
        grid_spec=pltpu.PrefetchScalarGridSpec(
            num_scalar_prefetch=1,
            grid=(1 + 2 * chunks,),
            in_specs=[whole(part.shape) for part in parts] + [whole(proj.shape)] * 3 + [by_chunk] * 2,
            out_specs=pl.BlockSpec((width, width), lambda step, me_ref: (0, step)),
            scratch_shapes=[pltpu.VMEM((hidden, width), single)],
        ),
        out_shape=in_hbm((width, width + 2 * hidden), bfloat),
        compiler_params=pltpu.CompilerParams(vmem_limit_bytes=48 << 20),
        cost_estimate=pl.CostEstimate(flops=20 << 30, transcendentals=0, bytes_accessed=32 << 20),
        name="weight_grads",
    )(me, *from_hbm([*parts, proj, normed, cot, upper, active]))


def project_back_kernel(count, passes, me_ref, *refs):
    pieces = refs[:count]
    pass_ref, gain_ref, shift_ref, weight_ref, grad_ref, stats_ref, last_sums_ref = refs[count : count + 7]
    *rows_refs, weight_grad_ref, sums_ref, held = refs[count + 7 :]
    slot = pl.program_id(0)
    step = pl.program_id(1)
    pass_index = me_ref[1 + slot]
    packed = grad_ref.shape[1]

    @pl.when((slot == 0) & (step == 0))
    def _():
        weight_grad_ref[...] = jnp.zeros(weight_grad_ref.shape, single)
        sums_ref[...] = jnp.zeros(sums_ref.shape, single)
        sums_ref[16:, :] = last_sums_ref[...]
        sums_ref[pl.ds(passes + me_ref[0], 1), :] = last_sums_ref[0:1, :]

    def column_sum(values):
        return jnp.sum(values, axis=0, keepdims=True)

    rows = pieces[0][...]
    for index in range(1, count):
        rows = jnp.where(slot == index, pieces[index][...], rows)
    stats = stats_ref[...]
    inverse = stats[:, 0:1]
    normed = (rows.astype(single) + pass_ref[pl.ds(pass_index, 1), :]) * inverse + stats[:, 1:2]
    low = (normed * gain_ref[...] + shift_ref[...]).astype(bfloat)
    grad = grad_ref[...]
    back = dot_nt(grad, weight_ref[...])
    weight_grad_ref[...] += dot_tn(low, grad)
    part = norm_back(back, gain_ref[...], normed, inverse)
    held[...] = part.astype(bfloat)
    sums_ref[pl.ds(me_ref[0], 1), :packed] += column_sum(grad.astype(single))
    sums_ref[pl.ds(passes + pass_index, 1), :] += column_sum(part)
    sums_ref[8:9, :] += column_sum(back * normed)
    sums_ref[9:10, :] += column_sum(back)
    for index in range(count):

        @pl.when(slot == index)
        def _():
            rows_refs[index][...] = held[...]


def project_back(order, pieces, pass_emb, gain, shift, weight, grads, stats, last_sums):
    count = len(pieces)
    length, width = pieces[0].shape
    passes, _, packed = grads.shape
    block = min(512, length)
    steps = length // block
    sums_shape = (16 + last_sums.shape[0], width)

    def piece_spec(index):
        def where(slot, step, order_ref):
            return (jnp.where(slot == index, step, jnp.where(slot < index, 0, steps - 1)), 0)

        return pl.BlockSpec((block, width), where)

    def whole(shape):
        return pl.BlockSpec(shape, lambda slot, step, order_ref: (0,) * len(shape))

    def by_pass(size):
        return pl.BlockSpec(
            (pl.Squeezed(), block, size), lambda slot, step, order_ref: (order_ref[1 + slot], step, 0)
        )

    small = [pass_emb, gain, shift]
    return pl.pallas_call(
        functools.partial(project_back_kernel, count, passes),
        grid_spec=pltpu.PrefetchScalarGridSpec(
            num_scalar_prefetch=1,
            grid=(count, steps),
            in_specs=[piece_spec(index) for index in range(count)]
            + [whole(operand.shape) for operand in small]
            + [whole(weight.shape), by_pass(packed), by_pass(2), whole(last_sums.shape)],
            out_specs=[piece_spec(index) for index in range(count)]
            + [whole((width, packed)), whole(sums_shape)],
            scratch_shapes=[pltpu.VMEM((block, width), bfloat)],
        ),
        out_shape=[in_hbm((length, width), bfloat)] * count
        + [jax.ShapeDtypeStruct((width, packed), single), jax.ShapeDtypeStruct(sums_shape, single)],
        compiler_params=pltpu.CompilerParams(vmem_limit_bytes=48 << 20),
        cost_estimate=pl.CostEstimate(flops=16 << 30, transcendentals=0, bytes_accessed=20 << 20),
        name="project_back",
    )(order, *from_hbm(pieces), *small, *from_hbm([weight, grads, stats]), last_sums)


def exchange(value, axis, distance):
    return lax.ppermute(value, axis, [(k, k ^ distance) for k in range(lax.axis_size(axis))])


def sum_everywhere(value):
    for axis in ("seq", "pass"):
        distance = 1
        while distance < lax.axis_size(axis):
            value = value + exchange(value, axis, distance)
            distance *= 2
    return value


def per_device(
    x_rows,
    pass_depth,
    cotangent,
    pass_emb,
    ln1_gain,
    ln1_bias,
    w_qkv,
    q_bias,
    v_bias,
    w_out,
    out_bias,
    ln2_gain,
    ln2_bias,
    w_up,
    up_bias,
    w_down,
    down_bias,
):
    everyone = ("seq", "pass")
    _, length, width = x_rows.shape
    hidden = w_up.shape[1]
    passes = lax.axis_size("pass")
    devices = passes * lax.axis_size("seq")
    shard = w_qkv.shape[0]
    group = width // passes
    group_heads = group // HEAD_DIM
    me = lax.axis_index("pass")
    order = jnp.concatenate([me[None], jnp.bitwise_xor(me, jnp.arange(passes))]).astype(jnp.int32)

    def swap(value, distance):
        return exchange(value, "pass", distance)

    x_own = x_rows[0]

    by_group = w_qkv.reshape(shard, 3, passes, group).transpose(2, 0, 1, 3).reshape(passes, shard, 3 * group)
    by_rows = lax.all_to_all(by_group, "pass", 0, 0, tiled=True).reshape(passes * shard, 3 * group)
    by_rows, x_ready = lax.optimization_barrier((by_rows, x_own))
    x_one = swap(x_ready, 1)
    x_two = swap(x_ready, 2)
    w_heads = lax.all_gather(by_rows, "seq", axis=0, tiled=True)

    down_cols = w_down.reshape(passes, shard, width).transpose(1, 0, 2).reshape(shard, hidden)
    gathered = lax.all_gather(
        jnp.concatenate([w_out, w_up, down_cols], axis=1), everyone, axis=0, tiled=True
    )
    in_place = shard % 8 == 0
    full_down = None
    if not in_place:
        full_down = (
            gathered[:, width + hidden :]
            .reshape(devices, shard, hidden // width, width)
            .transpose(0, 2, 1, 3)
            .reshape(hidden, width)
        )

    gain_one, shift_one = ln1_gain[None], ln1_bias[None]
    own_q_bias = lax.dynamic_slice_in_dim(q_bias, me * group, group)
    own_v_bias = lax.dynamic_slice_in_dim(v_bias, me * group, group)
    bias_row = jnp.concatenate([own_q_bias, jnp.zeros((group,), single), own_v_bias])[None]
    pad = (-3 * group) % LANES
    w_wide = jnp.pad(w_heads, ((0, 0), (0, pad)))
    bias_wide = jnp.pad(bias_row, ((0, 0), (0, pad)))
    depth = pass_depth.reshape(length, 1)
    near = project(
        order[:3], (x_own, x_one), passes, pass_emb, gain_one, shift_one, w_wide, bias_wide, depth, None
    )
    x_two, near = lax.optimization_barrier((x_two, near))
    x_three = swap(x_two, 1)
    far_order = jnp.concatenate([order[:1], order[3:]])
    queries, keys, values, stats = project(
        far_order, (x_two, x_three), passes, pass_emb, gain_one, shift_one, w_wide, bias_wide, depth, near
    )

    def trade(pieces):
        return list(pieces[:1]) + [swap(pieces[slot], slot) for slot in range(1, passes)]

    pass_row = lax.dynamic_index_in_dim(pass_emb, me, 0, keepdims=True)
    outs, logged = [None, None], [None, None]
    for half in (1, 0):
        outs[half], logged[half] = attend(order[:1], queries, keys, values, half)
    parts = [trade(outs[half]) for half in range(2)]
    results = None
    head_grads = [None, None]
    for half in (1, 0):
        results, head_grads[half], full_down = middle(
            order[:1],
            parts[half],
            x_own,
            cotangent[0],
            pass_row,
            out_bias[None],
            ln2_gain[None],
            ln2_bias[None],
            up_bias[None],
            down_bias[None],
            gathered,
            full_down,
            shard,
            half,
            results,
        )
        head_grads[half] = trade(head_grads[half])
    out_rows, mixed_grad, normed_two, activated, upper_low, proj_low, sums = results

    weight_parts = weight_grads(
        order[:1],
        *parts,
        proj_low,
        normed_two,
        cotangent[0],
        upper_low,
        activated,
        shard if in_place else None,
    )
    if not in_place:
        down_part = (
            weight_parts[:, width + hidden :]
            .reshape(width, hidden // width, width)
            .transpose(1, 0, 2)
            .reshape(devices, hidden // width, shard, width)
            .transpose(0, 2, 1, 3)
            .reshape(width, hidden)
        )
        weight_parts = jnp.concatenate([weight_parts[:, : width + hidden], down_part], axis=1)
    weight_parts, logged, head_grads = lax.optimization_barrier((weight_parts, logged, head_grads))
    reduced = lax.psum_scatter(weight_parts, everyone, scatter_dimension=0, tiled=True).astype(single)
    shard_out = reduced[:, :width]
    shard_up = reduced[:, width : width + hidden]
    shard_down = (
        reduced[:, width + hidden :]
        .reshape(shard, hidden // width, width)
        .transpose(1, 0, 2)
        .reshape(w_down.shape)
    )

    qkv_low = attend_back(order[:1], logged, keys, values, outs, head_grads)
    near_own, near_one, far_two, far_three, head_weight, sums = project_back(
        order, (x_own, x_one, x_two, x_three), pass_emb, gain_one, shift_one, w_heads, qkv_low, stats, sums
    )

    near_one, far_three = swap(near_one, 1), swap(far_three, 1)
    far_sum = (far_two.astype(single) + far_three.astype(single)).astype(bfloat)
    far_sum = swap(far_sum, 2)
    x_grad = mixed_grad + near_own.astype(single) + near_one.astype(single) + far_sum.astype(single)

    pieces = head_weight.astype(bfloat).reshape(devices, shard, 3 * group)
    pieces = lax.all_to_all(pieces, everyone, 0, 0, tiled=True)
    pieces = pieces.reshape(devices // passes, passes, shard, 3, group).astype(single).sum(axis=0)
    shard_qkv = pieces.transpose(1, 2, 0, 3).reshape(w_qkv.shape)

    totals = sum_everywhere(sums)
    biases = totals[:passes, : 3 * group].reshape(passes, 3, group)
    pass_grad = lax.dynamic_slice_in_dim(totals, passes + me, 1, 0)
    up_rows = hidden // width
    return (
        out_rows[None],
        x_grad[None],
        shard_qkv,
        biases[:, 0].reshape(-1),
        biases[:, 2].reshape(-1),
        shard_out,
        totals[16],
        totals[8],
        totals[9],
        totals[17],
        totals[18],
        shard_up,
        totals[20 : 20 + up_rows].reshape(-1),
        shard_down,
        totals[19],
        pass_grad,
    )


def solution(mesh):
    placed = (
        P("pass", "seq", None),
        P("seq", None),
        P("pass", "seq", None),
        P(),
        P(),
        P(),
        P(("seq", "pass"), None),
        P(),
        P(),
        P(("seq", "pass"), None),
        P(),
        P(),
        P(),
        P(("seq", "pass"), None),
        P(),
        P(("seq", "pass"), None),
        P(),
    )
    return jax.shard_map(
        per_device,
        mesh=mesh,
        in_specs=placed,
        out_specs=(
            P("pass", "seq", None),
            P("pass", "seq", None),
            P(("seq", "pass"), None),
            P(),
            P(),
            P(("seq", "pass"), None),
            P(),
            P(),
            P(),
            P(),
            P(),
            P(("seq", "pass"), None),
            P(),
            P(("seq", "pass"), None),
            P(),
            P("pass", None),
        ),
        check_vma=False,
    )
```

```python
import functools

import jax
import jax.numpy as jnp
from jax import lax
from jax.experimental import pallas as pl
from jax.experimental.pallas import tpu as pltpu
from jax.sharding import PartitionSpec as P

HEADS = 12
HEAD_DIM = 64
LANES = 128
NORM_EPS = 1e-05
MASKED = -1e30
BIAS_COL = 64
STAT_COL = 65
DELTA_COL = 64

bfloat = jnp.bfloat16
single = jnp.float32


def in_hbm(shape, dtype):
    return pltpu.HBM(shape, dtype)


def from_hbm(values):
    return [pltpu.with_memory_space_constraint(value, pltpu.HBM) for value in values]


def dot_nn(a, b):
    return jnp.dot(a, b, preferred_element_type=single)


def dot_nt(a, b):
    return lax.dot_general(a, b, (((1,), (1,)), ((), ())), preferred_element_type=single)


def dot_tn(a, b):
    return lax.dot_general(a, b, (((0,), (0,)), ((), ())), preferred_element_type=single)


def three_parts(value):
    first = value.astype(bfloat).astype(single)
    rest = value - first
    second = rest.astype(bfloat).astype(single)
    return first, second, rest - second


def with_columns(base, start, columns):
    lane = lax.broadcasted_iota(jnp.int32, base.shape, 1)
    for offset, column in enumerate(columns):
        base = jnp.where(lane == start + offset, column, base)
    return base


def norm_parts(values):
    center = values - jnp.mean(values, axis=-1, keepdims=True)
    inverse = lax.rsqrt(jnp.mean(center * center, axis=-1, keepdims=True) + NORM_EPS)
    return center * inverse, inverse


def norm_back(grad, gain, normed, inverse):
    scaled = grad * gain
    mean_one = jnp.mean(scaled, axis=-1, keepdims=True)
    mean_two = jnp.mean(scaled * normed, axis=-1, keepdims=True)
    return inverse * (scaled - mean_one - normed * mean_two)


def head_slab(packed, index):
    low = (index // 2) * LANES
    slab = packed[:, low : low + LANES]
    if index % 2:
        slab = pltpu.roll(slab, HEAD_DIM, axis=1)
    return slab


def pack_heads(slabs):
    packed = []
    lane = lax.broadcasted_iota(jnp.int32, slabs[0].shape, 1)
    for index in range(0, len(slabs), 2):
        if index + 1 < len(slabs):
            other = pltpu.roll(slabs[index + 1], HEAD_DIM, axis=1)
            packed.append(jnp.where(lane < HEAD_DIM, slabs[index], other))
        else:
            packed.append(slabs[index])
    width = len(slabs) * HEAD_DIM
    return jnp.concatenate(packed, axis=1)[:, :width]


def project_kernel(heads, count, me_ref, *refs):
    pieces = refs[:count]
    pass_ref, gain_ref, shift_ref, weight_ref, bias_ref, depth_ref = refs[count : count + 6]
    q_ref, k_ref, v_ref, stats_ref = refs[-4:]
    slot = pl.program_id(0)
    pass_index = me_ref[1 + slot]
    pass_row = pass_ref[pl.ds(pass_index, 1), :]
    rows = pieces[0][...]
    for index in range(1, count):
        rows = jnp.where(slot == index, pieces[index][...], rows)
    rows = rows.astype(single) + pass_row
    mean = jnp.mean(rows, axis=-1, keepdims=True)
    center = rows - mean
    inverse = lax.rsqrt(jnp.mean(center * center, axis=-1, keepdims=True) + NORM_EPS)
    lane = lax.broadcasted_iota(jnp.int32, stats_ref.shape, 1)
    stats_ref[...] = jnp.where(lane == 0, inverse, -mean * inverse)
    low = (center * inverse * gain_ref[...] + shift_ref[...]).astype(bfloat)
    projected = dot_nn(low, weight_ref[...]) + bias_ref[...]
    lane = lax.broadcasted_iota(jnp.int32, (low.shape[0], LANES), 1)
    inside = lane < HEAD_DIM
    depth_bias = jnp.where(pass_index < depth_ref[...], 0.0, MASKED)
    q_rest = jnp.where(lane == BIAS_COL, 1.0, 0.0)
    k_rest = jnp.where(
        lane == BIAS_COL, depth_bias, jnp.where((lane >= STAT_COL) & (lane < STAT_COL + 3), 1.0, 0.0)
    )
    v_rest = jnp.where((lane >= DELTA_COL) & (lane < DELTA_COL + 3), 1.0, 0.0)
    for head in range(heads):
        q_part = head_slab(projected, head).astype(bfloat).astype(single) * (HEAD_DIM**-0.5)
        q_ref[head] = jnp.where(inside, q_part, q_rest).astype(bfloat)
        k_ref[head] = jnp.where(inside, head_slab(projected, heads + head), k_rest).astype(bfloat)
        v_ref[head] = jnp.where(inside, head_slab(projected, 2 * heads + head), v_rest).astype(bfloat)


def project(order, pieces, passes, pass_emb, gain, shift, weight, bias, depth, previous):
    count = len(pieces)
    length, width = pieces[0].shape
    heads = weight.shape[1] // (3 * HEAD_DIM)
    block = min(512, length)
    steps = length // block

    def piece_spec(index):
        def where(slot, step, order_ref):
            return (jnp.where(slot == index, step, jnp.where(slot < index, 0, steps - 1)), 0)

        return pl.BlockSpec((block, width), where)

    def whole(shape):
        return pl.BlockSpec(shape, lambda slot, step, order_ref: (0,) * len(shape))

    out_spec = pl.BlockSpec(
        (heads, pl.Squeezed(), block, LANES),
        lambda slot, step, order_ref: (0, order_ref[1 + slot], step, 0),
    )
    shape = in_hbm((heads, passes, length, LANES), bfloat)
    stats_spec = pl.BlockSpec(
        (pl.Squeezed(), block, 2), lambda slot, step, order_ref: (order_ref[1 + slot], step, 0)
    )
    in_specs = [piece_spec(index) for index in range(count)] + [
        whole(pass_emb.shape),
        whole(gain.shape),
        whole(shift.shape),
        whole(weight.shape),
        whole(bias.shape),
        pl.BlockSpec((block, 1), lambda slot, step, order_ref: (step, 0)),
    ]
    operands = [*pieces, pass_emb, gain, shift, weight, bias, depth]
    aliases = {}
    if previous is not None:
        aliases = {1 + len(operands) + index: index for index in range(4)}
        in_specs += [pl.BlockSpec(memory_space=pl.ANY)] * 4
        operands += list(previous)
    return pl.pallas_call(
        functools.partial(project_kernel, heads, count),
        grid_spec=pltpu.PrefetchScalarGridSpec(
            num_scalar_prefetch=1,
            grid=(count, steps),
            in_specs=in_specs,
            out_specs=[out_spec] * 3 + [stats_spec],
        ),
        out_shape=[shape] * 3 + [in_hbm((passes, length, 2), single)],
        input_output_aliases=aliases,
        compiler_params=pltpu.CompilerParams(vmem_limit_bytes=40 << 20),
        cost_estimate=pl.CostEstimate(flops=8 << 30, transcendentals=0, bytes_accessed=12 << 20),
        name="project",
    )(order, *operands)


def attend_kernel(passes, block, first, last, me_ref, q_ref, k_ref, v_ref, *refs):
    out_refs, q_next_ref, held = refs[:passes], refs[passes], refs[passes + 1]
    heads = q_ref.shape[0]
    step = pl.program_id(0)
    row = lax.broadcasted_iota(jnp.int32, (block, block), 0)
    col = lax.broadcasted_iota(jnp.int32, (block, block), 1)
    causal = col <= row

    def one_head(head, count):
        kept = [[] for _ in range(passes)]
        highest = [None] * passes
        for key_pass in range(passes):
            span = passes - key_pass
            query = q_ref[head, key_pass:passes].reshape(span * block, LANES)
            for tile in range(count):
                both = dot_nt(query, k_ref[head, key_pass, tile * block : (tile + 1) * block, :])
                for query_pass in range(key_pass, passes):
                    start = (query_pass - key_pass) * block
                    scores = both[start : start + block]
                    if tile == count - 1:
                        scores = jnp.where(causal, scores, MASKED)
                    kept[query_pass].append(scores)
                    for lane in range(0, block, LANES):
                        part = scores[:, lane : lane + LANES]
                        old = highest[query_pass]
                        highest[query_pass] = part if old is None else jnp.maximum(old, part)
        highest = [jnp.max(part, axis=-1, keepdims=True) for part in highest]
        for query_pass in range(passes):
            total = None
            for index, scores in enumerate(kept[query_pass]):
                key_pass, tile = divmod(index, count)
                weights = jnp.exp(scores - highest[query_pass]).astype(bfloat)
                term = dot_nn(weights, v_ref[head, key_pass, tile * block : (tile + 1) * block, :])
                total = term if total is None else total + term
            row_sum = total[:, DELTA_COL : DELTA_COL + 1]
            log_sum = highest[query_pass] + jnp.log(row_sum)
            q_next_ref[head, query_pass] = with_columns(
                q_ref[head, query_pass].astype(single), STAT_COL, three_parts(-log_sum)
            ).astype(bfloat)
            held[head, query_pass] = total * (1.0 / row_sum)

    for index in range(first, last):

        @pl.when(step == index - first)
        def _():
            lax.fori_loop(0, heads, lambda head, _: (one_head(head, index + 1), 0)[1], 0)

    for slot in range(passes):
        query_pass = jnp.bitwise_xor(me_ref[0], slot)
        out_refs[slot][...] = pack_heads([held[head, query_pass] for head in range(heads)]).astype(bfloat)


def attend(me, queries, keys, values, half):
    heads, passes, length, _ = queries.shape
    block = min(256, length // 2)
    count = length // 2 // block
    first, last = half * count, (half + 1) * count
    seen = pl.BlockSpec(
        (heads, passes, last * block, LANES),
        lambda step, me_ref: (0, 0, 0, 0),
        pipeline_mode=pl.Buffered(1),
    )
    part = pl.BlockSpec((heads, passes, block, LANES), lambda step, me_ref: (0, 0, first + step, 0))
    part_out = pl.BlockSpec((heads, passes, block, LANES), lambda step, me_ref: (0, 0, step, 0))
    packed = heads * HEAD_DIM
    *outs, queries = pl.pallas_call(
        functools.partial(attend_kernel, passes, block, first, last),
        grid_spec=pltpu.PrefetchScalarGridSpec(
            num_scalar_prefetch=1,
            grid=(count,),
            in_specs=[part, seen, seen],
            out_specs=[pl.BlockSpec((block, packed), lambda step, me_ref: (step, 0))] * passes + [part_out],
            scratch_shapes=[pltpu.VMEM((heads, passes, block, LANES), single)],
        ),
        out_shape=[in_hbm((length // 2, packed), bfloat)] * passes
        + [in_hbm((heads, passes, length // 2, LANES), bfloat)],
        compiler_params=pltpu.CompilerParams(vmem_limit_bytes=48 << 20),
        cost_estimate=pl.CostEstimate(
            flops=(10 + 20 * half) << 30,
            transcendentals=heads * (1 + 2 * half) * length * length,
            bytes_accessed=12 << 20,
        ),
        name="attend",
    )(me, *from_hbm((queries, keys, values)))
    return outs, queries


def attend_back_kernel(passes, block, me_ref, *refs):
    q_refs, (k_ref, v_ref), refs = refs[:2], refs[2:4], refs[4:]
    out_refs = refs[:passes], refs[passes : 2 * passes]
    grad_refs = refs[2 * passes : 3 * passes], refs[3 * passes : 4 * passes]
    all_ref, key_acc, value_acc, grad_held, query_held = refs[4 * passes :]
    heads = k_ref.shape[0]
    blocks = k_ref.shape[2] // block
    step = pl.program_id(0)
    me = me_ref[0]
    row = lax.broadcasted_iota(jnp.int32, (block, block), 0)
    col = lax.broadcasted_iota(jnp.int32, (block, block), 1)
    causal = row <= col
    inside = lax.broadcasted_iota(jnp.int32, (block, LANES), 1) < HEAD_DIM
    padded = ((heads * HEAD_DIM + LANES - 1) // LANES) * LANES

    @pl.when(step == 0)
    def _():
        key_acc[...] = jnp.zeros(key_acc.shape, single)
        value_acc[...] = jnp.zeros(value_acc.shape, single)

    def prepare(half):
        for slot in range(passes):
            query_pass = jnp.bitwise_xor(me, slot)
            grad = grad_refs[half][slot][...].astype(single)
            out = out_refs[half][slot][...].astype(single)
            if padded > heads * HEAD_DIM:
                tail = jnp.zeros((block, padded - heads * HEAD_DIM), single)
                grad = jnp.concatenate([grad, tail], axis=1)
                out = jnp.concatenate([out, tail], axis=1)
            product = grad * out
            for head in range(heads):
                delta = jnp.sum(
                    jnp.where(inside, head_slab(product, head), 0.0), axis=-1, keepdims=True
                )
                base = jnp.where(inside, head_slab(grad, head), 0.0)
                grad_held[head, query_pass] = with_columns(base, DELTA_COL, three_parts(-delta)).astype(bfloat)

    def one_head(head, count, q_ref):
        query_sums = [None] * passes
        for key_pass in range(passes):
            span = passes - key_pass
            query = q_ref[head, key_pass:passes].reshape(span * block, LANES)
            grad = grad_held[head, key_pass:passes].reshape(span * block, LANES)
            for tile in range(count):
                window = slice(tile * block, (tile + 1) * block)
                key = k_ref[head, key_pass, window, :]
                value = v_ref[head, key_pass, window, :]
                prob = jnp.exp(dot_nt(key, query))
                if tile == count - 1:
                    prob = jnp.where(jnp.concatenate([causal] * span, axis=1), prob, 0.0)
                value_acc[head, key_pass, window, :] += dot_nn(prob.astype(bfloat), grad)
                score_grad = (prob * dot_nt(value, grad)).astype(bfloat)
                key_acc[head, key_pass, window, :] += dot_nn(score_grad, query)
                term = dot_tn(key, score_grad)
                for query_pass in range(key_pass, passes):
                    start = (query_pass - key_pass) * block
                    part = term[:, start : start + block]
                    old = query_sums[query_pass]
                    query_sums[query_pass] = part if old is None else old + part
        for query_pass in range(passes):
            query_held[head, query_pass] = query_sums[query_pass].T * (HEAD_DIM**-0.5)

    for index in range(blocks):

        @pl.when(step == blocks - 1 - index)
        def _():
            half = index // (blocks // 2)
            prepare(half)
            lax.fori_loop(0, heads, lambda head, _: (one_head(head, index + 1, q_refs[half]), 0)[1], 0)
            window = slice(index * block, (index + 1) * block)
            for query_pass in range(passes):
                slabs = [query_held[head, query_pass] for head in range(heads)]
                slabs += [key_acc[head, query_pass, window, :] for head in range(heads)]
                slabs += [value_acc[head, query_pass, window, :] for head in range(heads)]
                all_ref[query_pass] = pack_heads(slabs).astype(bfloat)


def attend_back(me, queries, keys, values, outs, grads):
    heads, passes, length, _ = keys.shape
    block = min(256, length // 2)
    count = length // 2 // block
    packed = heads * HEAD_DIM

    def spot(half):
        return lambda step: jnp.clip(2 * count - 1 - step - half * count, 0, count - 1)

    def query_spec(half):
        return pl.BlockSpec((heads, passes, block, LANES), lambda step, me_ref: (0, 0, spot(half)(step), 0))

    def rows_spec(half):
        return pl.BlockSpec((block, packed), lambda step, me_ref: (spot(half)(step), 0))

    whole = pl.BlockSpec(keys.shape, lambda step, me_ref: (0, 0, 0, 0), pipeline_mode=pl.Buffered(1))
    rows_specs = [rows_spec(half) for half in range(2) for _ in range(passes)]
    return pl.pallas_call(
        functools.partial(attend_back_kernel, passes, block),
        grid_spec=pltpu.PrefetchScalarGridSpec(
            num_scalar_prefetch=1,
            grid=(2 * count,),
            in_specs=[query_spec(0), query_spec(1), whole, whole] + rows_specs * 2,
            out_specs=pl.BlockSpec(
                (passes, block, 3 * packed), lambda step, me_ref: (0, 2 * count - 1 - step, 0)
            ),
            scratch_shapes=[
                pltpu.VMEM(keys.shape, single),
                pltpu.VMEM(keys.shape, single),
                pltpu.VMEM((heads, passes, block, LANES), bfloat),
                pltpu.VMEM((heads, passes, block, LANES), single),
            ],
        ),
        out_shape=in_hbm((passes, length, 3 * packed), bfloat),
        compiler_params=pltpu.CompilerParams(vmem_limit_bytes=58 << 20),
        cost_estimate=pl.CostEstimate(
            flops=300 << 30, transcendentals=heads * 6 * length * length, bytes_accessed=20 << 20
        ),
        name="attend_back",
    )(me, *from_hbm((*queries, keys, values, *outs[0], *outs[1], *grads[0], *grads[1])))


def middle_kernel(groups, downs, shard, begins, me_ref, *refs):
    parts = refs[:groups]
    x_ref, cot_ref, pass_ref, out_bias_ref, gain_ref, shift_ref, down_bias_ref, up_bias_ref, w_out_ref, w_up_ref = refs[
        groups : groups + 10
    ]
    refs = refs[groups + 10 :]
    down_refs = refs[:downs]
    last_sums_ref = None if begins else refs[downs]
    outs, scratch = refs[-12 - groups : -5 - groups], refs[-5:]
    rows_ref, mixed_grad_ref, normed_ref, active_ref, upper_ref, proj_ref, sums_ref = outs
    grads = refs[-5 - groups : -5]
    normed_held, inverse_held, total_held, back_held, w_down_held = scratch
    me = me_ref[0]
    width = x_ref.shape[1]
    packed = width // groups
    step = pl.program_id(0)

    def group_window(slot):
        start = pl.multiple_of(jnp.bitwise_xor(me, slot) * packed, packed)
        return pl.ds(start, packed)

    def column_sum(values):
        return jnp.sum(values, axis=0, keepdims=True)

    @pl.when(step == 0)
    def _():
        sums_ref[...] = jnp.zeros(sums_ref.shape, single) if begins else last_sums_ref[...]
        mixed = x_ref[...].astype(single) + pass_ref[...] + out_bias_ref[...]
        for slot in range(groups):
            mixed += dot_nn(parts[slot][...], w_out_ref[group_window(slot), :])
        normed, inverse = norm_parts(mixed)
        normed_ref[...] = (normed * gain_ref[...] + shift_ref[...]).astype(bfloat)
        normed_held[...] = normed
        inverse_held[...] = jnp.broadcast_to(inverse, inverse_held.shape)
        total_held[...] = mixed + down_bias_ref[...]
        back_held[...] = jnp.zeros(back_held.shape, single)

    if shard:
        for start in range(0, down_refs[0].shape[0], 2 * shard):
            blocks = [ref[start : start + 2 * shard, :].astype(single) for ref in down_refs]
            pieces = [block[side * shard : (side + 1) * shard] for side in range(2) for block in blocks]
            w_down_held[start * downs : (start + 2 * shard) * downs, :] = jnp.concatenate(
                pieces, axis=0
            ).astype(bfloat)
        w_down_ref = w_down_held
    else:
        w_down_ref = down_refs[0]

    upper = dot_nn(normed_ref[...], w_up_ref[...]) + up_bias_ref[...]
    below = 0.5 + 0.5 * lax.erf(upper * (0.5**0.5))
    density = jnp.exp(-0.5 * upper * upper) * 0.3989422804014327
    active = (upper * below).astype(bfloat)
    active_ref[...] = active
    total_held[...] += dot_nn(active, w_down_ref[...])
    upper_low = (dot_nt(cot_ref[...], w_down_ref[...]) * (below + upper * density)).astype(bfloat)
    upper_ref[...] = upper_low
    sums_ref[pl.ds(4 + step, 1), :] += column_sum(upper_low.astype(single))
    back_held[...] += dot_nt(upper_low, w_up_ref[...])

    @pl.when(step == pl.num_programs(0) - 1)
    def _():
        rows_ref[...] = total_held[...].astype(bfloat)
        out_grad = cot_ref[...].astype(single)
        normed, back = normed_held[...], back_held[...]
        mixed_grad = out_grad + norm_back(back, gain_ref[...], normed, inverse_held[:, 0:1])
        mixed_grad_ref[...] = mixed_grad
        proj_low = mixed_grad.astype(bfloat)
        proj_ref[...] = proj_low
        for slot in range(groups):
            grads[slot][...] = dot_nt(proj_low, w_out_ref[group_window(slot), :]).astype(bfloat)
        sums_ref[0:1, :] += column_sum(mixed_grad)
        sums_ref[1:2, :] += column_sum(back * normed)
        sums_ref[2:3, :] += column_sum(back)
        sums_ref[3:4, :] += column_sum(out_grad)


def middle(
    me,
    parts,
    x_own,
    cot,
    pass_row,
    out_bias,
    gain,
    shift,
    up_bias,
    down_bias,
    gathered,
    w_down,
    shard,
    half,
    previous,
):
    length, width = x_own.shape
    hidden = up_bias.shape[1]
    chunks = hidden // width
    groups = len(parts)
    packed = width // groups
    block = length // 2

    def rows(size):
        return pl.BlockSpec((block, size), lambda step, me_ref: (half, 0))

    def half_rows(size):
        return pl.BlockSpec((block, size), lambda step, me_ref: (0, 0))

    def whole(shape):
        return pl.BlockSpec(shape, lambda step, me_ref: (0, 0), pipeline_mode=pl.Buffered(1))

    def fixed(shape):
        return pl.BlockSpec(shape, lambda step, me_ref: (0, 0))

    by_chunk = pl.BlockSpec((block, width), lambda step, me_ref: (half, step))
    sums_shape = ((4 + chunks + 7) // 8 * 8, width)
    square = (width, width)
    small = (pass_row, out_bias, gain, shift, down_bias)
    if w_down is None:
        downs = chunks

        def down_spec(col):
            return pl.BlockSpec((width // chunks, width), lambda step, me_ref: (step, 1 + chunks + col))

        down_specs = [down_spec(col) for col in range(chunks)]
        down = [gathered] * chunks
    else:
        downs = 1
        down_specs = [pl.BlockSpec(square, lambda step, me_ref: (step, 0))]
        down = [w_down]
        shard = None
    in_specs = (
        [half_rows(packed)] * groups
        + [rows(width), rows(width)]
        + [whole(operand.shape) for operand in small]
        + [pl.BlockSpec((1, width), lambda step, me_ref: (0, step))]
        + [whole(square), pl.BlockSpec(square, lambda step, me_ref: (0, 1 + step))]
        + down_specs
    )
    operands = [*from_hbm([*parts, x_own, cot]), *small, up_bias, *from_hbm([gathered] * 2 + down)]
    aliases = {}
    if previous is not None:
        in_specs += [fixed(sums_shape)] + [pl.BlockSpec(memory_space=pl.ANY)] * 6
        aliases = {2 + len(operands) + index: index for index in range(6)}
        operands += [previous[6], *previous[:6]]
    results = pl.pallas_call(
        functools.partial(middle_kernel, groups, downs, shard, previous is None),
        grid_spec=pltpu.PrefetchScalarGridSpec(
            num_scalar_prefetch=1,
            grid=(chunks,),
            in_specs=in_specs,
            out_specs=[rows(width), rows(width), rows(width), by_chunk, by_chunk, rows(width), fixed(sums_shape)]
            + [half_rows(packed)] * groups,
            scratch_shapes=[
                pltpu.VMEM((block, width), single),
                pltpu.VMEM((block, LANES), single),
                pltpu.VMEM((block, width), single),
                pltpu.VMEM((block, width), single),
                pltpu.VMEM(square, bfloat),
            ],
        ),
        out_shape=[
            in_hbm((length, width), bfloat),
            in_hbm((length, width), single),
            in_hbm((length, width), bfloat),
            in_hbm((length, hidden), bfloat),
            in_hbm((length, hidden), bfloat),
            in_hbm((length, width), bfloat),
            jax.ShapeDtypeStruct(sums_shape, single),
        ]
        + [in_hbm((length // 2, packed), bfloat)] * groups,
        input_output_aliases=aliases,
        compiler_params=pltpu.CompilerParams(vmem_limit_bytes=56 << 20),
        cost_estimate=pl.CostEstimate(
            flops=20 << 30, transcendentals=length * hidden, bytes_accessed=24 << 20
        ),
        name="middle",
    )(me, *operands)
    return results[:7], results[7:]


def weight_grad_kernel(groups, chunks, shard, me_ref, *refs):
    early, late = refs[:groups], refs[groups : 2 * groups]
    proj_ref, normed_ref, cot_ref, upper_ref, active_ref, out_ref, held = refs[2 * groups :]
    middle_row = proj_ref.shape[0] // 2
    step = pl.program_id(0)
    width = proj_ref.shape[1]
    packed = width // groups

    @pl.when(step == 0)
    def _():
        for slot in range(groups):
            start = pl.multiple_of(jnp.bitwise_xor(me_ref[0], slot) * packed, packed)
            out_ref[pl.ds(start, packed), :] = (
                dot_tn(early[slot][...], proj_ref[:middle_row, :])
                + dot_tn(late[slot][...], proj_ref[middle_row:, :])
            ).astype(bfloat)

    @pl.when((step >= 1) & (step <= chunks))
    def _():
        out_ref[...] = dot_tn(normed_ref[...], upper_ref[...]).astype(bfloat)
        start = pl.multiple_of((step - 1) * width, width)
        held[pl.ds(start, width), :] = dot_tn(active_ref[...], cot_ref[...])

    @pl.when(step > chunks)
    def _():
        if shard:
            def two_devices(index, _):
                start = pl.multiple_of((index * 2 * chunks + step - 1 - chunks) * shard, 8)
                first = held[pl.ds(start, shard), :]
                second = held[pl.ds(pl.multiple_of(start + chunks * shard, 8), shard), :]
                start = pl.multiple_of(index * 2 * shard, 2 * shard)
                out_ref[pl.ds(start, 2 * shard), :] = jnp.concatenate([first, second], axis=0).astype(bfloat)
                return 0

            lax.fori_loop(0, width // (2 * shard), two_devices, 0)
        else:
            start = pl.multiple_of((step - 1 - chunks) * width, width)
            out_ref[...] = held[pl.ds(start, width), :].astype(bfloat)


def weight_grads(me, early, late, proj, normed, cot, upper, active, shard):
    length, width = proj.shape
    hidden = upper.shape[1]
    chunks = hidden // width
    groups = len(early)
    parts = [*early, *late]

    def whole(shape):
        return pl.BlockSpec(shape, lambda step, me_ref: (0, 0), pipeline_mode=pl.Buffered(1))

    by_chunk = pl.BlockSpec((length, width), lambda step, me_ref: (0, jnp.clip(step - 1, 0, chunks - 1)))
    return pl.pallas_call(
        functools.partial(weight_grad_kernel, groups, chunks, shard),
        grid_spec=pltpu.PrefetchScalarGridSpec(
            num_scalar_prefetch=1,
            grid=(1 + 2 * chunks,),
            in_specs=[whole(part.shape) for part in parts] + [whole(proj.shape)] * 3 + [by_chunk] * 2,
            out_specs=pl.BlockSpec((width, width), lambda step, me_ref: (0, step)),
            scratch_shapes=[pltpu.VMEM((hidden, width), single)],
        ),
        out_shape=in_hbm((width, width + 2 * hidden), bfloat),
        compiler_params=pltpu.CompilerParams(vmem_limit_bytes=48 << 20),
        cost_estimate=pl.CostEstimate(flops=20 << 30, transcendentals=0, bytes_accessed=32 << 20),
        name="weight_grads",
    )(me, *from_hbm([*parts, proj, normed, cot, upper, active]))


def project_back_kernel(count, passes, me_ref, *refs):
    pieces = refs[:count]
    pass_ref, gain_ref, shift_ref, weight_ref, grad_ref, stats_ref, last_sums_ref = refs[count : count + 7]
    *rows_refs, weight_grad_ref, sums_ref, held = refs[count + 7 :]
    slot = pl.program_id(0)
    step = pl.program_id(1)
    pass_index = me_ref[1 + slot]
    packed = grad_ref.shape[1]

    @pl.when((slot == 0) & (step == 0))
    def _():
        weight_grad_ref[...] = jnp.zeros(weight_grad_ref.shape, single)
        sums_ref[...] = jnp.zeros(sums_ref.shape, single)
        sums_ref[16:, :] = last_sums_ref[...]
        sums_ref[pl.ds(passes + me_ref[0], 1), :] = last_sums_ref[0:1, :]

    def column_sum(values):
        return jnp.sum(values, axis=0, keepdims=True)

    rows = pieces[0][...]
    for index in range(1, count):
        rows = jnp.where(slot == index, pieces[index][...], rows)
    stats = stats_ref[...]
    inverse = stats[:, 0:1]
    normed = (rows.astype(single) + pass_ref[pl.ds(pass_index, 1), :]) * inverse + stats[:, 1:2]
    low = (normed * gain_ref[...] + shift_ref[...]).astype(bfloat)
    grad = grad_ref[...]
    back = dot_nt(grad, weight_ref[...])
    weight_grad_ref[...] += dot_tn(low, grad)
    part = norm_back(back, gain_ref[...], normed, inverse)
    held[...] = part.astype(bfloat)
    sums_ref[pl.ds(me_ref[0], 1), :packed] += column_sum(grad.astype(single))
    sums_ref[pl.ds(passes + pass_index, 1), :] += column_sum(part)
    sums_ref[8:9, :] += column_sum(back * normed)
    sums_ref[9:10, :] += column_sum(back)
    for index in range(count):

        @pl.when(slot == index)
        def _():
            rows_refs[index][...] = held[...]


def project_back(order, pieces, pass_emb, gain, shift, weight, grads, stats, last_sums):
    count = len(pieces)
    length, width = pieces[0].shape
    passes, _, packed = grads.shape
    block = min(512, length)
    steps = length // block
    sums_shape = (16 + last_sums.shape[0], width)

    def piece_spec(index):
        def where(slot, step, order_ref):
            return (jnp.where(slot == index, step, jnp.where(slot < index, 0, steps - 1)), 0)

        return pl.BlockSpec((block, width), where)

    def whole(shape):
        return pl.BlockSpec(shape, lambda slot, step, order_ref: (0,) * len(shape))

    def by_pass(size):
        return pl.BlockSpec(
            (pl.Squeezed(), block, size), lambda slot, step, order_ref: (order_ref[1 + slot], step, 0)
        )

    small = [pass_emb, gain, shift]
    return pl.pallas_call(
        functools.partial(project_back_kernel, count, passes),
        grid_spec=pltpu.PrefetchScalarGridSpec(
            num_scalar_prefetch=1,
            grid=(count, steps),
            in_specs=[piece_spec(index) for index in range(count)]
            + [whole(operand.shape) for operand in small]
            + [whole(weight.shape), by_pass(packed), by_pass(2), whole(last_sums.shape)],
            out_specs=[piece_spec(index) for index in range(count)]
            + [whole((width, packed)), whole(sums_shape)],
            scratch_shapes=[pltpu.VMEM((block, width), bfloat)],
        ),
        out_shape=[in_hbm((length, width), bfloat)] * count
        + [jax.ShapeDtypeStruct((width, packed), single), jax.ShapeDtypeStruct(sums_shape, single)],
        compiler_params=pltpu.CompilerParams(vmem_limit_bytes=48 << 20),
        cost_estimate=pl.CostEstimate(flops=16 << 30, transcendentals=0, bytes_accessed=20 << 20),
        name="project_back",
    )(order, *from_hbm(pieces), *small, *from_hbm([weight, grads, stats]), last_sums)


def exchange(value, axis, distance):
    return lax.ppermute(value, axis, [(k, k ^ distance) for k in range(lax.axis_size(axis))])


def summing_steps():
    passes, sequences = lax.axis_size("pass"), lax.axis_size("seq")
    steps = [("pass", distance) for distance in (2**power for power in range(1, passes)) if distance < passes]
    steps += [("seq", distance) for distance in (2**power for power in range(sequences)) if distance < sequences]
    return steps + [("pass", 1)]


def per_device(
    x_rows,
    pass_depth,
    cotangent,
    pass_emb,
    ln1_gain,
    ln1_bias,
    w_qkv,
    q_bias,
    v_bias,
    w_out,
    out_bias,
    ln2_gain,
    ln2_bias,
    w_up,
    up_bias,
    w_down,
    down_bias,
):
    everyone = ("seq", "pass")
    _, length, width = x_rows.shape
    hidden = w_up.shape[1]
    passes = lax.axis_size("pass")
    devices = passes * lax.axis_size("seq")
    shard = w_qkv.shape[0]
    group = width // passes
    group_heads = group // HEAD_DIM
    me = lax.axis_index("pass")
    order = jnp.concatenate([me[None], jnp.bitwise_xor(me, jnp.arange(passes))]).astype(jnp.int32)

    def swap(value, distance):
        return exchange(value, "pass", distance)

    x_own = x_rows[0]

    by_group = w_qkv.reshape(shard, 3, passes, group).transpose(2, 0, 1, 3).reshape(passes, shard, 3 * group)
    by_rows = lax.all_to_all(by_group, "pass", 0, 0, tiled=True).reshape(passes * shard, 3 * group)
    by_rows, x_ready = lax.optimization_barrier((by_rows, x_own))
    x_one = swap(x_ready, 1)
    x_two = swap(x_ready, 2)
    w_heads = lax.all_gather(by_rows, "seq", axis=0, tiled=True)

    down_cols = w_down.reshape(passes, shard, width).transpose(1, 0, 2).reshape(shard, hidden)
    gathered = lax.all_gather(
        jnp.concatenate([w_out, w_up, down_cols], axis=1), everyone, axis=0, tiled=True
    )
    in_place = shard % 8 == 0
    full_down = None
    if not in_place:
        full_down = (
            gathered[:, width + hidden :]
            .reshape(devices, shard, hidden // width, width)
            .transpose(0, 2, 1, 3)
            .reshape(hidden, width)
        )

    gain_one, shift_one = ln1_gain[None], ln1_bias[None]
    own_q_bias = lax.dynamic_slice_in_dim(q_bias, me * group, group)
    own_v_bias = lax.dynamic_slice_in_dim(v_bias, me * group, group)
    bias_row = jnp.concatenate([own_q_bias, jnp.zeros((group,), single), own_v_bias])[None]
    pad = (-3 * group) % LANES
    w_wide = jnp.pad(w_heads, ((0, 0), (0, pad)))
    bias_wide = jnp.pad(bias_row, ((0, 0), (0, pad)))
    depth = pass_depth.reshape(length, 1)
    near = project(
        order[:3], (x_own, x_one), passes, pass_emb, gain_one, shift_one, w_wide, bias_wide, depth, None
    )
    x_two, near = lax.optimization_barrier((x_two, near))
    x_three = swap(x_two, 1)
    far_order = jnp.concatenate([order[:1], order[3:]])
    queries, keys, values, stats = project(
        far_order, (x_two, x_three), passes, pass_emb, gain_one, shift_one, w_wide, bias_wide, depth, near
    )

    def trade(pieces):
        return list(pieces[:1]) + [swap(pieces[slot], slot) for slot in range(1, passes)]

    pass_row = lax.dynamic_index_in_dim(pass_emb, me, 0, keepdims=True)
    outs, logged = [None, None], [None, None]
    for half in (1, 0):
        outs[half], logged[half] = attend(order[:1], queries, keys, values, half)
    parts = [trade(outs[half]) for half in range(2)]
    results = None
    head_grads = [None, None]
    for half in (1, 0):
        results, head_grads[half] = middle(
            order[:1],
            parts[half],
            x_own,
            cotangent[0],
            pass_row,
            out_bias[None],
            ln2_gain[None],
            ln2_bias[None],
            up_bias[None],
            down_bias[None],
            gathered,
            full_down,
            shard,
            half,
            results,
        )
        head_grads[half] = trade(head_grads[half])
    out_rows, mixed_grad, normed_two, activated, upper_low, proj_low, sums = results

    weight_parts = weight_grads(
        order[:1],
        *parts,
        proj_low,
        normed_two,
        cotangent[0],
        upper_low,
        activated,
        shard if in_place else None,
    )
    if not in_place:
        down_part = (
            weight_parts[:, width + hidden :]
            .reshape(width, hidden // width, width)
            .transpose(1, 0, 2)
            .reshape(devices, hidden // width, shard, width)
            .transpose(0, 2, 1, 3)
            .reshape(width, hidden)
        )
        weight_parts = jnp.concatenate([weight_parts[:, : width + hidden], down_part], axis=1)
    weight_parts, logged, head_grads = lax.optimization_barrier((weight_parts, logged, head_grads))
    reduced = lax.psum_scatter(weight_parts, everyone, scatter_dimension=0, tiled=True).astype(single)
    shard_out = reduced[:, :width]
    shard_up = reduced[:, width : width + hidden]
    shard_down = (
        reduced[:, width + hidden :]
        .reshape(shard, hidden // width, width)
        .transpose(1, 0, 2)
        .reshape(w_down.shape)
    )

    qkv_low = attend_back(order[:1], logged, keys, values, outs, head_grads)
    near_own, near_one, far_two, far_three, head_weight, sums = project_back(
        order, (x_own, x_one, x_two, x_three), pass_emb, gain_one, shift_one, w_heads, qkv_low, stats, sums
    )

    near_one, far_three = swap(near_one, 1), swap(far_three, 1)
    far_sum = (far_two.astype(single) + far_three.astype(single)).astype(bfloat)
    pieces = head_weight.astype(bfloat).reshape(devices, shard, 3 * group)
    steps = summing_steps()
    totals = sums + exchange(sums, *steps[0])
    totals, far_sum, pieces = lax.optimization_barrier((totals, far_sum, pieces))
    far_sum = swap(far_sum, 2)
    x_grad = mixed_grad + near_own.astype(single) + near_one.astype(single) + far_sum.astype(single)

    pieces = lax.all_to_all(pieces, everyone, 0, 0, tiled=True)
    pieces = pieces.reshape(devices // passes, passes, shard, 3, group).astype(single).sum(axis=0)
    shard_qkv = pieces.transpose(1, 2, 0, 3).reshape(w_qkv.shape)

    for axis, distance in steps[1:]:
        totals = totals + exchange(totals, axis, distance)
    biases = totals[:passes, : 3 * group].reshape(passes, 3, group)
    pass_grad = lax.dynamic_slice_in_dim(totals, passes + me, 1, 0)
    up_rows = hidden // width
    return (
        out_rows[None],
        x_grad[None],
        shard_qkv,
        biases[:, 0].reshape(-1),
        biases[:, 2].reshape(-1),
        shard_out,
        totals[16],
        totals[8],
        totals[9],
        totals[17],
        totals[18],
        shard_up,
        totals[20 : 20 + up_rows].reshape(-1),
        shard_down,
        totals[19],
        pass_grad,
    )


def solution(mesh):
    placed = (
        P("pass", "seq", None),
        P("seq", None),
        P("pass", "seq", None),
        P(),
        P(),
        P(),
        P(("seq", "pass"), None),
        P(),
        P(),
        P(("seq", "pass"), None),
        P(),
        P(),
        P(),
        P(("seq", "pass"), None),
        P(),
        P(("seq", "pass"), None),
        P(),
    )
    return jax.shard_map(
        per_device,
        mesh=mesh,
        in_specs=placed,
        out_specs=(
            P("pass", "seq", None),
            P("pass", "seq", None),
            P(("seq", "pass"), None),
            P(),
            P(),
            P(("seq", "pass"), None),
            P(),
            P(),
            P(),
            P(),
            P(),
            P(("seq", "pass"), None),
            P(),
            P(("seq", "pass"), None),
            P(),
            P("pass", None),
        ),
        check_vma=False,
    )
```

```python
import functools

import jax
import jax.numpy as jnp
from jax import lax
from jax.experimental import pallas as pl
from jax.experimental.pallas import tpu as pltpu
from jax.sharding import PartitionSpec as P

HEADS = 12
HEAD_DIM = 64
LANES = 128
NORM_EPS = 1e-05
MASKED = -1e30
BIAS_COL = 64
STAT_COL = 65
DELTA_COL = 64

bfloat = jnp.bfloat16
single = jnp.float32


def in_hbm(shape, dtype):
    return pltpu.HBM(shape, dtype)


def from_hbm(values):
    return [pltpu.with_memory_space_constraint(value, pltpu.HBM) for value in values]


def dot_nn(a, b):
    return jnp.dot(a, b, preferred_element_type=single)


def dot_nt(a, b):
    return lax.dot_general(a, b, (((1,), (1,)), ((), ())), preferred_element_type=single)


def dot_tn(a, b):
    return lax.dot_general(a, b, (((0,), (0,)), ((), ())), preferred_element_type=single)


def three_parts(value):
    first = value.astype(bfloat).astype(single)
    rest = value - first
    second = rest.astype(bfloat).astype(single)
    return first, second, rest - second


def with_columns(base, start, columns):
    lane = lax.broadcasted_iota(jnp.int32, base.shape, 1)
    for offset, column in enumerate(columns):
        base = jnp.where(lane == start + offset, column, base)
    return base


def norm_parts(values):
    center = values - jnp.mean(values, axis=-1, keepdims=True)
    inverse = lax.rsqrt(jnp.mean(center * center, axis=-1, keepdims=True) + NORM_EPS)
    return center * inverse, inverse


def norm_back(grad, gain, normed, inverse):
    scaled = grad * gain
    mean_one = jnp.mean(scaled, axis=-1, keepdims=True)
    mean_two = jnp.mean(scaled * normed, axis=-1, keepdims=True)
    return inverse * (scaled - mean_one - normed * mean_two)


def head_slab(packed, index):
    low = (index // 2) * LANES
    slab = packed[:, low : low + LANES]
    if index % 2:
        slab = pltpu.roll(slab, HEAD_DIM, axis=1)
    return slab


def pack_heads(slabs):
    packed = []
    lane = lax.broadcasted_iota(jnp.int32, slabs[0].shape, 1)
    for index in range(0, len(slabs), 2):
        if index + 1 < len(slabs):
            other = pltpu.roll(slabs[index + 1], HEAD_DIM, axis=1)
            packed.append(jnp.where(lane < HEAD_DIM, slabs[index], other))
        else:
            packed.append(slabs[index])
    width = len(slabs) * HEAD_DIM
    return jnp.concatenate(packed, axis=1)[:, :width]


def project_kernel(heads, count, me_ref, *refs):
    pieces = refs[:count]
    pass_ref, gain_ref, shift_ref, weight_ref, bias_ref, depth_ref = refs[count : count + 6]
    q_ref, k_ref, v_ref, stats_ref = refs[-4:]
    slot = pl.program_id(0)
    pass_index = me_ref[1 + slot]
    pass_row = pass_ref[pl.ds(pass_index, 1), :]
    rows = pieces[0][...]
    for index in range(1, count):
        rows = jnp.where(slot == index, pieces[index][...], rows)
    rows = rows.astype(single) + pass_row
    mean = jnp.mean(rows, axis=-1, keepdims=True)
    center = rows - mean
    inverse = lax.rsqrt(jnp.mean(center * center, axis=-1, keepdims=True) + NORM_EPS)
    lane = lax.broadcasted_iota(jnp.int32, stats_ref.shape, 1)
    stats_ref[...] = jnp.where(lane == 0, inverse, -mean * inverse)
    low = (center * inverse * gain_ref[...] + shift_ref[...]).astype(bfloat)
    projected = dot_nn(low, weight_ref[...]) + bias_ref[...]
    lane = lax.broadcasted_iota(jnp.int32, (low.shape[0], LANES), 1)
    inside = lane < HEAD_DIM
    depth_bias = jnp.where(pass_index < depth_ref[...], 0.0, MASKED)
    q_rest = jnp.where(lane == BIAS_COL, 1.0, 0.0)
    k_rest = jnp.where(
        lane == BIAS_COL, depth_bias, jnp.where((lane >= STAT_COL) & (lane < STAT_COL + 3), 1.0, 0.0)
    )
    v_rest = jnp.where((lane >= DELTA_COL) & (lane < DELTA_COL + 3), 1.0, 0.0)
    for head in range(heads):
        q_part = head_slab(projected, head).astype(bfloat).astype(single) * (HEAD_DIM**-0.5)
        q_ref[head] = jnp.where(inside, q_part, q_rest).astype(bfloat)
        k_ref[head] = jnp.where(inside, head_slab(projected, heads + head), k_rest).astype(bfloat)
        v_ref[head] = jnp.where(inside, head_slab(projected, 2 * heads + head), v_rest).astype(bfloat)


def project(order, pieces, passes, pass_emb, gain, shift, weight, bias, depth, previous):
    count = len(pieces)
    length, width = pieces[0].shape
    heads = weight.shape[1] // (3 * HEAD_DIM)
    block = min(512, length)
    steps = length // block

    def piece_spec(index):
        def where(slot, step, order_ref):
            return (jnp.where(slot == index, step, jnp.where(slot < index, 0, steps - 1)), 0)

        return pl.BlockSpec((block, width), where)

    def whole(shape):
        return pl.BlockSpec(shape, lambda slot, step, order_ref: (0,) * len(shape))

    out_spec = pl.BlockSpec(
        (heads, pl.Squeezed(), block, LANES),
        lambda slot, step, order_ref: (0, order_ref[1 + slot], step, 0),
    )
    shape = in_hbm((heads, passes, length, LANES), bfloat)
    stats_spec = pl.BlockSpec(
        (pl.Squeezed(), block, 2), lambda slot, step, order_ref: (order_ref[1 + slot], step, 0)
    )
    in_specs = [piece_spec(index) for index in range(count)] + [
        whole(pass_emb.shape),
        whole(gain.shape),
        whole(shift.shape),
        whole(weight.shape),
        whole(bias.shape),
        pl.BlockSpec((block, 1), lambda slot, step, order_ref: (step, 0)),
    ]
    operands = [*pieces, pass_emb, gain, shift, weight, bias, depth]
    aliases = {}
    if previous is not None:
        aliases = {1 + len(operands) + index: index for index in range(4)}
        in_specs += [pl.BlockSpec(memory_space=pl.ANY)] * 4
        operands += list(previous)
    return pl.pallas_call(
        functools.partial(project_kernel, heads, count),
        grid_spec=pltpu.PrefetchScalarGridSpec(
            num_scalar_prefetch=1,
            grid=(count, steps),
            in_specs=in_specs,
            out_specs=[out_spec] * 3 + [stats_spec],
        ),
        out_shape=[shape] * 3 + [in_hbm((passes, length, 2), single)],
        input_output_aliases=aliases,
        compiler_params=pltpu.CompilerParams(vmem_limit_bytes=40 << 20),
        cost_estimate=pl.CostEstimate(flops=8 << 30, transcendentals=0, bytes_accessed=12 << 20),
        name="project",
    )(order, *operands)


def attend_kernel(passes, block, first, last, me_ref, q_ref, k_ref, v_ref, *refs):
    out_refs, q_next_ref, held = refs[:passes], refs[passes], refs[passes + 1]
    heads = q_ref.shape[0]
    step = pl.program_id(0)
    row = lax.broadcasted_iota(jnp.int32, (block, block), 0)
    col = lax.broadcasted_iota(jnp.int32, (block, block), 1)
    causal = col <= row

    def one_head(head, count):
        kept = [[] for _ in range(passes)]
        highest = [None] * passes
        for key_pass in range(passes):
            span = passes - key_pass
            query = q_ref[head, key_pass:passes].reshape(span * block, LANES)
            for tile in range(count):
                both = dot_nt(query, k_ref[head, key_pass, tile * block : (tile + 1) * block, :])
                for query_pass in range(key_pass, passes):
                    start = (query_pass - key_pass) * block
                    scores = both[start : start + block]
                    if tile == count - 1:
                        scores = jnp.where(causal, scores, MASKED)
                    kept[query_pass].append(scores)
                    for lane in range(0, block, LANES):
                        part = scores[:, lane : lane + LANES]
                        old = highest[query_pass]
                        highest[query_pass] = part if old is None else jnp.maximum(old, part)
        highest = [jnp.max(part, axis=-1, keepdims=True) for part in highest]
        for query_pass in range(passes):
            total = None
            for index, scores in enumerate(kept[query_pass]):
                key_pass, tile = divmod(index, count)
                weights = jnp.exp(scores - highest[query_pass]).astype(bfloat)
                term = dot_nn(weights, v_ref[head, key_pass, tile * block : (tile + 1) * block, :])
                total = term if total is None else total + term
            row_sum = total[:, DELTA_COL : DELTA_COL + 1]
            log_sum = highest[query_pass] + jnp.log(row_sum)
            q_next_ref[head, query_pass] = with_columns(
                q_ref[head, query_pass].astype(single), STAT_COL, three_parts(-log_sum)
            ).astype(bfloat)
            held[head, query_pass] = total * (1.0 / row_sum)

    for index in range(first, last):

        @pl.when(step == index - first)
        def _():
            lax.fori_loop(0, heads, lambda head, _: (one_head(head, index + 1), 0)[1], 0)

    for slot in range(passes):
        query_pass = jnp.bitwise_xor(me_ref[0], slot)
        out_refs[slot][...] = pack_heads([held[head, query_pass] for head in range(heads)]).astype(bfloat)


def attend(me, queries, keys, values, half):
    heads, passes, length, _ = queries.shape
    block = min(256, length // 2)
    count = length // 2 // block
    first, last = half * count, (half + 1) * count
    seen = pl.BlockSpec(
        (heads, passes, last * block, LANES),
        lambda step, me_ref: (0, 0, 0, 0),
        pipeline_mode=pl.Buffered(1),
    )
    part = pl.BlockSpec((heads, passes, block, LANES), lambda step, me_ref: (0, 0, first + step, 0))
    part_out = pl.BlockSpec((heads, passes, block, LANES), lambda step, me_ref: (0, 0, step, 0))
    packed = heads * HEAD_DIM
    *outs, queries = pl.pallas_call(
        functools.partial(attend_kernel, passes, block, first, last),
        grid_spec=pltpu.PrefetchScalarGridSpec(
            num_scalar_prefetch=1,
            grid=(count,),
            in_specs=[part, seen, seen],
            out_specs=[pl.BlockSpec((block, packed), lambda step, me_ref: (step, 0))] * passes + [part_out],
            scratch_shapes=[pltpu.VMEM((heads, passes, block, LANES), single)],
        ),
        out_shape=[in_hbm((length // 2, packed), bfloat)] * passes
        + [in_hbm((heads, passes, length // 2, LANES), bfloat)],
        compiler_params=pltpu.CompilerParams(vmem_limit_bytes=48 << 20),
        cost_estimate=pl.CostEstimate(
            flops=(10 + 20 * half) << 30,
            transcendentals=heads * (1 + 2 * half) * length * length,
            bytes_accessed=12 << 20,
        ),
        name="attend",
    )(me, *from_hbm((queries, keys, values)))
    return outs, queries


def attend_back_kernel(passes, block, me_ref, *refs):
    q_refs, (k_ref, v_ref), refs = refs[:2], refs[2:4], refs[4:]
    out_refs = refs[:passes], refs[passes : 2 * passes]
    grad_refs = refs[2 * passes : 3 * passes], refs[3 * passes : 4 * passes]
    all_ref, key_acc, value_acc, grad_held, query_held = refs[4 * passes :]
    heads = k_ref.shape[0]
    blocks = k_ref.shape[2] // block
    step = pl.program_id(0)
    me = me_ref[0]
    row = lax.broadcasted_iota(jnp.int32, (block, block), 0)
    col = lax.broadcasted_iota(jnp.int32, (block, block), 1)
    causal = row <= col
    inside = lax.broadcasted_iota(jnp.int32, (block, LANES), 1) < HEAD_DIM
    padded = ((heads * HEAD_DIM + LANES - 1) // LANES) * LANES

    @pl.when(step == 0)
    def _():
        key_acc[...] = jnp.zeros(key_acc.shape, single)
        value_acc[...] = jnp.zeros(value_acc.shape, single)

    def prepare(half):
        for slot in range(passes):
            query_pass = jnp.bitwise_xor(me, slot)
            grad = grad_refs[half][slot][...].astype(single)
            out = out_refs[half][slot][...].astype(single)
            if padded > heads * HEAD_DIM:
                tail = jnp.zeros((block, padded - heads * HEAD_DIM), single)
                grad = jnp.concatenate([grad, tail], axis=1)
                out = jnp.concatenate([out, tail], axis=1)
            product = grad * out
            for head in range(heads):
                delta = jnp.sum(
                    jnp.where(inside, head_slab(product, head), 0.0), axis=-1, keepdims=True
                )
                base = jnp.where(inside, head_slab(grad, head), 0.0)
                grad_held[head, query_pass] = with_columns(base, DELTA_COL, three_parts(-delta)).astype(bfloat)

    def one_head(head, count, q_ref):
        query_sums = [None] * passes
        for key_pass in range(passes):
            span = passes - key_pass
            query = q_ref[head, key_pass:passes].reshape(span * block, LANES)
            grad = grad_held[head, key_pass:passes].reshape(span * block, LANES)
            for tile in range(count):
                window = slice(tile * block, (tile + 1) * block)
                key = k_ref[head, key_pass, window, :]
                value = v_ref[head, key_pass, window, :]
                prob = jnp.exp(dot_nt(key, query))
                if tile == count - 1:
                    prob = jnp.where(jnp.concatenate([causal] * span, axis=1), prob, 0.0)
                value_acc[head, key_pass, window, :] += dot_nn(prob.astype(bfloat), grad)
                score_grad = (prob * dot_nt(value, grad)).astype(bfloat)
                key_acc[head, key_pass, window, :] += dot_nn(score_grad, query)
                term = dot_tn(key, score_grad)
                for query_pass in range(key_pass, passes):
                    start = (query_pass - key_pass) * block
                    part = term[:, start : start + block]
                    old = query_sums[query_pass]
                    query_sums[query_pass] = part if old is None else old + part
        for query_pass in range(passes):
            query_held[head, query_pass] = query_sums[query_pass].T * (HEAD_DIM**-0.5)

    for index in range(blocks):

        @pl.when(step == blocks - 1 - index)
        def _():
            half = index // (blocks // 2)
            prepare(half)
            lax.fori_loop(0, heads, lambda head, _: (one_head(head, index + 1, q_refs[half]), 0)[1], 0)
            window = slice(index * block, (index + 1) * block)
            for query_pass in range(passes):
                slabs = [query_held[head, query_pass] for head in range(heads)]
                slabs += [key_acc[head, query_pass, window, :] for head in range(heads)]
                slabs += [value_acc[head, query_pass, window, :] for head in range(heads)]
                all_ref[query_pass] = pack_heads(slabs).astype(bfloat)


def attend_back(me, queries, keys, values, outs, grads):
    heads, passes, length, _ = keys.shape
    block = min(256, length // 2)
    count = length // 2 // block
    packed = heads * HEAD_DIM

    def spot(half):
        return lambda step: jnp.clip(2 * count - 1 - step - half * count, 0, count - 1)

    def query_spec(half):
        return pl.BlockSpec((heads, passes, block, LANES), lambda step, me_ref: (0, 0, spot(half)(step), 0))

    def rows_spec(half):
        return pl.BlockSpec((block, packed), lambda step, me_ref: (spot(half)(step), 0))

    whole = pl.BlockSpec(keys.shape, lambda step, me_ref: (0, 0, 0, 0), pipeline_mode=pl.Buffered(1))
    rows_specs = [rows_spec(half) for half in range(2) for _ in range(passes)]
    return pl.pallas_call(
        functools.partial(attend_back_kernel, passes, block),
        grid_spec=pltpu.PrefetchScalarGridSpec(
            num_scalar_prefetch=1,
            grid=(2 * count,),
            in_specs=[query_spec(0), query_spec(1), whole, whole] + rows_specs * 2,
            out_specs=pl.BlockSpec(
                (passes, block, 3 * packed), lambda step, me_ref: (0, 2 * count - 1 - step, 0)
            ),
            scratch_shapes=[
                pltpu.VMEM(keys.shape, single),
                pltpu.VMEM(keys.shape, single),
                pltpu.VMEM((heads, passes, block, LANES), bfloat),
                pltpu.VMEM((heads, passes, block, LANES), single),
            ],
        ),
        out_shape=in_hbm((passes, length, 3 * packed), bfloat),
        compiler_params=pltpu.CompilerParams(vmem_limit_bytes=58 << 20),
        cost_estimate=pl.CostEstimate(
            flops=300 << 30, transcendentals=heads * 6 * length * length, bytes_accessed=20 << 20
        ),
        name="attend_back",
    )(me, *from_hbm((*queries, keys, values, *outs[0], *outs[1], *grads[0], *grads[1])))


def middle_kernel(groups, downs, shard, begins, me_ref, *refs):
    parts = refs[:groups]
    x_ref, cot_ref, pass_ref, out_bias_ref, gain_ref, shift_ref, down_bias_ref, up_bias_ref, w_out_ref, w_up_ref = refs[
        groups : groups + 10
    ]
    refs = refs[groups + 10 :]
    down_refs = refs[:downs]
    last_sums_ref = None if begins else refs[downs]
    outs, scratch = refs[-11 - groups : -5 - groups], refs[-5:]
    rows_ref, normed_ref, active_ref, upper_ref, proj_ref, sums_ref = outs
    grads = refs[-5 - groups : -5]
    normed_held, inverse_held, total_held, back_held, w_down_held = scratch
    me = me_ref[0]
    width = x_ref.shape[1]
    packed = width // groups
    step = pl.program_id(0)

    def group_window(slot):
        start = pl.multiple_of(jnp.bitwise_xor(me, slot) * packed, packed)
        return pl.ds(start, packed)

    def column_sum(values):
        return jnp.sum(values, axis=0, keepdims=True)

    @pl.when(step == 0)
    def _():
        sums_ref[...] = jnp.zeros(sums_ref.shape, single) if begins else last_sums_ref[...]
        mixed = x_ref[...].astype(single) + pass_ref[...] + out_bias_ref[...]
        for slot in range(groups):
            mixed += dot_nn(parts[slot][...], w_out_ref[group_window(slot), :])
        normed, inverse = norm_parts(mixed)
        normed_ref[...] = (normed * gain_ref[...] + shift_ref[...]).astype(bfloat)
        normed_held[...] = normed
        inverse_held[...] = jnp.broadcast_to(inverse, inverse_held.shape)
        total_held[...] = mixed + down_bias_ref[...]
        back_held[...] = jnp.zeros(back_held.shape, single)

    if shard:
        for start in range(0, down_refs[0].shape[0], 2 * shard):
            blocks = [ref[start : start + 2 * shard, :].astype(single) for ref in down_refs]
            pieces = [block[side * shard : (side + 1) * shard] for side in range(2) for block in blocks]
            w_down_held[start * downs : (start + 2 * shard) * downs, :] = jnp.concatenate(
                pieces, axis=0
            ).astype(bfloat)
        w_down_ref = w_down_held
    else:
        w_down_ref = down_refs[0]

    upper = dot_nn(normed_ref[...], w_up_ref[...]) + up_bias_ref[...]
    below = 0.5 + 0.5 * lax.erf(upper * (0.5**0.5))
    density = jnp.exp(-0.5 * upper * upper) * 0.3989422804014327
    active = (upper * below).astype(bfloat)
    active_ref[...] = active
    total_held[...] += dot_nn(active, w_down_ref[...])
    upper_low = (dot_nt(cot_ref[...], w_down_ref[...]) * (below + upper * density)).astype(bfloat)
    upper_ref[...] = upper_low
    sums_ref[pl.ds(4 + step, 1), :] += column_sum(upper_low.astype(single))
    back_held[...] += dot_nt(upper_low, w_up_ref[...])

    @pl.when(step == pl.num_programs(0) - 1)
    def _():
        rows_ref[...] = total_held[...].astype(bfloat)
        out_grad = cot_ref[...].astype(single)
        normed, back = normed_held[...], back_held[...]
        mixed_grad = out_grad + norm_back(back, gain_ref[...], normed, inverse_held[:, 0:1])
        proj_low = mixed_grad.astype(bfloat)
        proj_ref[...] = proj_low
        for slot in range(groups):
            grads[slot][...] = dot_nt(proj_low, w_out_ref[group_window(slot), :]).astype(bfloat)
        sums_ref[0:1, :] += column_sum(mixed_grad)
        sums_ref[1:2, :] += column_sum(back * normed)
        sums_ref[2:3, :] += column_sum(back)
        sums_ref[3:4, :] += column_sum(out_grad)


def middle(
    me,
    parts,
    x_own,
    cot,
    pass_row,
    out_bias,
    gain,
    shift,
    up_bias,
    down_bias,
    gathered,
    w_down,
    shard,
    half,
    previous,
):
    length, width = x_own.shape
    hidden = up_bias.shape[1]
    chunks = hidden // width
    groups = len(parts)
    packed = width // groups
    block = length // 2

    def rows(size):
        return pl.BlockSpec((block, size), lambda step, me_ref: (half, 0))

    def half_rows(size):
        return pl.BlockSpec((block, size), lambda step, me_ref: (0, 0))

    def whole(shape):
        return pl.BlockSpec(shape, lambda step, me_ref: (0, 0), pipeline_mode=pl.Buffered(1))

    def fixed(shape):
        return pl.BlockSpec(shape, lambda step, me_ref: (0, 0))

    by_chunk = pl.BlockSpec((block, width), lambda step, me_ref: (half, step))
    sums_shape = ((4 + chunks + 7) // 8 * 8, width)
    square = (width, width)
    small = (pass_row, out_bias, gain, shift, down_bias)
    if w_down is None:
        downs = chunks

        def down_spec(col):
            return pl.BlockSpec((width // chunks, width), lambda step, me_ref: (step, 1 + chunks + col))

        down_specs = [down_spec(col) for col in range(chunks)]
        down = [gathered] * chunks
    else:
        downs = 1
        down_specs = [pl.BlockSpec(square, lambda step, me_ref: (step, 0))]
        down = [w_down]
        shard = None
    in_specs = (
        [half_rows(packed)] * groups
        + [rows(width), rows(width)]
        + [whole(operand.shape) for operand in small]
        + [pl.BlockSpec((1, width), lambda step, me_ref: (0, step))]
        + [whole(square), pl.BlockSpec(square, lambda step, me_ref: (0, 1 + step))]
        + down_specs
    )
    operands = [*from_hbm([*parts, x_own, cot]), *small, up_bias, *from_hbm([gathered] * 2 + down)]
    aliases = {}
    if previous is not None:
        in_specs += [fixed(sums_shape)] + [pl.BlockSpec(memory_space=pl.ANY)] * 5
        aliases = {2 + len(operands) + index: index for index in range(5)}
        operands += [previous[5], *previous[:5]]
    results = pl.pallas_call(
        functools.partial(middle_kernel, groups, downs, shard, previous is None),
        grid_spec=pltpu.PrefetchScalarGridSpec(
            num_scalar_prefetch=1,
            grid=(chunks,),
            in_specs=in_specs,
            out_specs=[rows(width), rows(width), by_chunk, by_chunk, rows(width), fixed(sums_shape)]
            + [half_rows(packed)] * groups,
            scratch_shapes=[
                pltpu.VMEM((block, width), single),
                pltpu.VMEM((block, LANES), single),
                pltpu.VMEM((block, width), single),
                pltpu.VMEM((block, width), single),
                pltpu.VMEM(square, bfloat),
            ],
        ),
        out_shape=[
            in_hbm((length, width), bfloat),
            in_hbm((length, width), bfloat),
            in_hbm((length, hidden), bfloat),
            in_hbm((length, hidden), bfloat),
            in_hbm((length, width), bfloat),
            jax.ShapeDtypeStruct(sums_shape, single),
        ]
        + [in_hbm((length // 2, packed), bfloat)] * groups,
        input_output_aliases=aliases,
        compiler_params=pltpu.CompilerParams(vmem_limit_bytes=56 << 20),
        cost_estimate=pl.CostEstimate(
            flops=20 << 30, transcendentals=length * hidden, bytes_accessed=24 << 20
        ),
        name="middle",
    )(me, *operands)
    return results[:6], results[6:]


def weight_grad_kernel(groups, chunks, shard, me_ref, *refs):
    late_loads = refs[: 2 * groups + 1]
    normed_ref, cot_ref, upper_ref, active_ref, out_ref, staged, staged_down, sent, sent_down = refs[
        2 * groups + 1 : 2 * groups + 10
    ]
    loaded, loads = refs[2 * groups + 10 : -1], refs[-1]
    early, late, proj_ref = loaded[:groups], loaded[groups : 2 * groups], loaded[-1]
    length, width = normed_ref.shape
    middle_row = length // 2
    packed = width // groups
    rows = width // chunks
    step = pl.program_id(0)

    def columns_copy(index):
        start = pl.multiple_of(index * width, width)
        return pltpu.make_async_copy(staged.at[index], out_ref.at[:, pl.ds(start, width)], sent.at[index])

    def down_copy(index):
        if shard:
            start = pl.multiple_of(index * rows, rows)
            target = out_ref.at[pl.ds(start, rows), pl.ds((1 + chunks) * width, chunks * width)]
        else:
            start = pl.multiple_of((1 + chunks + index) * width, width)
            target = out_ref.at[:, pl.ds(start, width)]
        return pltpu.make_async_copy(staged_down.at[index], target, sent_down.at[index])

    def load(index):
        return pltpu.make_async_copy(late_loads[index], loaded[index], loads.at[index])

    @pl.when(step == 0)
    def _():
        for index in range(2 * groups + 1):
            load(index).start()

    @pl.when(step < chunks)
    def _():
        staged[step + 1] = dot_tn(normed_ref[...], upper_ref[...]).astype(bfloat)
        down = dot_tn(active_ref[...], cot_ref[...])
        if shard:
            for start in range(0, rows, 2 * shard):
                for chunk in range(chunks):
                    first = start * chunks + chunk * shard
                    second = first + chunks * shard
                    staged_down[step, start : start + 2 * shard, chunk * width : (chunk + 1) * width] = (
                        jnp.concatenate(
                            [down[first : first + shard], down[second : second + shard]], axis=0
                        ).astype(bfloat)
                    )
        else:
            staged_down[step] = down.astype(bfloat)
        columns_copy(step + 1).start()
        down_copy(step).start()

    @pl.when(step == chunks)
    def _():
        for index in range(2 * groups + 1):
            load(index).wait()
        for slot in range(groups):
            start = pl.multiple_of(jnp.bitwise_xor(me_ref[0], slot) * packed, packed)
            staged[0, pl.ds(start, packed), :] = (
                dot_tn(early[slot][...], proj_ref[:middle_row, :])
                + dot_tn(late[slot][...], proj_ref[middle_row:, :])
            ).astype(bfloat)
        columns_copy(0).start()
        for index in range(1 + chunks):
            columns_copy(index).wait()
        for index in range(chunks):
            down_copy(index).wait()


def weight_grads(me, early, late, proj, normed, cot, upper, active, shard):
    length, width = proj.shape
    hidden = upper.shape[1]
    chunks = hidden // width
    groups = len(early)
    parts = [*early, *late]

    def whole(shape):
        return pl.BlockSpec(shape, lambda step, me_ref: (0, 0), pipeline_mode=pl.Buffered(1))

    by_chunk = pl.BlockSpec((length, width), lambda step, me_ref: (0, jnp.minimum(step, chunks - 1)))
    late_loads = [*parts, proj]
    down_shape = (width // chunks, chunks * width) if shard else (width, width)
    return pl.pallas_call(
        functools.partial(weight_grad_kernel, groups, chunks, shard),
        grid_spec=pltpu.PrefetchScalarGridSpec(
            num_scalar_prefetch=1,
            grid=(1 + chunks,),
            in_specs=[pl.BlockSpec(memory_space=pl.ANY)] * len(late_loads)
            + [whole(proj.shape)] * 2
            + [by_chunk] * 2,
            out_specs=pl.BlockSpec(memory_space=pl.ANY),
            scratch_shapes=[
                pltpu.VMEM((1 + chunks, width, width), bfloat),
                pltpu.VMEM((chunks, *down_shape), bfloat),
                pltpu.SemaphoreType.DMA((1 + chunks,)),
                pltpu.SemaphoreType.DMA((chunks,)),
            ]
            + [pltpu.VMEM(operand.shape, bfloat) for operand in late_loads]
            + [pltpu.SemaphoreType.DMA((len(late_loads),))],
        ),
        out_shape=in_hbm((width, width + 2 * hidden), bfloat),
        compiler_params=pltpu.CompilerParams(vmem_limit_bytes=56 << 20),
        cost_estimate=pl.CostEstimate(flops=20 << 30, transcendentals=0, bytes_accessed=32 << 20),
        name="weight_grads",
    )(me, *from_hbm([*parts, proj, normed, cot, upper, active]))


def split_weights_kernel(chunks, in_ref, out_ref, up_ref, down_ref):
    shard, width = out_ref.shape
    out_ref[...] = in_ref[:, :width].astype(single)
    up_ref[...] = in_ref[:, width : (1 + chunks) * width].astype(single)
    for chunk in range(chunks):
        start = (1 + chunks + chunk) * width
        down_ref[chunk * shard : (chunk + 1) * shard, :] = in_ref[:, start : start + width].astype(single)


def split_weights(reduced, width):
    shard, columns = reduced.shape
    hidden = (columns - width) // 2
    struct = jax.ShapeDtypeStruct
    return pl.pallas_call(
        functools.partial(split_weights_kernel, hidden // width),
        out_shape=[
            struct((shard, width), single),
            struct((shard, hidden), single),
            struct((shard * hidden // width, width), single),
        ],
        name="split_weights",
    )(reduced)


def join_groups_kernel(passes, in_ref, out_ref):
    sequences = in_ref.shape[0] // passes
    packed = in_ref.shape[2]
    group = packed // 3
    sums = []
    for index in range(passes):
        total = in_ref[index].astype(single)
        for sequence in range(1, sequences):
            total += in_ref[sequence * passes + index].astype(single)
        sums.append(total)
    width = passes * group
    for part in range(3):
        out_ref[:, part * width : (part + 1) * width] = jnp.concatenate(
            [total[:, part * group : (part + 1) * group] for total in sums], axis=1
        )


def join_groups(pieces, passes):
    _, shard, packed = pieces.shape
    return pl.pallas_call(
        functools.partial(join_groups_kernel, passes),
        out_shape=jax.ShapeDtypeStruct((shard, passes * packed), single),
        name="join_groups",
    )(pieces)


def project_back_kernel(count, passes, me_ref, *refs):
    pieces = refs[:count]
    pass_ref, gain_ref, shift_ref, weight_ref, grad_ref, stats_ref, last_sums_ref = refs[count : count + 7]
    *rows_refs, weight_low_ref, sums_ref, held, weight_grad_ref = refs[count + 7 :]
    slot = pl.program_id(0)
    step = pl.program_id(1)
    pass_index = me_ref[1 + slot]
    packed = grad_ref.shape[1]

    @pl.when((slot == 0) & (step == 0))
    def _():
        weight_grad_ref[...] = jnp.zeros(weight_grad_ref.shape, single)
        sums_ref[...] = jnp.zeros(sums_ref.shape, single)
        sums_ref[16:, :] = last_sums_ref[...]
        sums_ref[pl.ds(passes + me_ref[0], 1), :] = last_sums_ref[0:1, :]

    def column_sum(values):
        return jnp.sum(values, axis=0, keepdims=True)

    rows = pieces[0][...]
    for index in range(1, count):
        rows = jnp.where(slot == index, pieces[index][...], rows)
    stats = stats_ref[...]
    inverse = stats[:, 0:1]
    normed = (rows.astype(single) + pass_ref[pl.ds(pass_index, 1), :]) * inverse + stats[:, 1:2]
    low = (normed * gain_ref[...] + shift_ref[...]).astype(bfloat)
    grad = grad_ref[...]
    back = dot_nt(grad, weight_ref[...])
    weight_grad_ref[...] += dot_tn(low, grad)
    part = norm_back(back, gain_ref[...], normed, inverse)
    held[...] = part.astype(bfloat)
    sums_ref[pl.ds(me_ref[0], 1), :packed] += column_sum(grad.astype(single))
    sums_ref[pl.ds(passes + pass_index, 1), :] += column_sum(part)
    sums_ref[8:9, :] += column_sum(back * normed)
    sums_ref[9:10, :] += column_sum(back)
    for index in range(count):

        @pl.when(slot == index)
        def _():
            rows_refs[index][...] = held[...]

    @pl.when((slot == count - 1) & (step == pl.num_programs(1) - 1))
    def _():
        weight_low_ref[...] = weight_grad_ref[...].astype(bfloat)


def project_back(order, pieces, pass_emb, gain, shift, weight, grads, stats, last_sums):
    count = len(pieces)
    length, width = pieces[0].shape
    passes, _, packed = grads.shape
    block = min(512, length)
    steps = length // block
    sums_shape = (16 + last_sums.shape[0], width)

    def piece_spec(index):
        def where(slot, step, order_ref):
            return (jnp.where(slot == index, step, jnp.where(slot < index, 0, steps - 1)), 0)

        return pl.BlockSpec((block, width), where)

    def whole(shape):
        return pl.BlockSpec(shape, lambda slot, step, order_ref: (0,) * len(shape))

    def by_pass(size):
        return pl.BlockSpec(
            (pl.Squeezed(), block, size), lambda slot, step, order_ref: (order_ref[1 + slot], step, 0)
        )

    small = [pass_emb, gain, shift]
    return pl.pallas_call(
        functools.partial(project_back_kernel, count, passes),
        grid_spec=pltpu.PrefetchScalarGridSpec(
            num_scalar_prefetch=1,
            grid=(count, steps),
            in_specs=[piece_spec(index) for index in range(count)]
            + [whole(operand.shape) for operand in small]
            + [whole(weight.shape), by_pass(packed), by_pass(2), whole(last_sums.shape)],
            out_specs=[piece_spec(index) for index in range(count)]
            + [whole((width, packed)), whole(sums_shape)],
            scratch_shapes=[pltpu.VMEM((block, width), bfloat), pltpu.VMEM((width, packed), single)],
        ),
        out_shape=[in_hbm((length, width), bfloat)] * count
        + [jax.ShapeDtypeStruct((width, packed), bfloat), jax.ShapeDtypeStruct(sums_shape, single)],
        compiler_params=pltpu.CompilerParams(vmem_limit_bytes=48 << 20),
        cost_estimate=pl.CostEstimate(flops=16 << 30, transcendentals=0, bytes_accessed=20 << 20),
        name="project_back",
    )(order, *from_hbm(pieces), *small, *from_hbm([weight, grads, stats]), last_sums)


def exchange(value, axis, distance):
    return lax.ppermute(value, axis, [(k, k ^ distance) for k in range(lax.axis_size(axis))])


def summing_steps():
    passes, sequences = lax.axis_size("pass"), lax.axis_size("seq")
    steps = [("pass", distance) for distance in (2**power for power in range(1, passes)) if distance < passes]
    steps += [("seq", distance) for distance in (2**power for power in range(sequences)) if distance < sequences]
    return steps + [("pass", 1)]


def per_device(
    x_rows,
    pass_depth,
    cotangent,
    pass_emb,
    ln1_gain,
    ln1_bias,
    w_qkv,
    q_bias,
    v_bias,
    w_out,
    out_bias,
    ln2_gain,
    ln2_bias,
    w_up,
    up_bias,
    w_down,
    down_bias,
):
    everyone = ("seq", "pass")
    _, length, width = x_rows.shape
    hidden = w_up.shape[1]
    passes = lax.axis_size("pass")
    devices = passes * lax.axis_size("seq")
    shard = w_qkv.shape[0]
    group = width // passes
    group_heads = group // HEAD_DIM
    me = lax.axis_index("pass")
    order = jnp.concatenate([me[None], jnp.bitwise_xor(me, jnp.arange(passes))]).astype(jnp.int32)

    def swap(value, distance):
        return exchange(value, "pass", distance)

    x_own = x_rows[0]

    by_group = w_qkv.reshape(shard, 3, passes, group).transpose(2, 0, 1, 3).reshape(passes, shard, 3 * group)
    by_rows = lax.all_to_all(by_group, "pass", 0, 0, tiled=True).reshape(passes * shard, 3 * group)
    by_rows, x_ready = lax.optimization_barrier((by_rows, x_own))
    x_one = swap(x_ready, 1)
    x_two = swap(x_ready, 2)
    w_heads = lax.all_gather(by_rows, "seq", axis=0, tiled=True)

    down_cols = w_down.reshape(passes, shard, width).transpose(1, 0, 2).reshape(shard, hidden)
    gathered = lax.all_gather(
        jnp.concatenate([w_out, w_up, down_cols], axis=1), everyone, axis=0, tiled=True
    )
    in_place = shard % 8 == 0
    full_down = None
    if not in_place:
        full_down = (
            gathered[:, width + hidden :]
            .reshape(devices, shard, hidden // width, width)
            .transpose(0, 2, 1, 3)
            .reshape(hidden, width)
        )

    gain_one, shift_one = ln1_gain[None], ln1_bias[None]
    own_q_bias = lax.dynamic_slice_in_dim(q_bias, me * group, group)
    own_v_bias = lax.dynamic_slice_in_dim(v_bias, me * group, group)
    bias_row = jnp.concatenate([own_q_bias, jnp.zeros((group,), single), own_v_bias])[None]
    pad = (-3 * group) % LANES
    w_wide = jnp.pad(w_heads, ((0, 0), (0, pad)))
    bias_wide = jnp.pad(bias_row, ((0, 0), (0, pad)))
    depth = pass_depth.reshape(length, 1)
    near = project(
        order[:3], (x_own, x_one), passes, pass_emb, gain_one, shift_one, w_wide, bias_wide, depth, None
    )
    x_two, near = lax.optimization_barrier((x_two, near))
    x_three = swap(x_two, 1)
    far_order = jnp.concatenate([order[:1], order[3:]])
    queries, keys, values, stats = project(
        far_order, (x_two, x_three), passes, pass_emb, gain_one, shift_one, w_wide, bias_wide, depth, near
    )

    def trade(pieces):
        return list(pieces[:1]) + [swap(pieces[slot], slot) for slot in range(1, passes)]

    pass_row = lax.dynamic_index_in_dim(pass_emb, me, 0, keepdims=True)
    outs, logged = [None, None], [None, None]
    for half in (1, 0):
        outs[half], logged[half] = attend(order[:1], queries, keys, values, half)
    parts = [trade(outs[half]) for half in range(2)]
    results = None
    head_grads = [None, None]
    for half in (1, 0):
        results, head_grads[half] = middle(
            order[:1],
            parts[half],
            x_own,
            cotangent[0],
            pass_row,
            out_bias[None],
            ln2_gain[None],
            ln2_bias[None],
            up_bias[None],
            down_bias[None],
            gathered,
            full_down,
            shard,
            half,
            results,
        )
        head_grads[half] = trade(head_grads[half])
    out_rows, normed_two, activated, upper_low, proj_low, sums = results

    weight_parts = weight_grads(
        order[:1],
        *parts,
        proj_low,
        normed_two,
        cotangent[0],
        upper_low,
        activated,
        shard if in_place else None,
    )
    if not in_place:
        down_part = (
            weight_parts[:, width + hidden :]
            .reshape(width, hidden // width, width)
            .transpose(1, 0, 2)
            .reshape(devices, hidden // width, shard, width)
            .transpose(0, 2, 1, 3)
            .reshape(width, hidden)
        )
        weight_parts = jnp.concatenate([weight_parts[:, : width + hidden], down_part], axis=1)
    weight_parts, logged, head_grads = lax.optimization_barrier((weight_parts, logged, head_grads))
    reduced = lax.psum_scatter(weight_parts, everyone, scatter_dimension=0, tiled=True)
    if in_place:
        shard_out, shard_up, shard_down = split_weights(reduced, width)
    else:
        reduced = reduced.astype(single)
        shard_out = reduced[:, :width]
        shard_up = reduced[:, width : width + hidden]
        shard_down = (
            reduced[:, width + hidden :]
            .reshape(shard, hidden // width, width)
            .transpose(1, 0, 2)
            .reshape(w_down.shape)
        )

    qkv_low = attend_back(order[:1], logged, keys, values, outs, head_grads)
    near_own, near_one, far_two, far_three, head_weight, sums = project_back(
        order, (x_own, x_one, x_two, x_three), pass_emb, gain_one, shift_one, w_heads, qkv_low, stats, sums
    )

    near_one, far_three = swap(near_one, 1), swap(far_three, 1)
    far_sum = (far_two.astype(single) + far_three.astype(single)).astype(bfloat)
    pieces = head_weight.reshape(devices, shard, 3 * group)
    steps = summing_steps()
    totals = sums + exchange(sums, *steps[0])
    totals, far_sum, pieces = lax.optimization_barrier((totals, far_sum, pieces))
    far_sum = swap(far_sum, 2)
    x_grad = (
        proj_low.astype(single)
        + near_own.astype(single)
        + near_one.astype(single)
        + far_sum.astype(single)
    )

    pieces = lax.all_to_all(pieces, everyone, 0, 0, tiled=True)
    if in_place:
        shard_qkv = join_groups(pieces, passes)
    else:
        pieces = pieces.reshape(devices // passes, passes, shard, 3, group).astype(single).sum(axis=0)
        shard_qkv = pieces.transpose(1, 2, 0, 3).reshape(w_qkv.shape)

    for axis, distance in steps[1:]:
        totals = totals + exchange(totals, axis, distance)
    biases = totals[:passes, : 3 * group].reshape(passes, 3, group)
    pass_grad = lax.dynamic_slice_in_dim(totals, passes + me, 1, 0)
    up_rows = hidden // width
    return (
        out_rows[None],
        x_grad[None],
        shard_qkv,
        biases[:, 0].reshape(-1),
        biases[:, 2].reshape(-1),
        shard_out,
        totals[16],
        totals[8],
        totals[9],
        totals[17],
        totals[18],
        shard_up,
        totals[20 : 20 + up_rows].reshape(-1),
        shard_down,
        totals[19],
        pass_grad,
    )


def solution(mesh):
    placed = (
        P("pass", "seq", None),
        P("seq", None),
        P("pass", "seq", None),
        P(),
        P(),
        P(),
        P(("seq", "pass"), None),
        P(),
        P(),
        P(("seq", "pass"), None),
        P(),
        P(),
        P(),
        P(("seq", "pass"), None),
        P(),
        P(("seq", "pass"), None),
        P(),
    )
    return jax.shard_map(
        per_device,
        mesh=mesh,
        in_specs=placed,
        out_specs=(
            P("pass", "seq", None),
            P("pass", "seq", None),
            P(("seq", "pass"), None),
            P(),
            P(),
            P(("seq", "pass"), None),
            P(),
            P(),
            P(),
            P(),
            P(),
            P(("seq", "pass"), None),
            P(),
            P(("seq", "pass"), None),
            P(),
            P("pass", None),
        ),
        check_vma=False,
    )
```

```python
import functools

import jax
import jax.numpy as jnp
from jax import lax
from jax.experimental import pallas as pl
from jax.experimental.pallas import tpu as pltpu
from jax.sharding import PartitionSpec as P

HEADS = 12
HEAD_DIM = 64
LANES = 128
NORM_EPS = 1e-05
MASKED = -1e30
BIAS_COL = 64
STAT_COL = 65
DELTA_COL = 64

bfloat = jnp.bfloat16
single = jnp.float32


def in_hbm(shape, dtype):
    return pltpu.HBM(shape, dtype)


def from_hbm(values):
    return [pltpu.with_memory_space_constraint(value, pltpu.HBM) for value in values]


def dot_nn(a, b):
    return jnp.dot(a, b, preferred_element_type=single)


def dot_nt(a, b):
    return lax.dot_general(a, b, (((1,), (1,)), ((), ())), preferred_element_type=single)


def dot_tn(a, b):
    return lax.dot_general(a, b, (((0,), (0,)), ((), ())), preferred_element_type=single)


def three_parts(value):
    first = value.astype(bfloat).astype(single)
    rest = value - first
    second = rest.astype(bfloat).astype(single)
    return first, second, rest - second


def with_columns(base, start, columns):
    lane = lax.broadcasted_iota(jnp.int32, base.shape, 1)
    for offset, column in enumerate(columns):
        base = jnp.where(lane == start + offset, column, base)
    return base


def norm_parts(values):
    center = values - jnp.mean(values, axis=-1, keepdims=True)
    inverse = lax.rsqrt(jnp.mean(center * center, axis=-1, keepdims=True) + NORM_EPS)
    return center * inverse, inverse


def norm_back(grad, gain, normed, inverse):
    scaled = grad * gain
    mean_one = jnp.mean(scaled, axis=-1, keepdims=True)
    mean_two = jnp.mean(scaled * normed, axis=-1, keepdims=True)
    return inverse * (scaled - mean_one - normed * mean_two)


def head_slab(packed, index):
    low = (index // 2) * LANES
    slab = packed[:, low : low + LANES]
    if index % 2:
        slab = pltpu.roll(slab, HEAD_DIM, axis=1)
    return slab


def pack_heads(slabs):
    packed = []
    lane = lax.broadcasted_iota(jnp.int32, slabs[0].shape, 1)
    for index in range(0, len(slabs), 2):
        if index + 1 < len(slabs):
            other = pltpu.roll(slabs[index + 1], HEAD_DIM, axis=1)
            packed.append(jnp.where(lane < HEAD_DIM, slabs[index], other))
        else:
            packed.append(slabs[index])
    width = len(slabs) * HEAD_DIM
    return jnp.concatenate(packed, axis=1)[:, :width]


def project_kernel(heads, count, me_ref, *refs):
    pieces = refs[:count]
    pass_ref, gain_ref, shift_ref, weight_ref, bias_ref, depth_ref = refs[count : count + 6]
    q_ref, k_ref, v_ref, stats_ref = refs[-4:]
    slot = pl.program_id(0)
    pass_index = me_ref[1 + slot]
    pass_row = pass_ref[pl.ds(pass_index, 1), :]
    rows = pieces[0][...]
    for index in range(1, count):
        rows = jnp.where(slot == index, pieces[index][...], rows)
    rows = rows.astype(single) + pass_row
    mean = jnp.mean(rows, axis=-1, keepdims=True)
    center = rows - mean
    inverse = lax.rsqrt(jnp.mean(center * center, axis=-1, keepdims=True) + NORM_EPS)
    lane = lax.broadcasted_iota(jnp.int32, stats_ref.shape, 1)
    stats_ref[...] = jnp.where(lane == 0, inverse, -mean * inverse)
    low = (center * inverse * gain_ref[...] + shift_ref[...]).astype(bfloat)
    projected = dot_nn(low, weight_ref[...]) + bias_ref[...]
    lane = lax.broadcasted_iota(jnp.int32, (low.shape[0], LANES), 1)
    inside = lane < HEAD_DIM
    depth_bias = jnp.where(pass_index < depth_ref[...], 0.0, MASKED)
    q_rest = jnp.where(lane == BIAS_COL, 1.0, 0.0)
    k_rest = jnp.where(
        lane == BIAS_COL, depth_bias, jnp.where((lane >= STAT_COL) & (lane < STAT_COL + 3), 1.0, 0.0)
    )
    v_rest = jnp.where((lane >= DELTA_COL) & (lane < DELTA_COL + 3), 1.0, 0.0)
    for head in range(heads):
        q_part = head_slab(projected, head).astype(bfloat).astype(single) * (HEAD_DIM**-0.5)
        q_ref[head] = jnp.where(inside, q_part, q_rest).astype(bfloat)
        k_ref[head] = jnp.where(inside, head_slab(projected, heads + head), k_rest).astype(bfloat)
        v_ref[head] = jnp.where(inside, head_slab(projected, 2 * heads + head), v_rest).astype(bfloat)


def project(order, pieces, passes, pass_emb, gain, shift, weight, bias, depth, previous):
    count = len(pieces)
    length, width = pieces[0].shape
    heads = weight.shape[1] // (3 * HEAD_DIM)
    block = min(512, length)
    steps = length // block

    def piece_spec(index):
        def where(slot, step, order_ref):
            return (jnp.where(slot == index, step, jnp.where(slot < index, 0, steps - 1)), 0)

        return pl.BlockSpec((block, width), where)

    def whole(shape):
        return pl.BlockSpec(shape, lambda slot, step, order_ref: (0,) * len(shape))

    out_spec = pl.BlockSpec(
        (heads, pl.Squeezed(), block, LANES),
        lambda slot, step, order_ref: (0, order_ref[1 + slot], step, 0),
    )
    shape = in_hbm((heads, passes, length, LANES), bfloat)
    stats_spec = pl.BlockSpec(
        (pl.Squeezed(), block, 2), lambda slot, step, order_ref: (order_ref[1 + slot], step, 0)
    )
    in_specs = [piece_spec(index) for index in range(count)] + [
        whole(pass_emb.shape),
        whole(gain.shape),
        whole(shift.shape),
        whole(weight.shape),
        whole(bias.shape),
        pl.BlockSpec((block, 1), lambda slot, step, order_ref: (step, 0)),
    ]
    operands = [*pieces, pass_emb, gain, shift, weight, bias, depth]
    aliases = {}
    if previous is not None:
        aliases = {1 + len(operands) + index: index for index in range(4)}
        in_specs += [pl.BlockSpec(memory_space=pl.ANY)] * 4
        operands += list(previous)
    return pl.pallas_call(
        functools.partial(project_kernel, heads, count),
        grid_spec=pltpu.PrefetchScalarGridSpec(
            num_scalar_prefetch=1,
            grid=(count, steps),
            in_specs=in_specs,
            out_specs=[out_spec] * 3 + [stats_spec],
        ),
        out_shape=[shape] * 3 + [in_hbm((passes, length, 2), single)],
        input_output_aliases=aliases,
        compiler_params=pltpu.CompilerParams(vmem_limit_bytes=40 << 20),
        cost_estimate=pl.CostEstimate(flops=8 << 30, transcendentals=0, bytes_accessed=12 << 20),
        name="project",
    )(order, *operands)


def attend_kernel(passes, block, first, last, me_ref, q_ref, k_ref, v_ref, *refs):
    out_refs, q_next_ref, held = refs[:passes], refs[passes], refs[passes + 1]
    heads = q_ref.shape[0]
    step = pl.program_id(0)
    row = lax.broadcasted_iota(jnp.int32, (block, block), 0)
    col = lax.broadcasted_iota(jnp.int32, (block, block), 1)
    causal = col <= row

    def one_head(head, count):
        kept = [[] for _ in range(passes)]
        highest = [None] * passes
        for key_pass in range(passes):
            span = passes - key_pass
            query = q_ref[head, key_pass:passes].reshape(span * block, LANES)
            for tile in range(count):
                both = dot_nt(query, k_ref[head, key_pass, tile * block : (tile + 1) * block, :])
                for query_pass in range(key_pass, passes):
                    start = (query_pass - key_pass) * block
                    scores = both[start : start + block]
                    if tile == count - 1:
                        scores = jnp.where(causal, scores, MASKED)
                    kept[query_pass].append(scores)
                    for lane in range(0, block, LANES):
                        part = scores[:, lane : lane + LANES]
                        old = highest[query_pass]
                        highest[query_pass] = part if old is None else jnp.maximum(old, part)
        highest = [jnp.max(part, axis=-1, keepdims=True) for part in highest]
        for query_pass in range(passes):
            total = None
            for index, scores in enumerate(kept[query_pass]):
                key_pass, tile = divmod(index, count)
                weights = jnp.exp(scores - highest[query_pass]).astype(bfloat)
                term = dot_nn(weights, v_ref[head, key_pass, tile * block : (tile + 1) * block, :])
                total = term if total is None else total + term
            row_sum = total[:, DELTA_COL : DELTA_COL + 1]
            log_sum = highest[query_pass] + jnp.log(row_sum)
            q_next_ref[head, query_pass] = with_columns(
                q_ref[head, query_pass].astype(single), STAT_COL, three_parts(-log_sum)
            ).astype(bfloat)
            held[head, query_pass] = total * (1.0 / row_sum)

    for index in range(first, last):

        @pl.when(step == index - first)
        def _():
            lax.fori_loop(0, heads, lambda head, _: (one_head(head, index + 1), 0)[1], 0)

    for slot in range(passes):
        query_pass = jnp.bitwise_xor(me_ref[0], slot)
        out_refs[slot][...] = pack_heads([held[head, query_pass] for head in range(heads)]).astype(bfloat)


def attend(me, queries, keys, values, half):
    heads, passes, length, _ = queries.shape
    block = min(256, length // 2)
    count = length // 2 // block
    first, last = half * count, (half + 1) * count
    seen = pl.BlockSpec(
        (heads, passes, last * block, LANES),
        lambda step, me_ref: (0, 0, 0, 0),
        pipeline_mode=pl.Buffered(1),
    )
    part = pl.BlockSpec((heads, passes, block, LANES), lambda step, me_ref: (0, 0, first + step, 0))
    part_out = pl.BlockSpec((heads, passes, block, LANES), lambda step, me_ref: (0, 0, step, 0))
    packed = heads * HEAD_DIM
    *outs, queries = pl.pallas_call(
        functools.partial(attend_kernel, passes, block, first, last),
        grid_spec=pltpu.PrefetchScalarGridSpec(
            num_scalar_prefetch=1,
            grid=(count,),
            in_specs=[part, seen, seen],
            out_specs=[pl.BlockSpec((block, packed), lambda step, me_ref: (step, 0))] * passes + [part_out],
            scratch_shapes=[pltpu.VMEM((heads, passes, block, LANES), single)],
        ),
        out_shape=[in_hbm((length // 2, packed), bfloat)] * passes
        + [in_hbm((heads, passes, length // 2, LANES), bfloat)],
        compiler_params=pltpu.CompilerParams(vmem_limit_bytes=48 << 20),
        cost_estimate=pl.CostEstimate(
            flops=(10 + 20 * half) << 30,
            transcendentals=heads * (1 + 2 * half) * length * length,
            bytes_accessed=12 << 20,
        ),
        name="attend",
    )(me, *from_hbm((queries, keys, values)))
    return outs, queries


def attend_back_kernel(passes, block, me_ref, *refs):
    q_refs, (k_ref, v_ref), refs = refs[:2], refs[2:4], refs[4:]
    out_refs = refs[:passes], refs[passes : 2 * passes]
    grad_refs = refs[2 * passes : 3 * passes], refs[3 * passes : 4 * passes]
    all_ref, key_acc, value_acc, grad_held, query_held = refs[4 * passes :]
    heads = k_ref.shape[0]
    blocks = k_ref.shape[2] // block
    step = pl.program_id(0)
    me = me_ref[0]
    row = lax.broadcasted_iota(jnp.int32, (block, block), 0)
    col = lax.broadcasted_iota(jnp.int32, (block, block), 1)
    causal = row <= col
    inside = lax.broadcasted_iota(jnp.int32, (block, LANES), 1) < HEAD_DIM
    padded = ((heads * HEAD_DIM + LANES - 1) // LANES) * LANES

    @pl.when(step == 0)
    def _():
        key_acc[...] = jnp.zeros(key_acc.shape, single)
        value_acc[...] = jnp.zeros(value_acc.shape, single)

    def prepare(half):
        for slot in range(passes):
            query_pass = jnp.bitwise_xor(me, slot)
            grad = grad_refs[half][slot][...].astype(single)
            out = out_refs[half][slot][...].astype(single)
            if padded > heads * HEAD_DIM:
                tail = jnp.zeros((block, padded - heads * HEAD_DIM), single)
                grad = jnp.concatenate([grad, tail], axis=1)
                out = jnp.concatenate([out, tail], axis=1)
            product = grad * out
            for head in range(heads):
                delta = jnp.sum(
                    jnp.where(inside, head_slab(product, head), 0.0), axis=-1, keepdims=True
                )
                base = jnp.where(inside, head_slab(grad, head), 0.0)
                grad_held[head, query_pass] = with_columns(base, DELTA_COL, three_parts(-delta)).astype(bfloat)

    def one_head(head, count, q_ref):
        query_sums = [None] * passes
        for key_pass in range(passes):
            span = passes - key_pass
            query = q_ref[head, key_pass:passes].reshape(span * block, LANES)
            grad = grad_held[head, key_pass:passes].reshape(span * block, LANES)
            for tile in range(count):
                window = slice(tile * block, (tile + 1) * block)
                key = k_ref[head, key_pass, window, :]
                value = v_ref[head, key_pass, window, :]
                prob = jnp.exp(dot_nt(key, query))
                if tile == count - 1:
                    prob = jnp.where(jnp.concatenate([causal] * span, axis=1), prob, 0.0)
                value_acc[head, key_pass, window, :] += dot_nn(prob.astype(bfloat), grad)
                score_grad = (prob * dot_nt(value, grad)).astype(bfloat)
                key_acc[head, key_pass, window, :] += dot_nn(score_grad, query)
                term = dot_tn(key, score_grad)
                for query_pass in range(key_pass, passes):
                    start = (query_pass - key_pass) * block
                    part = term[:, start : start + block]
                    old = query_sums[query_pass]
                    query_sums[query_pass] = part if old is None else old + part
        for query_pass in range(passes):
            query_held[head, query_pass] = query_sums[query_pass].T * (HEAD_DIM**-0.5)

    for index in range(blocks):

        @pl.when(step == blocks - 1 - index)
        def _():
            half = index // (blocks // 2)
            prepare(half)
            lax.fori_loop(0, heads, lambda head, _: (one_head(head, index + 1, q_refs[half]), 0)[1], 0)
            window = slice(index * block, (index + 1) * block)
            for query_pass in range(passes):
                slabs = [query_held[head, query_pass] for head in range(heads)]
                slabs += [key_acc[head, query_pass, window, :] for head in range(heads)]
                slabs += [value_acc[head, query_pass, window, :] for head in range(heads)]
                all_ref[query_pass] = pack_heads(slabs).astype(bfloat)


def attend_back(me, queries, keys, values, outs, grads):
    heads, passes, length, _ = keys.shape
    block = min(256, length // 2)
    count = length // 2 // block
    packed = heads * HEAD_DIM

    def spot(half):
        return lambda step: jnp.clip(2 * count - 1 - step - half * count, 0, count - 1)

    def query_spec(half):
        return pl.BlockSpec((heads, passes, block, LANES), lambda step, me_ref: (0, 0, spot(half)(step), 0))

    def rows_spec(half):
        return pl.BlockSpec((block, packed), lambda step, me_ref: (spot(half)(step), 0))

    whole = pl.BlockSpec(keys.shape, lambda step, me_ref: (0, 0, 0, 0), pipeline_mode=pl.Buffered(1))
    rows_specs = [rows_spec(half) for half in range(2) for _ in range(passes)]
    return pl.pallas_call(
        functools.partial(attend_back_kernel, passes, block),
        grid_spec=pltpu.PrefetchScalarGridSpec(
            num_scalar_prefetch=1,
            grid=(2 * count,),
            in_specs=[query_spec(0), query_spec(1), whole, whole] + rows_specs * 2,
            out_specs=pl.BlockSpec(
                (passes, block, 3 * packed), lambda step, me_ref: (0, 2 * count - 1 - step, 0)
            ),
            scratch_shapes=[
                pltpu.VMEM(keys.shape, single),
                pltpu.VMEM(keys.shape, single),
                pltpu.VMEM((heads, passes, block, LANES), bfloat),
                pltpu.VMEM((heads, passes, block, LANES), single),
            ],
        ),
        out_shape=in_hbm((passes, length, 3 * packed), bfloat),
        compiler_params=pltpu.CompilerParams(vmem_limit_bytes=58 << 20),
        cost_estimate=pl.CostEstimate(
            flops=300 << 30, transcendentals=heads * 6 * length * length, bytes_accessed=20 << 20
        ),
        name="attend_back",
    )(me, *from_hbm((*queries, keys, values, *outs[0], *outs[1], *grads[0], *grads[1])))


def middle_kernel(groups, downs, shard, begins, me_ref, *refs):
    parts = refs[:groups]
    x_ref, cot_ref, pass_ref, out_bias_ref, gain_ref, shift_ref, down_bias_ref, up_bias_ref, w_out_ref, w_up_ref = refs[
        groups : groups + 10
    ]
    refs = refs[groups + 10 :]
    down_refs = refs[:downs]
    last_sums_ref = None if begins else refs[downs]
    outs, scratch = refs[-11 - groups : -5 - groups], refs[-5:]
    rows_ref, normed_ref, active_ref, upper_ref, proj_ref, sums_ref = outs
    grads = refs[-5 - groups : -5]
    normed_held, inverse_held, total_held, back_held, w_down_held = scratch
    me = me_ref[0]
    width = x_ref.shape[1]
    packed = width // groups
    step = pl.program_id(0)

    def group_window(slot):
        start = pl.multiple_of(jnp.bitwise_xor(me, slot) * packed, packed)
        return pl.ds(start, packed)

    def column_sum(values):
        return jnp.sum(values, axis=0, keepdims=True)

    @pl.when(step == 0)
    def _():
        sums_ref[...] = jnp.zeros(sums_ref.shape, single) if begins else last_sums_ref[...]
        mixed = x_ref[...].astype(single) + pass_ref[...] + out_bias_ref[...]
        for slot in range(groups):
            mixed += dot_nn(parts[slot][...], w_out_ref[group_window(slot), :])
        normed, inverse = norm_parts(mixed)
        normed_ref[...] = (normed * gain_ref[...] + shift_ref[...]).astype(bfloat)
        normed_held[...] = normed
        inverse_held[...] = jnp.broadcast_to(inverse, inverse_held.shape)
        total_held[...] = mixed + down_bias_ref[...]
        back_held[...] = jnp.zeros(back_held.shape, single)

    if shard:
        for start in range(0, down_refs[0].shape[0], 2 * shard):
            blocks = [ref[start : start + 2 * shard, :].astype(single) for ref in down_refs]
            pieces = [block[side * shard : (side + 1) * shard] for side in range(2) for block in blocks]
            w_down_held[start * downs : (start + 2 * shard) * downs, :] = jnp.concatenate(
                pieces, axis=0
            ).astype(bfloat)
        w_down_ref = w_down_held
    else:
        w_down_ref = down_refs[0]

    upper = dot_nn(normed_ref[...], w_up_ref[...]) + up_bias_ref[...]
    below = 0.5 + 0.5 * lax.erf(upper * (0.5**0.5))
    density = jnp.exp(-0.5 * upper * upper) * 0.3989422804014327
    active = (upper * below).astype(bfloat)
    active_ref[...] = active
    total_held[...] += dot_nn(active, w_down_ref[...])
    upper_low = (dot_nt(cot_ref[...], w_down_ref[...]) * (below + upper * density)).astype(bfloat)
    upper_ref[...] = upper_low
    sums_ref[pl.ds(4 + step, 1), :] += column_sum(upper_low.astype(single))
    back_held[...] += dot_nt(upper_low, w_up_ref[...])

    @pl.when(step == pl.num_programs(0) - 1)
    def _():
        rows_ref[...] = total_held[...].astype(bfloat)
        out_grad = cot_ref[...].astype(single)
        normed, back = normed_held[...], back_held[...]
        mixed_grad = out_grad + norm_back(back, gain_ref[...], normed, inverse_held[:, 0:1])
        proj_low = mixed_grad.astype(bfloat)
        proj_ref[...] = proj_low
        for slot in range(groups):
            grads[slot][...] = dot_nt(proj_low, w_out_ref[group_window(slot), :]).astype(bfloat)
        sums_ref[0:1, :] += column_sum(mixed_grad)
        sums_ref[1:2, :] += column_sum(back * normed)
        sums_ref[2:3, :] += column_sum(back)
        sums_ref[3:4, :] += column_sum(out_grad)


def middle(
    me,
    parts,
    x_own,
    cot,
    pass_row,
    out_bias,
    gain,
    shift,
    up_bias,
    down_bias,
    gathered,
    w_down,
    shard,
    half,
    previous,
):
    length, width = x_own.shape
    hidden = up_bias.shape[1]
    chunks = hidden // width
    groups = len(parts)
    packed = width // groups
    block = length // 2

    def rows(size):
        return pl.BlockSpec((block, size), lambda step, me_ref: (half, 0))

    def half_rows(size):
        return pl.BlockSpec((block, size), lambda step, me_ref: (0, 0))

    def whole(shape):
        return pl.BlockSpec(shape, lambda step, me_ref: (0, 0), pipeline_mode=pl.Buffered(1))

    def fixed(shape):
        return pl.BlockSpec(shape, lambda step, me_ref: (0, 0))

    by_chunk = pl.BlockSpec((block, width), lambda step, me_ref: (half, step))
    sums_shape = ((4 + chunks + 7) // 8 * 8, width)
    square = (width, width)
    small = (pass_row, out_bias, gain, shift, down_bias)
    if w_down is None:
        downs = chunks

        def down_spec(col):
            return pl.BlockSpec((width // chunks, width), lambda step, me_ref: (step, 1 + chunks + col))

        down_specs = [down_spec(col) for col in range(chunks)]
        down = [gathered] * chunks
    else:
        downs = 1
        down_specs = [pl.BlockSpec(square, lambda step, me_ref: (step, 0))]
        down = [w_down]
        shard = None
    in_specs = (
        [half_rows(packed)] * groups
        + [rows(width), rows(width)]
        + [whole(operand.shape) for operand in small]
        + [pl.BlockSpec((1, width), lambda step, me_ref: (0, step))]
        + [whole(square), pl.BlockSpec(square, lambda step, me_ref: (0, 1 + step))]
        + down_specs
    )
    operands = [*from_hbm([*parts, x_own, cot]), *small, up_bias, *from_hbm([gathered] * 2 + down)]
    aliases = {}
    if previous is not None:
        in_specs += [fixed(sums_shape)] + [pl.BlockSpec(memory_space=pl.ANY)] * 5
        aliases = {2 + len(operands) + index: index for index in range(5)}
        operands += [previous[5], *previous[:5]]
    results = pl.pallas_call(
        functools.partial(middle_kernel, groups, downs, shard, previous is None),
        grid_spec=pltpu.PrefetchScalarGridSpec(
            num_scalar_prefetch=1,
            grid=(chunks,),
            in_specs=in_specs,
            out_specs=[rows(width), rows(width), by_chunk, by_chunk, rows(width), fixed(sums_shape)]
            + [half_rows(packed)] * groups,
            scratch_shapes=[
                pltpu.VMEM((block, width), single),
                pltpu.VMEM((block, LANES), single),
                pltpu.VMEM((block, width), single),
                pltpu.VMEM((block, width), single),
                pltpu.VMEM(square, bfloat),
            ],
        ),
        out_shape=[
            in_hbm((length, width), bfloat),
            in_hbm((length, width), bfloat),
            in_hbm((length, hidden), bfloat),
            in_hbm((length, hidden), bfloat),
            in_hbm((length, width), bfloat),
            jax.ShapeDtypeStruct(sums_shape, single),
        ]
        + [in_hbm((length // 2, packed), bfloat)] * groups,
        input_output_aliases=aliases,
        compiler_params=pltpu.CompilerParams(vmem_limit_bytes=56 << 20),
        cost_estimate=pl.CostEstimate(
            flops=20 << 30, transcendentals=length * hidden, bytes_accessed=24 << 20
        ),
        name="middle",
    )(me, *operands)
    return results[:6], results[6:]


def weight_grad_kernel(groups, chunks, shard, me_ref, *refs):
    late_loads = refs[: 2 * groups + 1]
    normed_ref, cot_ref, upper_ref, active_ref, out_ref, staged, staged_down, sent, sent_down = refs[
        2 * groups + 1 : 2 * groups + 10
    ]
    loaded, loads = refs[2 * groups + 10 : -1], refs[-1]
    early, late, proj_ref = loaded[:groups], loaded[groups : 2 * groups], loaded[-1]
    length, width = normed_ref.shape
    middle_row = length // 2
    packed = width // groups
    rows = width // chunks
    step = pl.program_id(0)

    def columns_copy(index):
        start = pl.multiple_of(index * width, width)
        return pltpu.make_async_copy(staged.at[index], out_ref.at[:, pl.ds(start, width)], sent.at[index])

    def down_copy(index):
        if shard:
            start = pl.multiple_of(index * rows, rows)
            target = out_ref.at[pl.ds(start, rows), pl.ds((1 + chunks) * width, chunks * width)]
        else:
            start = pl.multiple_of((1 + chunks + index) * width, width)
            target = out_ref.at[:, pl.ds(start, width)]
        return pltpu.make_async_copy(staged_down.at[index], target, sent_down.at[index])

    def load(index):
        return pltpu.make_async_copy(late_loads[index], loaded[index], loads.at[index])

    @pl.when(step == 0)
    def _():
        for index in range(2 * groups + 1):
            load(index).start()

    @pl.when(step < chunks)
    def _():
        staged[step + 1] = dot_tn(normed_ref[...], upper_ref[...]).astype(bfloat)
        down = dot_tn(active_ref[...], cot_ref[...])
        if shard:
            for start in range(0, rows, 2 * shard):
                for chunk in range(chunks):
                    first = start * chunks + chunk * shard
                    second = first + chunks * shard
                    staged_down[step, start : start + 2 * shard, chunk * width : (chunk + 1) * width] = (
                        jnp.concatenate(
                            [down[first : first + shard], down[second : second + shard]], axis=0
                        ).astype(bfloat)
                    )
        else:
            staged_down[step] = down.astype(bfloat)
        columns_copy(step + 1).start()
        down_copy(step).start()

    @pl.when(step == chunks)
    def _():
        for index in range(2 * groups + 1):
            load(index).wait()
        for slot in range(groups):
            start = pl.multiple_of(jnp.bitwise_xor(me_ref[0], slot) * packed, packed)
            staged[0, pl.ds(start, packed), :] = (
                dot_tn(early[slot][...], proj_ref[:middle_row, :])
                + dot_tn(late[slot][...], proj_ref[middle_row:, :])
            ).astype(bfloat)
        columns_copy(0).start()
        for index in range(1 + chunks):
            columns_copy(index).wait()
        for index in range(chunks):
            down_copy(index).wait()


def weight_grads(me, early, late, proj, normed, cot, upper, active, shard):
    length, width = proj.shape
    hidden = upper.shape[1]
    chunks = hidden // width
    groups = len(early)
    parts = [*early, *late]

    def whole(shape):
        return pl.BlockSpec(shape, lambda step, me_ref: (0, 0), pipeline_mode=pl.Buffered(1))

    by_chunk = pl.BlockSpec((length, width), lambda step, me_ref: (0, jnp.minimum(step, chunks - 1)))
    late_loads = [*parts, proj]
    down_shape = (width // chunks, chunks * width) if shard else (width, width)
    return pl.pallas_call(
        functools.partial(weight_grad_kernel, groups, chunks, shard),
        grid_spec=pltpu.PrefetchScalarGridSpec(
            num_scalar_prefetch=1,
            grid=(1 + chunks,),
            in_specs=[pl.BlockSpec(memory_space=pl.ANY)] * len(late_loads)
            + [whole(proj.shape)] * 2
            + [by_chunk] * 2,
            out_specs=pl.BlockSpec(memory_space=pl.ANY),
            scratch_shapes=[
                pltpu.VMEM((1 + chunks, width, width), bfloat),
                pltpu.VMEM((chunks, *down_shape), bfloat),
                pltpu.SemaphoreType.DMA((1 + chunks,)),
                pltpu.SemaphoreType.DMA((chunks,)),
            ]
            + [pltpu.VMEM(operand.shape, bfloat) for operand in late_loads]
            + [pltpu.SemaphoreType.DMA((len(late_loads),))],
        ),
        out_shape=in_hbm((width, width + 2 * hidden), bfloat),
        compiler_params=pltpu.CompilerParams(vmem_limit_bytes=56 << 20),
        cost_estimate=pl.CostEstimate(flops=20 << 30, transcendentals=0, bytes_accessed=32 << 20),
        name="weight_grads",
    )(me, *from_hbm([*parts, proj, normed, cot, upper, active]))


def split_weights_kernel(chunks, in_ref, out_ref, up_ref, down_ref):
    shard, width = out_ref.shape
    out_ref[...] = in_ref[:, :width].astype(single)
    up_ref[...] = in_ref[:, width : (1 + chunks) * width].astype(single)
    for chunk in range(chunks):
        start = (1 + chunks + chunk) * width
        down_ref[chunk * shard : (chunk + 1) * shard, :] = in_ref[:, start : start + width].astype(single)


def split_weights(reduced, width):
    shard, columns = reduced.shape
    hidden = (columns - width) // 2
    struct = jax.ShapeDtypeStruct
    return pl.pallas_call(
        functools.partial(split_weights_kernel, hidden // width),
        out_shape=[
            struct((shard, width), single),
            struct((shard, hidden), single),
            struct((shard * hidden // width, width), single),
        ],
        name="split_weights",
    )(reduced)


def join_groups_kernel(passes, in_ref, out_ref):
    sequences = in_ref.shape[0] // passes
    packed = in_ref.shape[2]
    group = packed // 3
    sums = []
    for index in range(passes):
        total = in_ref[index].astype(single)
        for sequence in range(1, sequences):
            total += in_ref[sequence * passes + index].astype(single)
        sums.append(total)
    width = passes * group
    for part in range(3):
        out_ref[:, part * width : (part + 1) * width] = jnp.concatenate(
            [total[:, part * group : (part + 1) * group] for total in sums], axis=1
        )


def join_groups(pieces, passes):
    _, shard, packed = pieces.shape
    return pl.pallas_call(
        functools.partial(join_groups_kernel, passes),
        out_shape=jax.ShapeDtypeStruct((shard, passes * packed), single),
        name="join_groups",
    )(pieces)


def project_back_kernel(count, passes, me_ref, *refs):
    pieces = refs[:count]
    pass_ref, gain_ref, shift_ref, weight_ref, grad_ref, stats_ref, last_sums_ref = refs[count : count + 7]
    *rows_refs, weight_low_ref, sums_ref, held, weight_grad_ref = refs[count + 7 :]
    slot = pl.program_id(0)
    step = pl.program_id(1)
    pass_index = me_ref[1 + slot]
    packed = grad_ref.shape[1]

    @pl.when((slot == 0) & (step == 0))
    def _():
        weight_grad_ref[...] = jnp.zeros(weight_grad_ref.shape, single)
        sums_ref[...] = jnp.zeros(sums_ref.shape, single)
        sums_ref[16:, :] = last_sums_ref[...]
        sums_ref[pl.ds(passes + me_ref[0], 1), :] = last_sums_ref[0:1, :]

    def column_sum(values):
        return jnp.sum(values, axis=0, keepdims=True)

    rows = pieces[0][...]
    for index in range(1, count):
        rows = jnp.where(slot == index, pieces[index][...], rows)
    stats = stats_ref[...]
    inverse = stats[:, 0:1]
    normed = (rows.astype(single) + pass_ref[pl.ds(pass_index, 1), :]) * inverse + stats[:, 1:2]
    low = (normed * gain_ref[...] + shift_ref[...]).astype(bfloat)
    grad = grad_ref[...]
    back = dot_nt(grad, weight_ref[...])
    weight_grad_ref[...] += dot_tn(low, grad)
    part = norm_back(back, gain_ref[...], normed, inverse)
    held[...] = part.astype(bfloat)
    sums_ref[pl.ds(me_ref[0], 1), :packed] += column_sum(grad.astype(single))
    sums_ref[pl.ds(passes + pass_index, 1), :] += column_sum(part)
    sums_ref[8:9, :] += column_sum(back * normed)
    sums_ref[9:10, :] += column_sum(back)
    for index in range(count):

        @pl.when(slot == index)
        def _():
            rows_refs[index][...] = held[...]

    @pl.when((slot == count - 1) & (step == pl.num_programs(1) - 1))
    def _():
        weight_low_ref[...] = weight_grad_ref[...].astype(bfloat)


def project_back(order, pieces, pass_emb, gain, shift, weight, grads, stats, last_sums):
    count = len(pieces)
    length, width = pieces[0].shape
    passes, _, packed = grads.shape
    block = min(512, length)
    steps = length // block
    sums_shape = (16 + last_sums.shape[0], width)

    def piece_spec(index):
        def where(slot, step, order_ref):
            return (jnp.where(slot == index, step, jnp.where(slot < index, 0, steps - 1)), 0)

        return pl.BlockSpec((block, width), where)

    def whole(shape):
        return pl.BlockSpec(shape, lambda slot, step, order_ref: (0,) * len(shape))

    def by_pass(size):
        return pl.BlockSpec(
            (pl.Squeezed(), block, size), lambda slot, step, order_ref: (order_ref[1 + slot], step, 0)
        )

    small = [pass_emb, gain, shift]
    return pl.pallas_call(
        functools.partial(project_back_kernel, count, passes),
        grid_spec=pltpu.PrefetchScalarGridSpec(
            num_scalar_prefetch=1,
            grid=(count, steps),
            in_specs=[piece_spec(index) for index in range(count)]
            + [whole(operand.shape) for operand in small]
            + [whole(weight.shape), by_pass(packed), by_pass(2), whole(last_sums.shape)],
            out_specs=[piece_spec(index) for index in range(count)]
            + [whole((width, packed)), whole(sums_shape)],
            scratch_shapes=[pltpu.VMEM((block, width), bfloat), pltpu.VMEM((width, packed), single)],
        ),
        out_shape=[in_hbm((length, width), bfloat)] * count
        + [jax.ShapeDtypeStruct((width, packed), bfloat), jax.ShapeDtypeStruct(sums_shape, single)],
        compiler_params=pltpu.CompilerParams(vmem_limit_bytes=48 << 20),
        cost_estimate=pl.CostEstimate(flops=16 << 30, transcendentals=0, bytes_accessed=20 << 20),
        name="project_back",
    )(order, *from_hbm(pieces), *small, *from_hbm([weight, grads, stats]), last_sums)


def exchange(value, axis, distance):
    return lax.ppermute(value, axis, [(k, k ^ distance) for k in range(lax.axis_size(axis))])


def summing_steps():
    passes, sequences = lax.axis_size("pass"), lax.axis_size("seq")
    steps = [("pass", distance) for distance in (2**power for power in range(1, passes)) if distance < passes]
    steps += [("seq", distance) for distance in (2**power for power in range(sequences)) if distance < sequences]
    return steps + [("pass", 1)]


def per_device(
    x_rows,
    pass_depth,
    cotangent,
    pass_emb,
    ln1_gain,
    ln1_bias,
    w_qkv,
    q_bias,
    v_bias,
    w_out,
    out_bias,
    ln2_gain,
    ln2_bias,
    w_up,
    up_bias,
    w_down,
    down_bias,
):
    everyone = ("seq", "pass")
    _, length, width = x_rows.shape
    hidden = w_up.shape[1]
    passes = lax.axis_size("pass")
    devices = passes * lax.axis_size("seq")
    shard = w_qkv.shape[0]
    group = width // passes
    group_heads = group // HEAD_DIM
    me = lax.axis_index("pass")
    order = jnp.concatenate([me[None], jnp.bitwise_xor(me, jnp.arange(passes))]).astype(jnp.int32)

    def swap(value, distance):
        return exchange(value, "pass", distance)

    x_own = x_rows[0]

    by_group = w_qkv.reshape(shard, 3, passes, group).transpose(2, 0, 1, 3).reshape(passes, shard, 3 * group)
    by_rows = lax.all_to_all(by_group, "pass", 0, 0, tiled=True).reshape(passes * shard, 3 * group)
    by_rows, x_ready = lax.optimization_barrier((by_rows, x_own))
    x_one = swap(x_ready, 1)
    x_two = swap(x_ready, 2)
    w_heads = lax.all_gather(by_rows, "seq", axis=0, tiled=True)

    down_cols = w_down.reshape(passes, shard, width).transpose(1, 0, 2).reshape(shard, hidden)
    own_weights = jnp.concatenate([w_out, w_up, down_cols], axis=1)
    own_weights, x_ready = lax.optimization_barrier((own_weights, x_ready))
    gathered = lax.all_gather(own_weights, everyone, axis=0, tiled=True)
    in_place = shard % 8 == 0
    full_down = None
    if not in_place:
        full_down = (
            gathered[:, width + hidden :]
            .reshape(devices, shard, hidden // width, width)
            .transpose(0, 2, 1, 3)
            .reshape(hidden, width)
        )

    gain_one, shift_one = ln1_gain[None], ln1_bias[None]
    own_q_bias = lax.dynamic_slice_in_dim(q_bias, me * group, group)
    own_v_bias = lax.dynamic_slice_in_dim(v_bias, me * group, group)
    bias_row = jnp.concatenate([own_q_bias, jnp.zeros((group,), single), own_v_bias])[None]
    pad = (-3 * group) % LANES
    w_wide = jnp.pad(w_heads, ((0, 0), (0, pad)))
    bias_wide = jnp.pad(bias_row, ((0, 0), (0, pad)))
    depth = pass_depth.reshape(length, 1)
    near = project(
        order[:3], (x_own, x_one), passes, pass_emb, gain_one, shift_one, w_wide, bias_wide, depth, None
    )
    x_two, near = lax.optimization_barrier((x_two, near))
    x_three = swap(x_two, 1)
    far_order = jnp.concatenate([order[:1], order[3:]])
    queries, keys, values, stats = project(
        far_order, (x_two, x_three), passes, pass_emb, gain_one, shift_one, w_wide, bias_wide, depth, near
    )

    def trade(pieces):
        return list(pieces[:1]) + [swap(pieces[slot], slot) for slot in range(1, passes)]

    pass_row = lax.dynamic_index_in_dim(pass_emb, me, 0, keepdims=True)
    outs, logged = [None, None], [None, None]
    for half in (1, 0):
        outs[half], logged[half] = attend(order[:1], queries, keys, values, half)
    parts = [trade(outs[half]) for half in range(2)]
    results = None
    head_grads = [None, None]
    for half in (1, 0):
        results, head_grads[half] = middle(
            order[:1],
            parts[half],
            x_own,
            cotangent[0],
            pass_row,
            out_bias[None],
            ln2_gain[None],
            ln2_bias[None],
            up_bias[None],
            down_bias[None],
            gathered,
            full_down,
            shard,
            half,
            results,
        )
        head_grads[half] = trade(head_grads[half])
    out_rows, normed_two, activated, upper_low, proj_low, sums = results

    weight_parts = weight_grads(
        order[:1],
        *parts,
        proj_low,
        normed_two,
        cotangent[0],
        upper_low,
        activated,
        shard if in_place else None,
    )
    if not in_place:
        down_part = (
            weight_parts[:, width + hidden :]
            .reshape(width, hidden // width, width)
            .transpose(1, 0, 2)
            .reshape(devices, hidden // width, shard, width)
            .transpose(0, 2, 1, 3)
            .reshape(width, hidden)
        )
        weight_parts = jnp.concatenate([weight_parts[:, : width + hidden], down_part], axis=1)
    weight_parts, logged, head_grads = lax.optimization_barrier((weight_parts, logged, head_grads))
    reduced = lax.psum_scatter(weight_parts, everyone, scatter_dimension=0, tiled=True)
    if in_place:
        shard_out, shard_up, shard_down = split_weights(reduced, width)
    else:
        reduced = reduced.astype(single)
        shard_out = reduced[:, :width]
        shard_up = reduced[:, width : width + hidden]
        shard_down = (
            reduced[:, width + hidden :]
            .reshape(shard, hidden // width, width)
            .transpose(1, 0, 2)
            .reshape(w_down.shape)
        )

    qkv_low = attend_back(order[:1], logged, keys, values, outs, head_grads)
    near_own, near_one, far_two, far_three, head_weight, sums = project_back(
        order, (x_own, x_one, x_two, x_three), pass_emb, gain_one, shift_one, w_heads, qkv_low, stats, sums
    )

    near_one, far_three = swap(near_one, 1), swap(far_three, 1)
    far_sum = (far_two.astype(single) + far_three.astype(single)).astype(bfloat)
    pieces = head_weight.reshape(devices, shard, 3 * group)
    steps = summing_steps()
    totals = sums + exchange(sums, *steps[0])
    totals, far_sum, pieces = lax.optimization_barrier((totals, far_sum, pieces))
    far_sum = swap(far_sum, 2)
    x_grad = (
        proj_low.astype(single)
        + near_own.astype(single)
        + near_one.astype(single)
        + far_sum.astype(single)
    )

    pieces = lax.all_to_all(pieces, everyone, 0, 0, tiled=True)
    if in_place:
        shard_qkv = join_groups(pieces, passes)
    else:
        pieces = pieces.reshape(devices // passes, passes, shard, 3, group).astype(single).sum(axis=0)
        shard_qkv = pieces.transpose(1, 2, 0, 3).reshape(w_qkv.shape)

    for axis, distance in steps[1:]:
        totals = totals + exchange(totals, axis, distance)
    biases = totals[:passes, : 3 * group].reshape(passes, 3, group)
    pass_grad = lax.dynamic_slice_in_dim(totals, passes + me, 1, 0)
    up_rows = hidden // width
    return (
        out_rows[None],
        x_grad[None],
        shard_qkv,
        biases[:, 0].reshape(-1),
        biases[:, 2].reshape(-1),
        shard_out,
        totals[16],
        totals[8],
        totals[9],
        totals[17],
        totals[18],
        shard_up,
        totals[20 : 20 + up_rows].reshape(-1),
        shard_down,
        totals[19],
        pass_grad,
    )


def solution(mesh):
    placed = (
        P("pass", "seq", None),
        P("seq", None),
        P("pass", "seq", None),
        P(),
        P(),
        P(),
        P(("seq", "pass"), None),
        P(),
        P(),
        P(("seq", "pass"), None),
        P(),
        P(),
        P(),
        P(("seq", "pass"), None),
        P(),
        P(("seq", "pass"), None),
        P(),
    )
    return jax.shard_map(
        per_device,
        mesh=mesh,
        in_specs=placed,
        out_specs=(
            P("pass", "seq", None),
            P("pass", "seq", None),
            P(("seq", "pass"), None),
            P(),
            P(),
            P(("seq", "pass"), None),
            P(),
            P(),
            P(),
            P(),
            P(),
            P(("seq", "pass"), None),
            P(),
            P(("seq", "pass"), None),
            P(),
            P("pass", None),
        ),
        check_vma=False,
    )
```

```python
import functools

import jax
import jax.numpy as jnp
from jax import lax
from jax.experimental import pallas as pl
from jax.experimental.pallas import tpu as pltpu
from jax.sharding import PartitionSpec as P

HEADS = 12
HEAD_DIM = 64
LANES = 128
NORM_EPS = 1e-05
MASKED = -1e30
BIAS_COL = 64
STAT_COL = 65
DELTA_COL = 64

bfloat = jnp.bfloat16
single = jnp.float32


def in_hbm(shape, dtype):
    return pltpu.HBM(shape, dtype)


def from_hbm(values):
    return [pltpu.with_memory_space_constraint(value, pltpu.HBM) for value in values]


def dot_nn(a, b):
    return jnp.dot(a, b, preferred_element_type=single)


def dot_nt(a, b):
    return lax.dot_general(a, b, (((1,), (1,)), ((), ())), preferred_element_type=single)


def dot_tn(a, b):
    return lax.dot_general(a, b, (((0,), (0,)), ((), ())), preferred_element_type=single)


def three_parts(value):
    first = value.astype(bfloat).astype(single)
    rest = value - first
    second = rest.astype(bfloat).astype(single)
    return first, second, rest - second


def with_columns(base, start, columns):
    lane = lax.broadcasted_iota(jnp.int32, base.shape, 1)
    for offset, column in enumerate(columns):
        base = jnp.where(lane == start + offset, column, base)
    return base


def norm_parts(values):
    center = values - jnp.mean(values, axis=-1, keepdims=True)
    inverse = lax.rsqrt(jnp.mean(center * center, axis=-1, keepdims=True) + NORM_EPS)
    return center * inverse, inverse


def norm_back(grad, gain, normed, inverse):
    scaled = grad * gain
    mean_one = jnp.mean(scaled, axis=-1, keepdims=True)
    mean_two = jnp.mean(scaled * normed, axis=-1, keepdims=True)
    return inverse * (scaled - mean_one - normed * mean_two)


def head_slab(packed, index):
    low = (index // 2) * LANES
    slab = packed[:, low : low + LANES]
    if index % 2:
        slab = pltpu.roll(slab, HEAD_DIM, axis=1)
    return slab


def pack_heads(slabs):
    packed = []
    lane = lax.broadcasted_iota(jnp.int32, slabs[0].shape, 1)
    for index in range(0, len(slabs), 2):
        if index + 1 < len(slabs):
            other = pltpu.roll(slabs[index + 1], HEAD_DIM, axis=1)
            packed.append(jnp.where(lane < HEAD_DIM, slabs[index], other))
        else:
            packed.append(slabs[index])
    width = len(slabs) * HEAD_DIM
    return jnp.concatenate(packed, axis=1)[:, :width]


def project_kernel(heads, count, me_ref, *refs):
    pieces = refs[:count]
    pass_ref, gain_ref, shift_ref, weight_ref, bias_ref, depth_ref = refs[count : count + 6]
    q_ref, k_ref, v_ref, stats_ref = refs[-4:]
    slot = pl.program_id(0)
    pass_index = me_ref[1 + slot]
    pass_row = pass_ref[pl.ds(pass_index, 1), :]
    rows = pieces[0][...]
    for index in range(1, count):
        rows = jnp.where(slot == index, pieces[index][...], rows)
    rows = rows.astype(single) + pass_row
    mean = jnp.mean(rows, axis=-1, keepdims=True)
    center = rows - mean
    inverse = lax.rsqrt(jnp.mean(center * center, axis=-1, keepdims=True) + NORM_EPS)
    lane = lax.broadcasted_iota(jnp.int32, stats_ref.shape, 1)
    stats_ref[...] = jnp.where(lane == 0, inverse, -mean * inverse)
    low = (center * inverse * gain_ref[...] + shift_ref[...]).astype(bfloat)
    projected = dot_nn(low, weight_ref[...]) + bias_ref[...]
    lane = lax.broadcasted_iota(jnp.int32, (low.shape[0], LANES), 1)
    inside = lane < HEAD_DIM
    depth_bias = jnp.where(pass_index < depth_ref[...], 0.0, MASKED)
    q_rest = jnp.where(lane == BIAS_COL, 1.0, 0.0)
    k_rest = jnp.where(
        lane == BIAS_COL, depth_bias, jnp.where((lane >= STAT_COL) & (lane < STAT_COL + 3), 1.0, 0.0)
    )
    v_rest = jnp.where((lane >= DELTA_COL) & (lane < DELTA_COL + 3), 1.0, 0.0)
    for head in range(heads):
        q_part = head_slab(projected, head).astype(bfloat).astype(single) * (HEAD_DIM**-0.5)
        q_ref[head] = jnp.where(inside, q_part, q_rest).astype(bfloat)
        k_ref[head] = jnp.where(inside, head_slab(projected, heads + head), k_rest).astype(bfloat)
        v_ref[head] = jnp.where(inside, head_slab(projected, 2 * heads + head), v_rest).astype(bfloat)


def project(order, pieces, passes, pass_emb, gain, shift, weight, bias, depth, previous):
    count = len(pieces)
    length, width = pieces[0].shape
    heads = weight.shape[1] // (3 * HEAD_DIM)
    block = min(512, length)
    steps = length // block

    def piece_spec(index):
        def where(slot, step, order_ref):
            return (jnp.where(slot == index, step, jnp.where(slot < index, 0, steps - 1)), 0)

        return pl.BlockSpec((block, width), where)

    def whole(shape):
        return pl.BlockSpec(shape, lambda slot, step, order_ref: (0,) * len(shape))

    out_spec = pl.BlockSpec(
        (heads, pl.Squeezed(), block, LANES),
        lambda slot, step, order_ref: (0, order_ref[1 + slot], step, 0),
    )
    shape = in_hbm((heads, passes, length, LANES), bfloat)
    stats_spec = pl.BlockSpec(
        (pl.Squeezed(), block, 2), lambda slot, step, order_ref: (order_ref[1 + slot], step, 0)
    )
    in_specs = [piece_spec(index) for index in range(count)] + [
        whole(pass_emb.shape),
        whole(gain.shape),
        whole(shift.shape),
        whole(weight.shape),
        whole(bias.shape),
        pl.BlockSpec((block, 1), lambda slot, step, order_ref: (step, 0)),
    ]
    operands = [*pieces, pass_emb, gain, shift, weight, bias, depth]
    aliases = {}
    if previous is not None:
        aliases = {1 + len(operands) + index: index for index in range(4)}
        in_specs += [pl.BlockSpec(memory_space=pl.ANY)] * 4
        operands += list(previous)
    return pl.pallas_call(
        functools.partial(project_kernel, heads, count),
        grid_spec=pltpu.PrefetchScalarGridSpec(
            num_scalar_prefetch=1,
            grid=(count, steps),
            in_specs=in_specs,
            out_specs=[out_spec] * 3 + [stats_spec],
        ),
        out_shape=[shape] * 3 + [in_hbm((passes, length, 2), single)],
        input_output_aliases=aliases,
        compiler_params=pltpu.CompilerParams(vmem_limit_bytes=40 << 20),
        cost_estimate=pl.CostEstimate(flops=8 << 30, transcendentals=0, bytes_accessed=12 << 20),
        name="project",
    )(order, *operands)


def attend_kernel(passes, block, first, last, me_ref, q_ref, k_ref, v_ref, *refs):
    out_refs, q_next_ref, held = refs[:passes], refs[passes], refs[passes + 1]
    heads = q_ref.shape[0]
    step = pl.program_id(0)
    row = lax.broadcasted_iota(jnp.int32, (block, block), 0)
    col = lax.broadcasted_iota(jnp.int32, (block, block), 1)
    causal = col <= row

    def one_head(head, count):
        kept = [[] for _ in range(passes)]
        highest = [None] * passes
        for key_pass in range(passes):
            span = passes - key_pass
            query = q_ref[head, key_pass:passes].reshape(span * block, LANES)
            for tile in range(count):
                both = dot_nt(query, k_ref[head, key_pass, tile * block : (tile + 1) * block, :])
                for query_pass in range(key_pass, passes):
                    start = (query_pass - key_pass) * block
                    scores = both[start : start + block]
                    if tile == count - 1:
                        scores = jnp.where(causal, scores, MASKED)
                    kept[query_pass].append(scores)
                    for lane in range(0, block, LANES):
                        part = scores[:, lane : lane + LANES]
                        old = highest[query_pass]
                        highest[query_pass] = part if old is None else jnp.maximum(old, part)
        highest = [jnp.max(part, axis=-1, keepdims=True) for part in highest]
        for query_pass in range(passes):
            total = None
            for index, scores in enumerate(kept[query_pass]):
                key_pass, tile = divmod(index, count)
                weights = jnp.exp(scores - highest[query_pass]).astype(bfloat)
                term = dot_nn(weights, v_ref[head, key_pass, tile * block : (tile + 1) * block, :])
                total = term if total is None else total + term
            row_sum = total[:, DELTA_COL : DELTA_COL + 1]
            log_sum = highest[query_pass] + jnp.log(row_sum)
            q_next_ref[head, query_pass] = with_columns(
                q_ref[head, query_pass].astype(single), STAT_COL, three_parts(-log_sum)
            ).astype(bfloat)
            held[head, query_pass] = total * (1.0 / row_sum)

    for index in range(first, last):

        @pl.when(step == index - first)
        def _():
            lax.fori_loop(0, heads, lambda head, _: (one_head(head, index + 1), 0)[1], 0)

    for slot in range(passes):
        query_pass = jnp.bitwise_xor(me_ref[0], slot)
        out_refs[slot][...] = pack_heads([held[head, query_pass] for head in range(heads)]).astype(bfloat)


def attend(me, queries, keys, values, half):
    heads, passes, length, _ = queries.shape
    block = min(256, length // 2)
    count = length // 2 // block
    first, last = half * count, (half + 1) * count
    seen = pl.BlockSpec(
        (heads, passes, last * block, LANES),
        lambda step, me_ref: (0, 0, 0, 0),
        pipeline_mode=pl.Buffered(1),
    )
    part = pl.BlockSpec((heads, passes, block, LANES), lambda step, me_ref: (0, 0, first + step, 0))
    part_out = pl.BlockSpec((heads, passes, block, LANES), lambda step, me_ref: (0, 0, step, 0))
    packed = heads * HEAD_DIM
    *outs, queries = pl.pallas_call(
        functools.partial(attend_kernel, passes, block, first, last),
        grid_spec=pltpu.PrefetchScalarGridSpec(
            num_scalar_prefetch=1,
            grid=(count,),
            in_specs=[part, seen, seen],
            out_specs=[pl.BlockSpec((block, packed), lambda step, me_ref: (step, 0))] * passes + [part_out],
            scratch_shapes=[pltpu.VMEM((heads, passes, block, LANES), single)],
        ),
        out_shape=[in_hbm((length // 2, packed), bfloat)] * passes
        + [in_hbm((heads, passes, length // 2, LANES), bfloat)],
        compiler_params=pltpu.CompilerParams(vmem_limit_bytes=48 << 20),
        cost_estimate=pl.CostEstimate(
            flops=(10 + 20 * half) << 30,
            transcendentals=heads * (1 + 2 * half) * length * length,
            bytes_accessed=12 << 20,
        ),
        name="attend",
    )(me, *from_hbm((queries, keys, values)))
    return outs, queries


def attend_back_kernel(passes, block, me_ref, *refs):
    q_refs, (k_ref, v_ref), refs = refs[:2], refs[2:4], refs[4:]
    out_refs = refs[:passes], refs[passes : 2 * passes]
    grad_refs = refs[2 * passes : 3 * passes], refs[3 * passes : 4 * passes]
    all_ref, key_acc, value_acc, grad_held, query_held = refs[4 * passes :]
    heads = k_ref.shape[0]
    blocks = k_ref.shape[2] // block
    step = pl.program_id(0)
    me = me_ref[0]
    row = lax.broadcasted_iota(jnp.int32, (block, block), 0)
    col = lax.broadcasted_iota(jnp.int32, (block, block), 1)
    causal = row <= col
    inside = lax.broadcasted_iota(jnp.int32, (block, LANES), 1) < HEAD_DIM
    padded = ((heads * HEAD_DIM + LANES - 1) // LANES) * LANES

    @pl.when(step == 0)
    def _():
        key_acc[...] = jnp.zeros(key_acc.shape, single)
        value_acc[...] = jnp.zeros(value_acc.shape, single)

    def prepare(half):
        for slot in range(passes):
            query_pass = jnp.bitwise_xor(me, slot)
            grad = grad_refs[half][slot][...].astype(single)
            out = out_refs[half][slot][...].astype(single)
            if padded > heads * HEAD_DIM:
                tail = jnp.zeros((block, padded - heads * HEAD_DIM), single)
                grad = jnp.concatenate([grad, tail], axis=1)
                out = jnp.concatenate([out, tail], axis=1)
            product = grad * out
            for head in range(heads):
                delta = jnp.sum(
                    jnp.where(inside, head_slab(product, head), 0.0), axis=-1, keepdims=True
                )
                base = jnp.where(inside, head_slab(grad, head), 0.0)
                grad_held[head, query_pass] = with_columns(base, DELTA_COL, three_parts(-delta)).astype(bfloat)

    def one_head(head, count, q_ref):
        query_sums = [None] * passes
        for key_pass in range(passes):
            span = passes - key_pass
            query = q_ref[head, key_pass:passes].reshape(span * block, LANES)
            grad = grad_held[head, key_pass:passes].reshape(span * block, LANES)
            for tile in range(count):
                window = slice(tile * block, (tile + 1) * block)
                key = k_ref[head, key_pass, window, :]
                value = v_ref[head, key_pass, window, :]
                prob = jnp.exp(dot_nt(key, query))
                if tile == count - 1:
                    prob = jnp.where(jnp.concatenate([causal] * span, axis=1), prob, 0.0)
                value_acc[head, key_pass, window, :] += dot_nn(prob.astype(bfloat), grad)
                score_grad = (prob * dot_nt(value, grad)).astype(bfloat)
                key_acc[head, key_pass, window, :] += dot_nn(score_grad, query)
                term = dot_tn(key, score_grad)
                for query_pass in range(key_pass, passes):
                    start = (query_pass - key_pass) * block
                    part = term[:, start : start + block]
                    old = query_sums[query_pass]
                    query_sums[query_pass] = part if old is None else old + part
        for query_pass in range(passes):
            query_held[head, query_pass] = query_sums[query_pass].T * (HEAD_DIM**-0.5)

    for index in range(blocks):

        @pl.when(step == blocks - 1 - index)
        def _():
            half = index // (blocks // 2)
            prepare(half)
            lax.fori_loop(0, heads, lambda head, _: (one_head(head, index + 1, q_refs[half]), 0)[1], 0)
            window = slice(index * block, (index + 1) * block)
            for query_pass in range(passes):
                slabs = [query_held[head, query_pass] for head in range(heads)]
                slabs += [key_acc[head, query_pass, window, :] for head in range(heads)]
                slabs += [value_acc[head, query_pass, window, :] for head in range(heads)]
                all_ref[query_pass] = pack_heads(slabs).astype(bfloat)


def attend_back(me, queries, keys, values, outs, grads):
    heads, passes, length, _ = keys.shape
    block = min(256, length // 2)
    count = length // 2 // block
    packed = heads * HEAD_DIM

    def spot(half):
        return lambda step: jnp.clip(2 * count - 1 - step - half * count, 0, count - 1)

    def query_spec(half):
        return pl.BlockSpec((heads, passes, block, LANES), lambda step, me_ref: (0, 0, spot(half)(step), 0))

    def rows_spec(half):
        return pl.BlockSpec((block, packed), lambda step, me_ref: (spot(half)(step), 0))

    whole = pl.BlockSpec(keys.shape, lambda step, me_ref: (0, 0, 0, 0), pipeline_mode=pl.Buffered(1))
    rows_specs = [rows_spec(half) for half in range(2) for _ in range(passes)]
    return pl.pallas_call(
        functools.partial(attend_back_kernel, passes, block),
        grid_spec=pltpu.PrefetchScalarGridSpec(
            num_scalar_prefetch=1,
            grid=(2 * count,),
            in_specs=[query_spec(0), query_spec(1), whole, whole] + rows_specs * 2,
            out_specs=pl.BlockSpec(
                (passes, block, 3 * packed), lambda step, me_ref: (0, 2 * count - 1 - step, 0)
            ),
            scratch_shapes=[
                pltpu.VMEM(keys.shape, single),
                pltpu.VMEM(keys.shape, single),
                pltpu.VMEM((heads, passes, block, LANES), bfloat),
                pltpu.VMEM((heads, passes, block, LANES), single),
            ],
        ),
        out_shape=in_hbm((passes, length, 3 * packed), bfloat),
        compiler_params=pltpu.CompilerParams(vmem_limit_bytes=58 << 20),
        cost_estimate=pl.CostEstimate(
            flops=300 << 30, transcendentals=heads * 6 * length * length, bytes_accessed=20 << 20
        ),
        name="attend_back",
    )(me, *from_hbm((*queries, keys, values, *outs[0], *outs[1], *grads[0], *grads[1])))


def middle_kernel(groups, downs, shard, begins, me_ref, *refs):
    parts = refs[:groups]
    x_ref, cot_ref, pass_ref, out_bias_ref, gain_ref, shift_ref, down_bias_ref, up_bias_ref, w_out_ref, w_up_ref = refs[
        groups : groups + 10
    ]
    refs = refs[groups + 10 :]
    down_refs = refs[:downs]
    last_sums_ref = None if begins else refs[downs]
    outs, scratch = refs[-11 - groups : -5 - groups], refs[-5:]
    rows_ref, normed_ref, active_ref, upper_ref, proj_ref, sums_ref = outs
    grads = refs[-5 - groups : -5]
    normed_held, inverse_held, total_held, back_held, w_down_held = scratch
    me = me_ref[0]
    width = x_ref.shape[1]
    packed = width // groups
    step = pl.program_id(0)

    def group_window(slot):
        start = pl.multiple_of(jnp.bitwise_xor(me, slot) * packed, packed)
        return pl.ds(start, packed)

    def column_sum(values):
        return jnp.sum(values, axis=0, keepdims=True)

    @pl.when(step == 0)
    def _():
        sums_ref[...] = jnp.zeros(sums_ref.shape, single) if begins else last_sums_ref[...]
        mixed = x_ref[...].astype(single) + pass_ref[...] + out_bias_ref[...]
        for slot in range(groups):
            mixed += dot_nn(parts[slot][...], w_out_ref[group_window(slot), :])
        normed, inverse = norm_parts(mixed)
        normed_ref[...] = (normed * gain_ref[...] + shift_ref[...]).astype(bfloat)
        normed_held[...] = normed
        inverse_held[...] = jnp.broadcast_to(inverse, inverse_held.shape)
        total_held[...] = mixed + down_bias_ref[...]
        back_held[...] = jnp.zeros(back_held.shape, single)

    if shard:
        for start in range(0, down_refs[0].shape[0], 2 * shard):
            blocks = [ref[start : start + 2 * shard, :].astype(single) for ref in down_refs]
            pieces = [block[side * shard : (side + 1) * shard] for side in range(2) for block in blocks]
            w_down_held[start * downs : (start + 2 * shard) * downs, :] = jnp.concatenate(
                pieces, axis=0
            ).astype(bfloat)
        w_down_ref = w_down_held
    else:
        w_down_ref = down_refs[0]

    upper = dot_nn(normed_ref[...], w_up_ref[...]) + up_bias_ref[...]
    below = 0.5 + 0.5 * lax.erf(upper * (0.5**0.5))
    density = jnp.exp(-0.5 * upper * upper) * 0.3989422804014327
    active = (upper * below).astype(bfloat)
    active_ref[...] = active
    total_held[...] += dot_nn(active, w_down_ref[...])
    upper_low = (dot_nt(cot_ref[...], w_down_ref[...]) * (below + upper * density)).astype(bfloat)
    upper_ref[...] = upper_low
    sums_ref[pl.ds(4 + step, 1), :] += column_sum(upper_low.astype(single))
    back_held[...] += dot_nt(upper_low, w_up_ref[...])

    @pl.when(step == pl.num_programs(0) - 1)
    def _():
        rows_ref[...] = total_held[...].astype(bfloat)
        out_grad = cot_ref[...].astype(single)
        normed, back = normed_held[...], back_held[...]
        mixed_grad = out_grad + norm_back(back, gain_ref[...], normed, inverse_held[:, 0:1])
        proj_low = mixed_grad.astype(bfloat)
        proj_ref[...] = proj_low
        for slot in range(groups):
            grads[slot][...] = dot_nt(proj_low, w_out_ref[group_window(slot), :]).astype(bfloat)
        sums_ref[0:1, :] += column_sum(mixed_grad)
        sums_ref[1:2, :] += column_sum(back * normed)
        sums_ref[2:3, :] += column_sum(back)
        sums_ref[3:4, :] += column_sum(out_grad)


def middle(
    me,
    parts,
    x_own,
    cot,
    pass_row,
    out_bias,
    gain,
    shift,
    up_bias,
    down_bias,
    gathered,
    w_down,
    shard,
    half,
    previous,
):
    length, width = x_own.shape
    hidden = up_bias.shape[1]
    chunks = hidden // width
    groups = len(parts)
    packed = width // groups
    block = length // 2

    def rows(size):
        return pl.BlockSpec((block, size), lambda step, me_ref: (half, 0))

    def half_rows(size):
        return pl.BlockSpec((block, size), lambda step, me_ref: (0, 0))

    def whole(shape):
        return pl.BlockSpec(shape, lambda step, me_ref: (0, 0), pipeline_mode=pl.Buffered(1))

    def fixed(shape):
        return pl.BlockSpec(shape, lambda step, me_ref: (0, 0))

    by_chunk = pl.BlockSpec((block, width), lambda step, me_ref: (half, step))
    sums_shape = ((4 + chunks + 7) // 8 * 8, width)
    square = (width, width)
    small = (pass_row, out_bias, gain, shift, down_bias)
    if w_down is None:
        downs = chunks

        def down_spec(col):
            return pl.BlockSpec((width // chunks, width), lambda step, me_ref: (step, 1 + chunks + col))

        down_specs = [down_spec(col) for col in range(chunks)]
        down = [gathered] * chunks
    else:
        downs = 1
        down_specs = [pl.BlockSpec(square, lambda step, me_ref: (step, 0))]
        down = [w_down]
        shard = None
    in_specs = (
        [half_rows(packed)] * groups
        + [rows(width), rows(width)]
        + [whole(operand.shape) for operand in small]
        + [pl.BlockSpec((1, width), lambda step, me_ref: (0, step))]
        + [whole(square), pl.BlockSpec(square, lambda step, me_ref: (0, 1 + step))]
        + down_specs
    )
    operands = [*from_hbm([*parts, x_own, cot]), *small, up_bias, *from_hbm([gathered] * 2 + down)]
    aliases = {}
    if previous is not None:
        in_specs += [fixed(sums_shape)] + [pl.BlockSpec(memory_space=pl.ANY)] * 5
        aliases = {2 + len(operands) + index: index for index in range(5)}
        operands += [previous[5], *previous[:5]]
    results = pl.pallas_call(
        functools.partial(middle_kernel, groups, downs, shard, previous is None),
        grid_spec=pltpu.PrefetchScalarGridSpec(
            num_scalar_prefetch=1,
            grid=(chunks,),
            in_specs=in_specs,
            out_specs=[rows(width), rows(width), by_chunk, by_chunk, rows(width), fixed(sums_shape)]
            + [half_rows(packed)] * groups,
            scratch_shapes=[
                pltpu.VMEM((block, width), single),
                pltpu.VMEM((block, LANES), single),
                pltpu.VMEM((block, width), single),
                pltpu.VMEM((block, width), single),
                pltpu.VMEM(square, bfloat),
            ],
        ),
        out_shape=[
            in_hbm((length, width), bfloat),
            in_hbm((length, width), bfloat),
            in_hbm((length, hidden), bfloat),
            in_hbm((length, hidden), bfloat),
            in_hbm((length, width), bfloat),
            jax.ShapeDtypeStruct(sums_shape, single),
        ]
        + [in_hbm((length // 2, packed), bfloat)] * groups,
        input_output_aliases=aliases,
        compiler_params=pltpu.CompilerParams(vmem_limit_bytes=56 << 20),
        cost_estimate=pl.CostEstimate(
            flops=20 << 30, transcendentals=length * hidden, bytes_accessed=24 << 20
        ),
        name="middle",
    )(me, *operands)
    return results[:6], results[6:]


def weight_grad_kernel(groups, chunks, shard, me_ref, *refs):
    late_loads = refs[: 2 * groups + 1]
    normed_ref, cot_ref, upper_ref, active_ref, out_ref, staged, staged_down, sent, sent_down = refs[
        2 * groups + 1 : 2 * groups + 10
    ]
    loaded, loads = refs[2 * groups + 10 : -1], refs[-1]
    early, late, proj_ref = loaded[:groups], loaded[groups : 2 * groups], loaded[-1]
    length, width = normed_ref.shape
    middle_row = length // 2
    packed = width // groups
    rows = width // chunks
    step = pl.program_id(0)

    def columns_copy(index):
        start = pl.multiple_of(index * width, width)
        return pltpu.make_async_copy(staged.at[index], out_ref.at[:, pl.ds(start, width)], sent.at[index])

    def down_copy(index):
        if shard:
            start = pl.multiple_of(index * rows, rows)
            target = out_ref.at[pl.ds(start, rows), pl.ds((1 + chunks) * width, chunks * width)]
        else:
            start = pl.multiple_of((1 + chunks + index) * width, width)
            target = out_ref.at[:, pl.ds(start, width)]
        return pltpu.make_async_copy(staged_down.at[index], target, sent_down.at[index])

    def load(index):
        return pltpu.make_async_copy(late_loads[index], loaded[index], loads.at[index])

    @pl.when(step == 0)
    def _():
        for index in range(2 * groups + 1):
            load(index).start()

    @pl.when(step < chunks)
    def _():
        staged[step + 1] = dot_tn(normed_ref[...], upper_ref[...]).astype(bfloat)
        down = dot_tn(active_ref[...], cot_ref[...])
        if shard:
            for start in range(0, rows, 2 * shard):
                for chunk in range(chunks):
                    first = start * chunks + chunk * shard
                    second = first + chunks * shard
                    staged_down[step, start : start + 2 * shard, chunk * width : (chunk + 1) * width] = (
                        jnp.concatenate(
                            [down[first : first + shard], down[second : second + shard]], axis=0
                        ).astype(bfloat)
                    )
        else:
            staged_down[step] = down.astype(bfloat)
        columns_copy(step + 1).start()
        down_copy(step).start()

    @pl.when(step == chunks)
    def _():
        for index in range(2 * groups + 1):
            load(index).wait()
        for slot in range(groups):
            start = pl.multiple_of(jnp.bitwise_xor(me_ref[0], slot) * packed, packed)
            staged[0, pl.ds(start, packed), :] = (
                dot_tn(early[slot][...], proj_ref[:middle_row, :])
                + dot_tn(late[slot][...], proj_ref[middle_row:, :])
            ).astype(bfloat)
        columns_copy(0).start()
        for index in range(1 + chunks):
            columns_copy(index).wait()
        for index in range(chunks):
            down_copy(index).wait()


def weight_grads(me, early, late, proj, normed, cot, upper, active, shard):
    length, width = proj.shape
    hidden = upper.shape[1]
    chunks = hidden // width
    groups = len(early)
    parts = [*early, *late]

    def whole(shape):
        return pl.BlockSpec(shape, lambda step, me_ref: (0, 0), pipeline_mode=pl.Buffered(1))

    by_chunk = pl.BlockSpec((length, width), lambda step, me_ref: (0, jnp.minimum(step, chunks - 1)))
    late_loads = [*parts, proj]
    down_shape = (width // chunks, chunks * width) if shard else (width, width)
    return pl.pallas_call(
        functools.partial(weight_grad_kernel, groups, chunks, shard),
        grid_spec=pltpu.PrefetchScalarGridSpec(
            num_scalar_prefetch=1,
            grid=(1 + chunks,),
            in_specs=[pl.BlockSpec(memory_space=pl.ANY)] * len(late_loads)
            + [whole(proj.shape)] * 2
            + [by_chunk] * 2,
            out_specs=pl.BlockSpec(memory_space=pl.ANY),
            scratch_shapes=[
                pltpu.VMEM((1 + chunks, width, width), bfloat),
                pltpu.VMEM((chunks, *down_shape), bfloat),
                pltpu.SemaphoreType.DMA((1 + chunks,)),
                pltpu.SemaphoreType.DMA((chunks,)),
            ]
            + [pltpu.VMEM(operand.shape, bfloat) for operand in late_loads]
            + [pltpu.SemaphoreType.DMA((len(late_loads),))],
        ),
        out_shape=in_hbm((width, width + 2 * hidden), bfloat),
        compiler_params=pltpu.CompilerParams(vmem_limit_bytes=56 << 20),
        cost_estimate=pl.CostEstimate(flops=20 << 30, transcendentals=0, bytes_accessed=32 << 20),
        name="weight_grads",
    )(me, *from_hbm([*parts, proj, normed, cot, upper, active]))


def split_weights_kernel(chunks, in_ref, out_ref, up_ref, down_ref):
    shard, width = out_ref.shape
    out_ref[...] = in_ref[:, :width].astype(single)
    up_ref[...] = in_ref[:, width : (1 + chunks) * width].astype(single)
    for chunk in range(chunks):
        start = (1 + chunks + chunk) * width
        down_ref[chunk * shard : (chunk + 1) * shard, :] = in_ref[:, start : start + width].astype(single)


def split_weights(reduced, width):
    shard, columns = reduced.shape
    hidden = (columns - width) // 2
    struct = jax.ShapeDtypeStruct
    return pl.pallas_call(
        functools.partial(split_weights_kernel, hidden // width),
        out_shape=[
            struct((shard, width), single),
            struct((shard, hidden), single),
            struct((shard * hidden // width, width), single),
        ],
        name="split_weights",
    )(reduced)


def join_groups_kernel(passes, in_ref, out_ref):
    sequences = in_ref.shape[0] // passes
    packed = in_ref.shape[2]
    group = packed // 3
    sums = []
    for index in range(passes):
        total = in_ref[index].astype(single)
        for sequence in range(1, sequences):
            total += in_ref[sequence * passes + index].astype(single)
        sums.append(total)
    width = passes * group
    for part in range(3):
        out_ref[:, part * width : (part + 1) * width] = jnp.concatenate(
            [total[:, part * group : (part + 1) * group] for total in sums], axis=1
        )


def join_groups(pieces, passes):
    _, shard, packed = pieces.shape
    return pl.pallas_call(
        functools.partial(join_groups_kernel, passes),
        out_shape=jax.ShapeDtypeStruct((shard, passes * packed), single),
        name="join_groups",
    )(pieces)


def project_back_kernel(count, passes, me_ref, *refs):
    pieces = refs[:count]
    pass_ref, gain_ref, shift_ref, weight_ref, grad_ref, stats_ref, last_sums_ref = refs[count : count + 7]
    *rows_refs, weight_low_ref, sums_ref, held, weight_grad_ref = refs[count + 7 :]
    slot = pl.program_id(0)
    step = pl.program_id(1)
    pass_index = me_ref[1 + slot]
    packed = grad_ref.shape[1]

    @pl.when((slot == 0) & (step == 0))
    def _():
        weight_grad_ref[...] = jnp.zeros(weight_grad_ref.shape, single)
        sums_ref[...] = jnp.zeros(sums_ref.shape, single)
        sums_ref[16:, :] = last_sums_ref[...]
        sums_ref[pl.ds(passes + me_ref[0], 1), :] = last_sums_ref[0:1, :]

    def column_sum(values):
        return jnp.sum(values, axis=0, keepdims=True)

    rows = pieces[0][...]
    for index in range(1, count):
        rows = jnp.where(slot == index, pieces[index][...], rows)
    stats = stats_ref[...]
    inverse = stats[:, 0:1]
    normed = (rows.astype(single) + pass_ref[pl.ds(pass_index, 1), :]) * inverse + stats[:, 1:2]
    low = (normed * gain_ref[...] + shift_ref[...]).astype(bfloat)
    grad = grad_ref[...]
    back = dot_nt(grad, weight_ref[...])
    weight_grad_ref[...] += dot_tn(low, grad)
    part = norm_back(back, gain_ref[...], normed, inverse)
    held[...] = part.astype(bfloat)
    sums_ref[pl.ds(me_ref[0], 1), :packed] += column_sum(grad.astype(single))
    sums_ref[pl.ds(passes + pass_index, 1), :] += column_sum(part)
    sums_ref[8:9, :] += column_sum(back * normed)
    sums_ref[9:10, :] += column_sum(back)
    for index in range(count):

        @pl.when(slot == index)
        def _():
            rows_refs[index][...] = held[...]

    @pl.when((slot == count - 1) & (step == pl.num_programs(1) - 1))
    def _():
        weight_low_ref[...] = weight_grad_ref[...].astype(bfloat)


def project_back(order, pieces, pass_emb, gain, shift, weight, grads, stats, last_sums):
    count = len(pieces)
    length, width = pieces[0].shape
    passes, _, packed = grads.shape
    block = min(512, length)
    steps = length // block
    sums_shape = (16 + last_sums.shape[0], width)

    def piece_spec(index):
        def where(slot, step, order_ref):
            return (jnp.where(slot == index, step, jnp.where(slot < index, 0, steps - 1)), 0)

        return pl.BlockSpec((block, width), where)

    def whole(shape):
        return pl.BlockSpec(shape, lambda slot, step, order_ref: (0,) * len(shape))

    def by_pass(size):
        return pl.BlockSpec(
            (pl.Squeezed(), block, size), lambda slot, step, order_ref: (order_ref[1 + slot], step, 0)
        )

    small = [pass_emb, gain, shift]
    return pl.pallas_call(
        functools.partial(project_back_kernel, count, passes),
        grid_spec=pltpu.PrefetchScalarGridSpec(
            num_scalar_prefetch=1,
            grid=(count, steps),
            in_specs=[piece_spec(index) for index in range(count)]
            + [whole(operand.shape) for operand in small]
            + [whole(weight.shape), by_pass(packed), by_pass(2), whole(last_sums.shape)],
            out_specs=[piece_spec(index) for index in range(count)]
            + [whole((width, packed)), whole(sums_shape)],
            scratch_shapes=[pltpu.VMEM((block, width), bfloat), pltpu.VMEM((width, packed), single)],
        ),
        out_shape=[in_hbm((length, width), bfloat)] * count
        + [jax.ShapeDtypeStruct((width, packed), bfloat), jax.ShapeDtypeStruct(sums_shape, single)],
        compiler_params=pltpu.CompilerParams(vmem_limit_bytes=48 << 20),
        cost_estimate=pl.CostEstimate(flops=16 << 30, transcendentals=0, bytes_accessed=20 << 20),
        name="project_back",
    )(order, *from_hbm(pieces), *small, *from_hbm([weight, grads, stats]), last_sums)


def exchange(value, axis, distance):
    return lax.ppermute(value, axis, [(k, k ^ distance) for k in range(lax.axis_size(axis))])


def summing_steps():
    passes, sequences = lax.axis_size("pass"), lax.axis_size("seq")
    steps = [("pass", distance) for distance in (2**power for power in range(1, passes)) if distance < passes]
    steps += [("seq", distance) for distance in (2**power for power in range(sequences)) if distance < sequences]
    return steps + [("pass", 1)]


def per_device(
    x_rows,
    pass_depth,
    cotangent,
    pass_emb,
    ln1_gain,
    ln1_bias,
    w_qkv,
    q_bias,
    v_bias,
    w_out,
    out_bias,
    ln2_gain,
    ln2_bias,
    w_up,
    up_bias,
    w_down,
    down_bias,
):
    everyone = ("seq", "pass")
    _, length, width = x_rows.shape
    hidden = w_up.shape[1]
    passes = lax.axis_size("pass")
    devices = passes * lax.axis_size("seq")
    shard = w_qkv.shape[0]
    group = width // passes
    group_heads = group // HEAD_DIM
    me = lax.axis_index("pass")
    order = jnp.concatenate([me[None], jnp.bitwise_xor(me, jnp.arange(passes))]).astype(jnp.int32)

    def swap(value, distance):
        return exchange(value, "pass", distance)

    x_own = x_rows[0]

    by_group = w_qkv.reshape(shard, 3, passes, group).transpose(2, 0, 1, 3).reshape(passes, shard, 3 * group)
    by_rows = lax.all_to_all(by_group, "pass", 0, 0, tiled=True).reshape(passes * shard, 3 * group)
    by_rows, x_ready = lax.optimization_barrier((by_rows, x_own))
    x_one = swap(x_ready, 1)
    x_two = swap(x_ready, 2)
    w_heads = lax.all_gather(by_rows, "seq", axis=0, tiled=True)

    down_cols = w_down.reshape(passes, shard, width).transpose(1, 0, 2).reshape(shard, hidden)
    own_weights = jnp.concatenate([w_out, w_up, down_cols], axis=1)
    own_weights, x_ready = lax.optimization_barrier((own_weights, x_ready))
    gathered = lax.all_gather(own_weights, everyone, axis=0, tiled=True)
    in_place = shard % 8 == 0
    full_down = None
    if not in_place:
        full_down = (
            gathered[:, width + hidden :]
            .reshape(devices, shard, hidden // width, width)
            .transpose(0, 2, 1, 3)
            .reshape(hidden, width)
        )

    gain_one, shift_one = ln1_gain[None], ln1_bias[None]
    own_q_bias = lax.dynamic_slice_in_dim(q_bias, me * group, group)
    own_v_bias = lax.dynamic_slice_in_dim(v_bias, me * group, group)
    bias_row = jnp.concatenate([own_q_bias, jnp.zeros((group,), single), own_v_bias])[None]
    pad = (-3 * group) % LANES
    w_wide = jnp.pad(w_heads, ((0, 0), (0, pad)))
    bias_wide = jnp.pad(bias_row, ((0, 0), (0, pad)))
    depth = pass_depth.reshape(length, 1)
    near = project(
        order[:3], (x_own, x_one), passes, pass_emb, gain_one, shift_one, w_wide, bias_wide, depth, None
    )
    x_two, near = lax.optimization_barrier((x_two, near))
    x_three = swap(x_two, 1)
    far_order = jnp.concatenate([order[:1], order[3:]])
    queries, keys, values, stats = project(
        far_order, (x_two, x_three), passes, pass_emb, gain_one, shift_one, w_wide, bias_wide, depth, near
    )

    def trade(pieces):
        return list(pieces[:1]) + [swap(pieces[slot], slot) for slot in range(1, passes)]

    pass_row = lax.dynamic_index_in_dim(pass_emb, me, 0, keepdims=True)
    outs, logged = [None, None], [None, None]
    for half in (1, 0):
        outs[half], logged[half] = attend(order[:1], queries, keys, values, half)
    parts = [trade(outs[half]) for half in range(2)]
    results = None
    head_grads = [None, None]
    for half in (1, 0):
        results, head_grads[half] = middle(
            order[:1],
            parts[half],
            x_own,
            cotangent[0],
            pass_row,
            out_bias[None],
            ln2_gain[None],
            ln2_bias[None],
            up_bias[None],
            down_bias[None],
            gathered,
            full_down,
            shard,
            half,
            results,
        )
        head_grads[half] = trade(head_grads[half])
    out_rows, normed_two, activated, upper_low, proj_low, sums = results

    weight_parts = weight_grads(
        order[:1],
        *parts,
        proj_low,
        normed_two,
        cotangent[0],
        upper_low,
        activated,
        shard if in_place else None,
    )
    if not in_place:
        down_part = (
            weight_parts[:, width + hidden :]
            .reshape(width, hidden // width, width)
            .transpose(1, 0, 2)
            .reshape(devices, hidden // width, shard, width)
            .transpose(0, 2, 1, 3)
            .reshape(width, hidden)
        )
        weight_parts = jnp.concatenate([weight_parts[:, : width + hidden], down_part], axis=1)
    weight_parts, logged, head_grads = lax.optimization_barrier((weight_parts, logged, head_grads))
    reduced = lax.psum_scatter(weight_parts, everyone, scatter_dimension=0, tiled=True)
    if in_place:
        shard_out, shard_up, shard_down = split_weights(reduced, width)
    else:
        reduced = reduced.astype(single)
        shard_out = reduced[:, :width]
        shard_up = reduced[:, width : width + hidden]
        shard_down = (
            reduced[:, width + hidden :]
            .reshape(shard, hidden // width, width)
            .transpose(1, 0, 2)
            .reshape(w_down.shape)
        )

    qkv_low = attend_back(order[:1], logged, keys, values, outs, head_grads)
    near_own, near_one, far_two, far_three, head_weight, sums = project_back(
        order, (x_own, x_one, x_two, x_three), pass_emb, gain_one, shift_one, w_heads, qkv_low, stats, sums
    )

    near_one, far_three = swap(near_one, 1), swap(far_three, 1)
    far_sum = (far_two.astype(single) + far_three.astype(single)).astype(bfloat)
    pieces = head_weight.reshape(devices, shard, 3 * group)
    steps = summing_steps()
    totals = sums + exchange(sums, *steps[0])
    totals, far_sum, pieces = lax.optimization_barrier((totals, far_sum, pieces))
    far_sum = swap(far_sum, 2)
    pieces = lax.all_to_all(pieces, everyone, 0, 0, tiled=True)
    if in_place:
        shard_qkv = join_groups(pieces, passes)
    else:
        pieces = pieces.reshape(devices // passes, passes, shard, 3, group).astype(single).sum(axis=0)
        shard_qkv = pieces.transpose(1, 2, 0, 3).reshape(w_qkv.shape)

    far_sum, shard_qkv = lax.optimization_barrier((far_sum, shard_qkv))
    x_grad = (
        proj_low.astype(single)
        + near_own.astype(single)
        + near_one.astype(single)
        + far_sum.astype(single)
    )

    for axis, distance in steps[1:]:
        totals = totals + exchange(totals, axis, distance)
    biases = totals[:passes, : 3 * group].reshape(passes, 3, group)
    pass_grad = lax.dynamic_slice_in_dim(totals, passes + me, 1, 0)
    up_rows = hidden // width
    return (
        out_rows[None],
        x_grad[None],
        shard_qkv,
        biases[:, 0].reshape(-1),
        biases[:, 2].reshape(-1),
        shard_out,
        totals[16],
        totals[8],
        totals[9],
        totals[17],
        totals[18],
        shard_up,
        totals[20 : 20 + up_rows].reshape(-1),
        shard_down,
        totals[19],
        pass_grad,
    )


def solution(mesh):
    placed = (
        P("pass", "seq", None),
        P("seq", None),
        P("pass", "seq", None),
        P(),
        P(),
        P(),
        P(("seq", "pass"), None),
        P(),
        P(),
        P(("seq", "pass"), None),
        P(),
        P(),
        P(),
        P(("seq", "pass"), None),
        P(),
        P(("seq", "pass"), None),
        P(),
    )
    return jax.shard_map(
        per_device,
        mesh=mesh,
        in_specs=placed,
        out_specs=(
            P("pass", "seq", None),
            P("pass", "seq", None),
            P(("seq", "pass"), None),
            P(),
            P(),
            P(("seq", "pass"), None),
            P(),
            P(),
            P(),
            P(),
            P(),
            P(("seq", "pass"), None),
            P(),
            P(("seq", "pass"), None),
            P(),
            P("pass", None),
        ),
        check_vma=False,
    )
```
